32 devices in a mesh: fsdp: 8 (over y, x, core), rep: 4 (over z).
Axes of the slice: x: 2, y: 2, z: 4, core: 2. Of those that a mesh axis runs over, the one named last changes fastest.
Arguments:
- tokens: bfloat16 [8192, 1152], P(('fsdp', 'rep')), may hold values from -6 to 6
- cond: bfloat16 [128, 1152], P(('fsdp', 'rep')), may hold values from -6 to 6
- image_sizes: int32 [128], P(('fsdp', 'rep')), may hold values from 0 to 256, as said below
- w_ada: bfloat16 [1152, 6912], P('fsdp'), may hold values from -0.1875 to 0.1875
- b_ada: bfloat16 [6912], P('fsdp'), may hold values from -1.5 to 1.5
- w_qkv: bfloat16 [1152, 3456], P('fsdp'), may hold values from -0.1875 to 0.1875
- b_qkv: bfloat16 [2304], P('fsdp'), may hold values from -2.5 to 2.5
- w_out: bfloat16 [1152, 1152], P('fsdp'), may hold values from -0.75 to 0.75
- b_out: bfloat16 [1152], P('fsdp'), may hold values from -1.5 to 1.5
- w_up: bfloat16 [1152, 4608], P('fsdp'), may hold values from -0.1875 to 0.1875
- b_up: bfloat16 [4608], P('fsdp'), may hold values from -2.5 to 2.5
- w_down: bfloat16 [4608, 1152], P('fsdp'), may hold values from -0.09375 to 0.09375
- b_down: bfloat16 [1152], P('fsdp'), may hold values from -1.5 to 1.5
- cotangent: bfloat16 [8192, 1152], P(('fsdp', 'rep')), may hold values from -6 to 6
Outputs:
- output: bfloat16 [8192, 1152], P(('fsdp', 'rep'))
- grad_input: float32 [8192, 1152], P(('fsdp', 'rep'))
- grad_cond: float32 [128, 1152], P(('fsdp', 'rep'))
- grad_w_ada: float32 [1152, 6912], P('fsdp')
- grad_b_ada: float32 [6912], P('fsdp')
- grad_w_qkv: float32 [1152, 3456], P('fsdp')
- grad_b_qkv: float32 [2304], P('fsdp')
- grad_w_out: float32 [1152, 1152], P('fsdp')
- grad_b_out: float32 [1152], P('fsdp')
- grad_w_up: float32 [1152, 4608], P('fsdp')
- grad_b_up: float32 [4608], P('fsdp')
- grad_w_down: float32 [4608, 1152], P('fsdp')
- grad_b_down: float32 [1152], P('fsdp')
The draws below stay inside these ranges and needn't reach their ends.
Inputs may be any that keep to these rules, and one draw needn't show every extreme that they name: `image_sizes`: in each group of 4 slots of one device, either the first slot holds one image of 256 patches and the rest are 0, or the first k slots (k from 1 to 4) hold images of 64 patches and the rest are 0; in every draw some device's images fill all its 256 slots.
All inputs are finite; a program needn't handle non-finite values.
Results may differ from the reference program's by a relative error of at most 0.02.
Values may be sent and summed in bfloat16 or wider, within the bound.
A program may use at most 256 MiB of HBM per device.

```python
import jax
import jax.numpy as jnp
from jax import lax

D = 1152
H = 16
HD = 72
FF = 4608
TOK_DEV = 256
SLOTS = 4
SMALL = 64
TOKENS = 8192
IMAGES = 128


def draw_image_sizes(key, part):
    device_total = IMAGES // SLOTS
    kind_key, pick_key = jax.random.split(jax.random.fold_in(key, 17))
    image_kind = jax.random.randint(kind_key, (device_total,), 0, SLOTS + 1)
    forced_device = jax.random.randint(pick_key, (), 0, device_total)
    image_kind = jnp.where(jnp.arange(device_total) == forced_device, 0, image_kind)
    slot_index = jnp.arange(SLOTS)[None, :]
    big_image = jnp.where(slot_index == 0, TOK_DEV, 0)
    small_image = jnp.where(slot_index < image_kind[:, None], SMALL, 0)
    sizes_table = jnp.where(image_kind[:, None] == 0, big_image, small_image)
    return sizes_table.reshape(-1).astype(jnp.int32)


def shard_levels(stream_key, dims, pieces, smallest, high):
    factor_of = 1.0
    for position, parts in pieces:
        heights = jax.random.uniform(jax.random.fold_in(jax.random.fold_in(stream_key, 6), position), (parts,), jnp.float32, smallest / len(pieces), high / len(pieces))
        factor_of = factor_of * jnp.repeat(jnp.exp(heights), dims[position] // parts).reshape((-1,) + (1,) * (len(dims) - 1 - position))
    return factor_of


def bell_draw(rng, shape, deviation, limit, cuts=(), held_as=jnp.bfloat16):
    gain = shard_levels(rng, shape, cuts, -0.22, 0.18) if cuts else 1.0
    entries = jax.random.normal(rng, shape, jnp.float32) * deviation * gain
    return jnp.minimum(jnp.maximum(entries, -limit), limit).astype(held_as)


def setup_inputs(seed: int = 0) -> dict:
    keys = jax.random.split(jax.random.key(seed), 15)
    tokens = bell_draw(keys[0], (TOKENS, D), 1.0, 6.0, ((0, 32),))
    cond = bell_draw(keys[1], (IMAGES, D), 1.0, 6.0, ((0, 32),))
    image_sizes = draw_image_sizes(jax.random.fold_in(keys[14], 71), 0)
    w_ada = bell_draw(keys[3], (D, 6 * D), D ** -0.5, 0.1875, ((0, 8),))
    b_ada = bell_draw(keys[4], (6 * D,), 0.3, 1.5, ((0, 8),))
    w_qkv = bell_draw(keys[5], (D, 3 * D), D ** -0.5, 0.1875, ((0, 8),))
    b_qkv = bell_draw(keys[6], (2 * D,), 0.5, 2.5, ((0, 8),))
    w_out = bell_draw(keys[7], (D, D), (D // 16) ** -0.5, 0.75, ((0, 8),))
    b_out = bell_draw(keys[8], (D,), 0.3, 1.5, ((0, 8),))
    w_up = bell_draw(keys[9], (D, FF), D ** -0.5, 0.1875, ((0, 8),))
    b_up = bell_draw(keys[10], (FF,), 0.5, 2.5, ((0, 8),))
    w_down = bell_draw(keys[11], (FF, D), FF ** -0.5, 0.09375, ((0, 8),))
    b_down = bell_draw(keys[12], (D,), 0.3, 1.5, ((0, 8),))
    cotangent = bell_draw(keys[13], (TOKENS, D), 1.0, 6.0, ((0, 32),))
    return {"tokens": tokens, "cond": cond, "image_sizes": image_sizes, "w_ada": w_ada, "b_ada": b_ada, "w_qkv": w_qkv, "b_qkv": b_qkv, "w_out": w_out, "b_out": b_out, "w_up": w_up, "b_up": b_up, "w_down": w_down, "b_down": b_down, "cotangent": cotangent}


@jax.custom_vjp
def low(v):
    return lax.optimization_barrier(v.astype(jnp.bfloat16)).astype(jnp.float32)

@jax.custom_vjp
def low_back(v):
    return v

def low_keep(v):
    return (low(v), None)

def low_pass(kept, grad):
    return (grad,)

def back_keep(v):
    return (v, None)

def back_low(kept, grad):
    return (low(grad),)
low.defvjp(low_keep, low_pass)
low_back.defvjp(back_keep, back_low)
EPSILON = 1e-06
HIGHEST = lax.Precision.HIGHEST
MASKED = -1e+30

def matmul(first_operand, second_operand):
    return jnp.dot(first_operand, second_operand, precision=HIGHEST)

def layer_norm(inputs):
    average = lax.optimization_barrier(jnp.mean(inputs, axis=-1, keepdims=True))
    centered = inputs - average
    variance = lax.optimization_barrier(jnp.mean(centered * centered, axis=-1, keepdims=True))
    return centered * lax.rsqrt(variance + EPSILON)

def image_layout(size_row):
    image_ends = jnp.cumsum(size_row)
    positions = jnp.arange(TOK_DEV, dtype=jnp.int32)
    image_ids = lax.optimization_barrier(jnp.sum((positions[:, None] >= image_ends[None, :]).astype(jnp.int32), axis=1))
    selector = (image_ids[:, None] == jnp.arange(SLOTS, dtype=jnp.int32)[None, :]).astype(jnp.float32)
    return (image_ids, selector)

def forward(params, hidden, cond_rows, size_row):
    w_ada, b_ada, w_qkv, b_qkv, w_out, b_out, w_up, b_up, w_down, b_down = params
    image_ids, selector = image_layout(size_row)
    activ = low(jax.nn.silu(cond_rows))
    modulation = low_back(matmul(activ, w_ada) + b_ada)
    per_token = matmul(selector, modulation)
    shift_a, scale_a, gate_a, shift_b, scale_b, gate_b = jnp.split(per_token, 6, axis=1)
    normed_a = low(layer_norm(hidden) * (1.0 + scale_a) + shift_a)
    bias_full = jnp.concatenate([b_qkv[:D], jnp.zeros((D,), jnp.float32), b_qkv[D:]])
    projected = low_back(low(matmul(normed_a, w_qkv) + bias_full))
    query_heads = projected[:, :D].reshape(TOK_DEV, H, HD)
    key_heads = projected[:, D:2 * D].reshape(TOK_DEV, H, HD)
    value_heads = projected[:, 2 * D:].reshape(TOK_DEV, H, HD)
    scores = jnp.einsum('qhd,khd->hqk', query_heads, key_heads, precision=HIGHEST) * HD ** (-0.5)
    scores = low_back(scores)
    same_image = image_ids[:, None] == image_ids[None, :]
    scores = jnp.where(same_image[None], scores, MASKED)
    row_max = lax.optimization_barrier(jnp.max(scores, axis=-1, keepdims=True))
    exponent = jnp.exp(scores - row_max)
    probabilities = low(exponent / lax.optimization_barrier(jnp.sum(exponent, axis=-1, keepdims=True)))
    attended = jnp.einsum('hqk,khd->qhd', probabilities, value_heads, precision=HIGHEST).reshape(TOK_DEV, D)
    attended = low_back(low(attended))
    branch_a = low_back(matmul(attended, w_out) + b_out)
    middle = hidden + gate_a * branch_a
    normed_b = low(layer_norm(middle) * (1.0 + scale_b) + shift_b)
    inner_pre = low_back(matmul(normed_b, w_up) + b_up)
    activated = low(jax.nn.gelu(inner_pre, approximate=True))
    branch_b = low_back(matmul(activated, w_down) + b_down)
    return middle + gate_b * branch_b

def add_trees(first_tree, second_tree):
    return jax.tree.map(jnp.add, first_tree, second_tree)

def reference(tokens, cond, image_sizes, w_ada, b_ada, w_qkv, b_qkv, w_out, b_out, w_up, b_up, w_down, b_down, cotangent):
    params = tuple((weight.astype(jnp.float32) for weight in (w_ada, b_ada, w_qkv, b_qkv, w_out, b_out, w_up, b_up, w_down, b_down)))
    buffers = tokens.astype(jnp.float32).reshape(-1, TOK_DEV, D)
    cond_groups = cond.astype(jnp.float32).reshape(-1, SLOTS, D)
    size_groups = image_sizes.reshape(-1, SLOTS)
    cotangent_groups = cotangent.astype(jnp.float32).reshape(-1, TOK_DEV, D)

    def step(totals, block_item):
        buffer, cond_rows, size_row, cotangent_rows = block_item

        def apply_layer(layer_params, hidden, cond_values):
            return forward(layer_params, hidden, cond_values, size_row)
        result, pullback = jax.vjp(apply_layer, params, buffer, cond_rows)
        grad_params, grad_buffer, grad_cond_rows = pullback(cotangent_rows)
        return (add_trees(totals, grad_params), (result.astype(jnp.bfloat16), grad_buffer, grad_cond_rows))
    zeros = tuple((jnp.zeros_like(weight) for weight in params))
    totals, (outputs, grad_tokens, grad_conds) = lax.scan(step, zeros, (buffers, cond_groups, size_groups, cotangent_groups))
    return (outputs.reshape(-1, D), grad_tokens.reshape(-1, D), grad_conds.reshape(-1, D), totals[0], totals[1], totals[2], totals[3], totals[4], totals[5], totals[6], totals[7], totals[8], totals[9])
```

```python
import functools

import jax
import jax.numpy as jnp
from jax import lax
from jax.experimental import pallas as pl
from jax.experimental.pallas import tpu as pltpu
from jax.sharding import PartitionSpec as P

H = 16


EPSILON = 1e-06
HIGHEST = lax.Precision.HIGHEST
MASKED = -1e30


def layer_norm(inputs):
    average = jnp.mean(inputs, axis=-1, keepdims=True)
    centered = inputs - average
    variance = jnp.mean(centered * centered, axis=-1, keepdims=True)
    return centered * lax.rsqrt(variance + EPSILON)


def modulate(hidden, shift_part, scale_part):
    return layer_norm(hidden) * (1.0 + scale_part) + shift_part


def gelu_tanh(inputs):
    return jax.nn.gelu(inputs, approximate=True)


def product(first_operand, second_operand):
    return jnp.dot(first_operand, second_operand, preferred_element_type=jnp.float32)


def product_back(first_operand, second_operand):
    return lax.dot_general(
        first_operand, second_operand, (((1,), (1,)), ((), ())), preferred_element_type=jnp.float32
    )


def outer_sum(first_operand, second_operand):
    return lax.dot_general(
        first_operand, second_operand, (((0,), (0,)), ((), ())), preferred_element_type=jnp.float32
    )


def fetch_forward(weight, bias_piece):
    return (
        lax.all_gather(weight, "fsdp", axis=0, tiled=True),
        lax.all_gather(bias_piece, "fsdp", axis=0, tiled=True),
    )


def weights_again(weight):
    return lax.all_gather(weight, "fsdp", axis=0, tiled=True)


def reduce_grads(weight_grad, bias_grad):
    row_part, bias_part = (
        lax.psum_scatter(weight_grad, "fsdp", scatter_dimension=0, tiled=True),
        lax.psum_scatter(bias_grad, "fsdp", scatter_dimension=0, tiled=True),
    )
    column_part = lax.psum_scatter(row_part, "rep", scatter_dimension=1, tiled=True)
    whole_rows, bias_stack = (
        lax.all_gather(column_part, "rep", axis=1, tiled=True),
        lax.all_gather(bias_part[None], "rep", axis=0, tiled=True),
    )
    return (whole_rows, jnp.sum(bias_stack, axis=0))


def local(
    tokens,
    cond,
    image_sizes,
    w_ada,
    b_ada,
    w_qkv,
    b_qkv,
    w_out,
    b_out,
    w_up,
    b_up,
    w_down,
    b_down,
    cotangent,
):
    row_count, model_width = tokens.shape
    head_count = H
    head_dim = model_width // head_count
    slot_count = image_sizes.shape[0]
    scale_factor = head_dim ** (-0.5)
    block_rows = min(512, row_count)
    block_count = row_count // block_rows
    image_ends = jnp.sum(
        jnp.where(jnp.arange(slot_count)[:, None] >= jnp.arange(slot_count)[None, :], image_sizes[None, :], 0), axis=1
    )
    positions = jnp.arange(row_count, dtype=jnp.int32)
    image_ids = jnp.sum((positions[:, None] >= image_ends[None, :]).astype(jnp.int32), axis=1)
    selector = (image_ids[:, None] == jnp.arange(slot_count, dtype=jnp.int32)[None, :]).astype(
        jnp.float32
    )
    cond_float = cond.astype(jnp.float32)
    activ_float, silu_pull = jax.vjp(jax.nn.silu, cond_float)
    activ_low = activ_float.astype(jnp.bfloat16)
    full_ada, full_bada = fetch_forward(w_ada, b_ada)
    modulation = product(activ_low, full_ada) + full_bada.astype(jnp.float32)
    per_token = jnp.dot(selector, modulation, precision=HIGHEST)
    shift_a, scale_a, gate_a, shift_b, scale_b, gate_b = jnp.split(per_token, 6, axis=1)
    hidden = tokens.astype(jnp.float32)
    normed_a, pull_a = jax.vjp(modulate, hidden, shift_a, scale_a)
    normed_a_low = normed_a.astype(jnp.bfloat16)
    full_qkv, full_bqkv = fetch_forward(w_qkv, b_qkv)
    bias_qkv = full_bqkv.astype(jnp.float32)
    bias_full = jnp.concatenate(
        [bias_qkv[:model_width], jnp.zeros((model_width,), jnp.float32), bias_qkv[model_width:]]
    )
    projected = (product(normed_a_low, full_qkv) + bias_full).astype(jnp.bfloat16)
    query_heads = projected[:, :model_width].reshape(row_count, head_count, head_dim)
    key_heads = projected[:, model_width : 2 * model_width].reshape(row_count, head_count, head_dim)
    value_heads = projected[:, 2 * model_width :].reshape(row_count, head_count, head_dim)
    query_blocks = query_heads.reshape(block_count, block_rows, head_count, head_dim)
    id_blocks = image_ids.reshape(block_count, block_rows)

    def scores_of(query_block, id_block):
        raw_scores = (
            jnp.einsum("qhd,khd->hqk", query_block, key_heads, preferred_element_type=jnp.float32)
            * scale_factor
        )
        same_image = id_block[:, None] == image_ids[None, :]
        return jnp.where(same_image[None], raw_scores, MASKED)

    def forward_block(block_item):
        query_block, id_block = block_item
        scores = scores_of(query_block, id_block)
        row_max = jnp.max(scores, axis=-1, keepdims=True)
        exponent = jnp.exp(scores - row_max)
        row_total = jnp.sum(exponent, axis=-1, keepdims=True)
        probabilities = (exponent / row_total).astype(jnp.bfloat16)
        attended_block = jnp.einsum(
            "hqk,khd->qhd", probabilities, value_heads, preferred_element_type=jnp.float32
        )
        return (attended_block.astype(jnp.bfloat16), (row_max + jnp.log(row_total))[:, :, 0])

    attended_blocks, lse_blocks = lax.map(forward_block, (query_blocks, id_blocks))
    attended = attended_blocks.reshape(row_count, model_width)
    full_out, full_bout = fetch_forward(w_out, b_out)
    branch_a = product(attended, full_out) + full_bout.astype(jnp.float32)
    middle = hidden + gate_a * branch_a
    normed_b, pull_b = jax.vjp(modulate, middle, shift_b, scale_b)
    normed_b_low = normed_b.astype(jnp.bfloat16)
    full_up, full_bup = fetch_forward(w_up, b_up)
    inner_pre = product(normed_b_low, full_up) + full_bup.astype(jnp.float32)
    activated, gelu_pull = jax.vjp(gelu_tanh, inner_pre)
    activated_low = activated.astype(jnp.bfloat16)
    full_down, full_bdown = fetch_forward(w_down, b_down)
    branch_b = product(activated_low, full_down) + full_bdown.astype(jnp.float32)
    output = (middle + gate_b * branch_b).astype(jnp.bfloat16)
    grad_out = cotangent.astype(jnp.float32)
    grad_gate_b = grad_out * branch_b
    grad_branch_b = (gate_b * grad_out).astype(jnp.bfloat16)
    grad_w_down, grad_b_down = reduce_grads(
        outer_sum(activated_low, grad_branch_b), jnp.sum(grad_branch_b.astype(jnp.float32), axis=0)
    )
    back_down = weights_again(w_down)
    grad_activated = product_back(grad_branch_b, back_down)
    (grad_inner,) = gelu_pull(grad_activated)
    grad_inner_low = grad_inner.astype(jnp.bfloat16)
    grad_w_up, grad_b_up = reduce_grads(
        outer_sum(normed_b_low, grad_inner_low), jnp.sum(grad_inner_low.astype(jnp.float32), axis=0)
    )
    back_up = weights_again(w_up)
    grad_normed_b = product_back(grad_inner_low, back_up)
    grad_middle_norm, grad_shift_b, grad_scale_b = pull_b(grad_normed_b)
    grad_middle = grad_out + grad_middle_norm
    grad_gate_a = grad_middle * branch_a
    grad_branch_a = (gate_a * grad_middle).astype(jnp.bfloat16)
    grad_w_out, grad_b_out = reduce_grads(
        outer_sum(attended, grad_branch_a), jnp.sum(grad_branch_a.astype(jnp.float32), axis=0)
    )
    back_out = weights_again(w_out)
    grad_attended = product_back(grad_branch_a, back_out).astype(jnp.bfloat16)
    grad_att_blocks = grad_attended.reshape(block_count, block_rows, head_count, head_dim)

    def backward_block(carried, block_item):
        key_grad, value_grad = carried
        query_block, id_block, grad_block, lse_block = block_item
        scores = scores_of(query_block, id_block)
        probabilities = jnp.exp(scores - lse_block[:, :, None])
        probabilities_low = probabilities.astype(jnp.bfloat16)
        grad_probs = jnp.einsum(
            "qhd,khd->hqk", grad_block, value_heads, preferred_element_type=jnp.float32
        )
        row_delta = jnp.sum(probabilities * grad_probs, axis=-1, keepdims=True)
        grad_scores = (probabilities * (grad_probs - row_delta)).astype(jnp.bfloat16)
        query_grad = (
            jnp.einsum("hqk,khd->qhd", grad_scores, key_heads, preferred_element_type=jnp.float32)
            * scale_factor
        )
        key_grad = (
            key_grad
            + jnp.einsum(
                "hqk,qhd->khd", grad_scores, query_block, preferred_element_type=jnp.float32
            )
            * scale_factor
        )
        value_grad = value_grad + jnp.einsum(
            "hqk,qhd->khd", probabilities_low, grad_block, preferred_element_type=jnp.float32
        )
        return ((key_grad, value_grad), query_grad)

    zero_heads = jnp.zeros((row_count, head_count, head_dim), jnp.float32)
    (grad_keys, grad_values), grad_query_blocks = lax.scan(
        backward_block,
        (zero_heads, zero_heads),
        (query_blocks, id_blocks, grad_att_blocks, lse_blocks),
    )
    grad_projected = jnp.concatenate(
        [
            grad_query_blocks.reshape(row_count, model_width),
            grad_keys.reshape(row_count, model_width),
            grad_values.reshape(row_count, model_width),
        ],
        axis=1,
    ).astype(jnp.bfloat16)
    column_sums = jnp.sum(grad_projected.astype(jnp.float32), axis=0)
    grad_bias_qkv = jnp.concatenate([column_sums[:model_width], column_sums[2 * model_width :]])
    grad_w_qkv, grad_b_qkv = reduce_grads(outer_sum(normed_a_low, grad_projected), grad_bias_qkv)
    back_qkv = weights_again(w_qkv)
    grad_normed_a = product_back(grad_projected, back_qkv)
    grad_hidden_norm, grad_shift_a, grad_scale_a = pull_a(grad_normed_a)
    grad_input = grad_middle + grad_hidden_norm
    grad_per_token = jnp.concatenate(
        [grad_shift_a, grad_scale_a, grad_gate_a, grad_shift_b, grad_scale_b, grad_gate_b], axis=1
    )
    grad_modulation = lax.dot_general(
        selector, grad_per_token, (((0,), (0,)), ((), ())), precision=HIGHEST
    ).astype(jnp.bfloat16)
    grad_w_ada, grad_b_ada = reduce_grads(
        outer_sum(activ_low, grad_modulation), jnp.sum(grad_modulation.astype(jnp.float32), axis=0)
    )
    back_ada = weights_again(w_ada)
    grad_activ = product_back(grad_modulation, back_ada)
    (grad_cond,) = silu_pull(grad_activ)
    return (
        output,
        grad_input,
        grad_cond,
        grad_w_ada,
        grad_b_ada,
        grad_w_qkv,
        grad_b_qkv,
        grad_w_out,
        grad_b_out,
        grad_w_up,
        grad_b_up,
        grad_w_down,
        grad_b_down,
    )


MESH = pl.DeviceIdType.MESH
F32, BF16 = jnp.float32, jnp.bfloat16

def place():
    index = lax.axis_index("fsdp")
    return index // 4, (index // 2) % 2, index % 2

def peer(offset):
    y, x, core = place()
    y = 1 - y if offset & 4 else y
    x = 1 - x if offset & 2 else x
    core = 1 - core if offset & 1 else core
    return {"fsdp": y * 4 + x * 2 + core}

def greet(offsets):
    barrier = pltpu.get_barrier_semaphore()
    for offset in offsets:
        pl.semaphore_signal(barrier, inc=1, device_id=peer(offset), device_id_type=MESH)
    pl.semaphore_wait(barrier, len(offsets))

def remote(src, dst, send, recv, offset):
    return pltpu.make_async_remote_copy(src_ref=src, dst_ref=dst, send_sem=send, recv_sem=recv, device_id=peer(offset), device_id_type=MESH)

def nt(a, b):
    return lax.dot_general(a, b, (((1,), (1,)), ((), ())), preferred_element_type=F32)
def tn(a, b):
    return lax.dot_general(a, b, (((0,), (0,)), ((), ())), preferred_element_type=F32)
def nn(a, b):
    return jnp.dot(a, b, preferred_element_type=F32)

GELU_C = 0.7978845608028654
def gelu_parts(u):
    u2 = u * u
    t = jnp.tanh(GELU_C * u * (1.0 + 0.044715 * u2))
    half = 0.5 * (1.0 + t)
    act = u * half
    slope = half + 0.5 * u * (1.0 - t * t) * (GELU_C * (1.0 + 3 * 0.044715 * u2))
    return act, slope

def mlp_kernel(nb_ref, gbb_ref, wup_ref, bup_ref, wdn_ref,
               bb_ref, gnb_ref, gdn_ref, gup_ref, gbup_ref,
               nb_all, gbb_all, act_all, gi_all, mine, out_pair, in_pair, out_far, in_far,
               ag_send, ag_recv, fw_send, fw_recv, pr_send, pr_recv, far_send, far_recv):
    greet((1, 2, 4, 6))
    srcs = (nb_ref, gbb_ref)
    alls = (nb_all, gbb_all)
    sends = []
    for offset in (1, 2, 4, 6):
        for a in (0, 1):
            cp = remote(srcs[a], alls[a].at[offset], ag_send.at[a, offset], ag_recv.at[a, offset], offset)
            cp.start()
            sends.append(cp)
    nb_all[0] = nb_ref[...]
    gbb_all[0] = gbb_ref[...]
    def arrived(a, slot):
        return remote(alls[a].at[slot], alls[a].at[slot], ag_send.at[a, slot], ag_recv.at[a, slot], slot)
    def forward(a, slot):
        return remote(alls[a].at[slot], alls[a].at[slot + 1], fw_send.at[a, slot], fw_recv.at[a, slot], 1)

    def one(slot):
        inner = nn(nb_all[slot], wup_ref[...]) + bup_ref[...]
        act, slope = gelu_parts(inner)
        act = act.astype(BF16)
        act_all[slot] = act
        ga = nt(gbb_all[slot], wdn_ref[...])
        gi = (slope * ga).astype(BF16)
        gi_all[slot] = gi
        return nt(gi, wup_ref[...]), nn(act, wdn_ref[...])

    def pair_copy(a, p):
        return remote(out_pair.at[a, p], in_pair.at[a, p], pr_send.at[a, p], pr_recv.at[a, p], 1)
    def far_copy(a, p):
        return remote(out_far.at[a, p], in_far.at[a, p], far_send.at[a, p], far_recv.at[a, p], 2 * p)

    def finish(p):
        for a in (0, 1):
            pair_copy(a, p).wait()
            total = mine[a, p].astype(F32) + in_pair[a, p].astype(F32)
            if p == 0:
                (gnb_ref, bb_ref)[a][...] = total
            else:
                out_far[a, p] = total.astype(BF16)
                far_copy(a, p).start()

    for p in range(4):
        if p > 0:
            for a in (0, 1):
                arrived(a, 2 * p).wait_recv()
                forward(a, 2 * p).start()
        for h in (0, 1):
            slot = 2 * p + h
            if h == 1:
                for a in (0, 1):
                    if p == 0:
                        arrived(a, 1).wait_recv()
                    else:
                        forward(a, 2 * p).wait_recv()
            parts = one(slot)
            for a in (0, 1):
                if h == 0:
                    mine[a, p] = parts[a].astype(BF16)
                else:
                    out_pair[a, p] = parts[a].astype(BF16)
                    pair_copy(a, p).start()
        if p > 0:
            finish(p - 1)
    finish(3)
    hid = gdn_ref.shape[0]
    rows = nb_ref.shape[0]
    acts = act_all[...].reshape(8 * rows, hid)
    gis = gi_all[...].reshape(8 * rows, hid)
    gdn_ref[...] = tn(acts, gbb_all[...].reshape(8 * rows, -1)).astype(gdn_ref.dtype)
    gup_ref[...] = tn(nb_all[...].reshape(8 * rows, -1), gis).astype(gup_ref.dtype)
    gbup_ref[...] = jnp.sum(gis.astype(F32), axis=0, keepdims=True)
    for p in (1, 2, 3):
        for a in (0, 1):
            far_copy(a, p).wait()
            forward(a, 2 * p).wait_send()
            out = (gnb_ref, bb_ref)[a]
            out[...] += in_far[a, p].astype(F32)
    for cp in sends:
        cp.wait_send()

def mlp(nb, gbb, wup, bup, wdn):
    rows, width = nb.shape
    hid = wup.shape[1]
    S = jax.ShapeDtypeStruct
    vm = pl.BlockSpec(memory_space=pltpu.VMEM)
    dma = pltpu.SemaphoreType.DMA
    return pl.pallas_call(
        mlp_kernel,
        out_shape=(S((rows, width), F32), S((rows, width), F32), S((hid, width), BF16), S((width, hid), BF16), S((1, hid), F32)),
        in_specs=[vm] * 5, out_specs=(vm,) * 5,
        scratch_shapes=[
            pltpu.VMEM((8, rows, width), BF16), pltpu.VMEM((8, rows, width), BF16),
            pltpu.VMEM((8, rows, hid), BF16), pltpu.VMEM((8, rows, hid), BF16),
            pltpu.VMEM((2, 4, rows, width), BF16), pltpu.VMEM((2, 4, rows, width), BF16), pltpu.VMEM((2, 4, rows, width), BF16),
            pltpu.VMEM((2, 4, rows, width), BF16), pltpu.VMEM((2, 4, rows, width), BF16),
            dma((2, 8)), dma((2, 8)), dma((2, 8)), dma((2, 8)), dma((2, 4)), dma((2, 4)), dma((2, 4)), dma((2, 4)),
        ],
        compiler_params=pltpu.CompilerParams(collective_id=1, has_side_effects=True, vmem_limit_bytes=60 << 20),
    )(nb, gbb, wup, bup, wdn)


def fast(tokens, cond, image_sizes, w_ada, b_ada, w_qkv, b_qkv, w_out, b_out, w_up, b_up, w_down, b_down, cotangent):
    rows, width = tokens.shape
    heads, head_dim = H, width // H
    slots = image_sizes.shape[0]
    part = w_ada.shape[0]
    hid = w_down.shape[0]
    index = lax.axis_index("fsdp")
    core = index % 2
    order = jnp.arange(slots)
    image_ends = jnp.sum(jnp.where(order[:, None] >= order[None, :], image_sizes[None, :], 0), axis=1)
    ids = jnp.sum((jnp.arange(rows, dtype=jnp.int32)[:, None] >= image_ends[None, :]).astype(jnp.int32), axis=1)
    selector = (ids[:, None] == order[None, :]).astype(F32)
    full_qkv = lax.all_gather(w_qkv, "fsdp", axis=0, tiled=True)
    full_out = lax.all_gather(w_out, "fsdp", axis=0, tiled=True)
    biases = jnp.concatenate([b_ada, b_qkv, b_out, b_down])[None]
    biases = lax.all_gather(biases, "fsdp", axis=0, tiled=True).astype(F32)
    n_ada, n_qkv = b_ada.shape[0], b_qkv.shape[0]
    bias_ada = biases[:, :n_ada].reshape(-1)
    bias_qkv = biases[:, n_ada : n_ada + n_qkv].reshape(-1)
    bias_out = biases[:, n_ada + n_qkv : n_ada + n_qkv + part].reshape(-1)
    bias_down = biases[:, n_ada + n_qkv + part :].reshape(-1)
    activ, silu_pull = jax.vjp(jax.nn.silu, cond.astype(F32))
    activ_low = activ.astype(BF16)
    activ_plane = lax.all_gather(activ_low, "fsdp", axis=0, tiled=True)
    mine = lax.dynamic_slice(activ_plane, (0, index * part), (activ_plane.shape[0], part))
    modulation = lax.psum_scatter(nn(mine, w_ada), "fsdp", scatter_dimension=0, tiled=True) + bias_ada
    per_token = jnp.dot(selector, modulation, precision=HIGHEST)
    shift_a, scale_a, gate_a, shift_b, scale_b, gate_b = jnp.split(per_token, 6, axis=1)
    hidden = tokens.astype(F32)
    grad_out = cotangent.astype(F32)
    gbb = (gate_b * grad_out).astype(BF16)
    normed_a, pull_a = jax.vjp(modulate, hidden, shift_a, scale_a)
    na = normed_a.astype(BF16)
    bias_full = jnp.concatenate([bias_qkv[:width], jnp.zeros((width,), F32), bias_qkv[width:]])
    projected = (nn(na, full_qkv) + bias_full).astype(BF16)
    q, k, v = [projected[:, i * width : (i + 1) * width].reshape(rows, heads, head_dim) for i in range(3)]
    scale = head_dim ** (-0.5)
    scores = jnp.einsum("qhd,khd->hqk", q, k, preferred_element_type=F32) * scale
    scores = jnp.where((ids[:, None] == ids[None, :])[None], scores, MASKED)
    exponent = jnp.exp(scores - jnp.max(scores, axis=-1, keepdims=True))
    probs = exponent / jnp.sum(exponent, axis=-1, keepdims=True)
    probs_low = probs.astype(BF16)
    attended = jnp.einsum("hqk,khd->qhd", probs_low, v, preferred_element_type=F32).astype(BF16).reshape(rows, width)
    branch_a = nn(attended, full_out) + bias_out
    middle = hidden + gate_a * branch_a
    normed_b, pull_b = jax.vjp(modulate, middle, shift_b, scale_b)
    nb = normed_b.astype(BF16)
    wide = hid + 64
    pieces = [
        w_up[:, 2 * hid * (j // 2) + (2 * hid - wide) * (j % 2) :][:, :wide] for j in range(8)
    ]
    wup = lax.all_to_all(jnp.stack(pieces), "fsdp", 0, 0, tiled=True).reshape(width, wide)
    place_row = core * (wide - hid)
    wdn = lax.dynamic_update_slice(jnp.zeros((wide, width), BF16), w_down, (place_row, 0))
    bup = lax.dynamic_update_slice(jnp.zeros((1, wide), F32), b_up.astype(F32)[None], (0, place_row))
    branch_b, grad_nb, gdn, gup, gbup = mlp(nb, gbb, wup, bup, wdn)
    branch_b = branch_b + bias_down
    output = (middle + gate_b * branch_b).astype(BF16)
    grad_gate_b = grad_out * branch_b
    grad_middle_norm, grad_shift_b, grad_scale_b = pull_b(grad_nb)
    grad_middle = grad_out + grad_middle_norm
    grad_gate_a = grad_middle * branch_a
    gba = (gate_a * grad_middle).astype(BF16)
    gout = tn(attended, gba).astype(BF16)
    gatt = nt(gba, full_out).astype(BF16).reshape(rows, heads, head_dim)
    grad_probs = jnp.einsum("qhd,khd->hqk", gatt, v, preferred_element_type=F32)
    delta = jnp.sum(probs * grad_probs, axis=-1, keepdims=True)
    grad_scores = (probs * (grad_probs - delta)).astype(BF16)
    gq = jnp.einsum("hqk,khd->qhd", grad_scores, k, preferred_element_type=F32) * scale
    gk = jnp.einsum("hqk,qhd->khd", grad_scores, q, preferred_element_type=F32) * scale
    gv = jnp.einsum("hqk,qhd->khd", probs_low, gatt, preferred_element_type=F32)
    gp = jnp.concatenate([t.reshape(rows, width) for t in (gq, gk, gv)], axis=1).astype(BF16)
    gqkv = tn(na, gp).astype(BF16)
    grad_na = nt(gp, full_qkv)
    grad_norm, grad_shift_a, grad_scale_a = pull_a(grad_na)
    grad_input = grad_middle + grad_norm
    grad_mod = lax.dot_general(
        selector,
        jnp.concatenate([grad_shift_a, grad_scale_a, grad_gate_a, grad_shift_b, grad_scale_b, grad_gate_b], axis=1),
        (((0,), (0,)), ((), ())),
        precision=HIGHEST,
    ).astype(BF16)
    both = ("fsdp", "rep")
    mod_all = lax.all_gather(grad_mod, both, axis=0, tiled=True)
    activ_all = lax.all_gather(activ_low, both, axis=0, tiled=True)
    g_ada = tn(lax.dynamic_slice(activ_all, (0, index * part), (activ_all.shape[0], part)), mod_all)
    g_bada = lax.dynamic_slice(jnp.sum(mod_all.astype(F32), axis=0), (index * n_ada,), (n_ada,))
    mod_plane = lax.all_gather(grad_mod, "fsdp", axis=0, tiled=True)
    back = nt(mod_plane, w_ada)
    grad_activ = lax.all_to_all(back.reshape(8, slots, part), "fsdp", 0, 0, tiled=True)
    (grad_cond,) = silu_pull(grad_activ.transpose(1, 0, 2).reshape(slots, width))
    cols = jnp.sum(gp.astype(F32), axis=0)
    vector = jnp.concatenate(
        [cols[:width], cols[2 * width :], jnp.sum(gba.astype(F32), axis=0), jnp.sum(gbb.astype(F32), axis=0)]
    )
    vector = lax.psum(vector, both)
    g_bqkv = lax.dynamic_slice(vector[: 2 * width], (index * n_qkv,), (n_qkv,))
    g_bout = lax.dynamic_slice(vector[2 * width : 3 * width], (index * part,), (part,))
    g_bdown = lax.dynamic_slice(vector[3 * width :], (index * part,), (part,))
    g_bup = lax.psum(lax.dynamic_slice(gbup[0], (place_row,), (hid,)), "rep")
    own_qkv = lax.psum_scatter(gqkv, "fsdp", scatter_dimension=0, tiled=True)
    own_out = lax.psum_scatter(gout, "fsdp", scatter_dimension=0, tiled=True)
    got = lax.all_to_all(gup.reshape(8, part, wide), "fsdp", 0, 0, tiled=True).astype(F32)
    lap = wide - hid
    strips = []
    for c in range(4):
        left, right = got[2 * c], got[2 * c + 1]
        strips += [left[:, : hid - lap], left[:, hid - lap :] + right[:, : 2 * lap], right[:, 2 * lap :]]
    own_up = jnp.concatenate(strips, axis=1).astype(BF16)
    own_down = lax.dynamic_slice(gdn, (place_row, 0), (hid, width))
    g_qkv, g_out, g_up, g_down = [
        lax.psum(t, "rep").astype(F32) for t in (own_qkv, own_out, own_up, own_down)
    ]
    return (output, grad_input, grad_cond, g_ada, g_bada, g_qkv, g_bqkv, g_out, g_bout, g_up, g_bup, g_down, g_bdown)


def solution(mesh):
    placed = (
        P(("fsdp", "rep"), None),
        P(("fsdp", "rep"), None),
        P(("fsdp", "rep")),
        P("fsdp", None),
        P("fsdp"),
        P("fsdp", None),
        P("fsdp"),
        P("fsdp", None),
        P("fsdp"),
        P("fsdp", None),
        P("fsdp"),
        P("fsdp", None),
        P("fsdp"),
        P(("fsdp", "rep"), None),
    )
    fits = mesh.shape["fsdp"] == 8
    return jax.shard_map(
        fast if fits else local,
        mesh=mesh,
        in_specs=placed,
        out_specs=(
            P(("fsdp", "rep"), None),
            P(("fsdp", "rep"), None),
            P(("fsdp", "rep"), None),
            P("fsdp", None),
            P("fsdp"),
            P("fsdp", None),
            P("fsdp"),
            P("fsdp", None),
            P("fsdp"),
            P("fsdp", None),
            P("fsdp"),
            P("fsdp", None),
            P("fsdp"),
        ),
        check_vma=False,
    )
```

```python
import functools

import jax
import jax.numpy as jnp
from jax import lax
from jax.experimental import pallas as pl
from jax.experimental.pallas import tpu as pltpu
from jax.sharding import PartitionSpec as P

H = 16
EPSILON = 1e-06
HIGHEST = lax.Precision.HIGHEST
MASKED = -1e30


def layer_norm(inputs):
    average = jnp.mean(inputs, axis=-1, keepdims=True)
    centered = inputs - average
    variance = jnp.mean(centered * centered, axis=-1, keepdims=True)
    return centered * lax.rsqrt(variance + EPSILON)


def modulate(hidden, shift_part, scale_part):
    return layer_norm(hidden) * (1.0 + scale_part) + shift_part


def gelu_tanh(inputs):
    return jax.nn.gelu(inputs, approximate=True)


def product(first_operand, second_operand):
    return jnp.dot(first_operand, second_operand, preferred_element_type=jnp.float32)


def product_back(first_operand, second_operand):
    return lax.dot_general(
        first_operand, second_operand, (((1,), (1,)), ((), ())), preferred_element_type=jnp.float32
    )


def outer_sum(first_operand, second_operand):
    return lax.dot_general(
        first_operand, second_operand, (((0,), (0,)), ((), ())), preferred_element_type=jnp.float32
    )


def fetch_forward(weight, bias_piece):
    return (
        lax.all_gather(weight, "fsdp", axis=0, tiled=True),
        lax.all_gather(bias_piece, "fsdp", axis=0, tiled=True),
    )


def weights_again(weight):
    return lax.all_gather(weight, "fsdp", axis=0, tiled=True)


def reduce_grads(weight_grad, bias_grad):
    row_part, bias_part = (
        lax.psum_scatter(weight_grad, "fsdp", scatter_dimension=0, tiled=True),
        lax.psum_scatter(bias_grad, "fsdp", scatter_dimension=0, tiled=True),
    )
    column_part = lax.psum_scatter(row_part, "rep", scatter_dimension=1, tiled=True)
    whole_rows, bias_stack = (
        lax.all_gather(column_part, "rep", axis=1, tiled=True),
        lax.all_gather(bias_part[None], "rep", axis=0, tiled=True),
    )
    return (whole_rows, jnp.sum(bias_stack, axis=0))


def local(
    tokens,
    cond,
    image_sizes,
    w_ada,
    b_ada,
    w_qkv,
    b_qkv,
    w_out,
    b_out,
    w_up,
    b_up,
    w_down,
    b_down,
    cotangent,
):
    row_count, model_width = tokens.shape
    head_count = H
    head_dim = model_width // head_count
    slot_count = image_sizes.shape[0]
    scale_factor = head_dim ** (-0.5)
    block_rows = min(512, row_count)
    block_count = row_count // block_rows
    image_ends = jnp.sum(
        jnp.where(jnp.arange(slot_count)[:, None] >= jnp.arange(slot_count)[None, :], image_sizes[None, :], 0), axis=1
    )
    positions = jnp.arange(row_count, dtype=jnp.int32)
    image_ids = jnp.sum((positions[:, None] >= image_ends[None, :]).astype(jnp.int32), axis=1)
    selector = (image_ids[:, None] == jnp.arange(slot_count, dtype=jnp.int32)[None, :]).astype(
        jnp.float32
    )
    cond_float = cond.astype(jnp.float32)
    activ_float, silu_pull = jax.vjp(jax.nn.silu, cond_float)
    activ_low = activ_float.astype(jnp.bfloat16)
    full_ada, full_bada = fetch_forward(w_ada, b_ada)
    modulation = product(activ_low, full_ada) + full_bada.astype(jnp.float32)
    per_token = jnp.dot(selector, modulation, precision=HIGHEST)
    shift_a, scale_a, gate_a, shift_b, scale_b, gate_b = jnp.split(per_token, 6, axis=1)
    hidden = tokens.astype(jnp.float32)
    normed_a, pull_a = jax.vjp(modulate, hidden, shift_a, scale_a)
    normed_a_low = normed_a.astype(jnp.bfloat16)
    full_qkv, full_bqkv = fetch_forward(w_qkv, b_qkv)
    bias_qkv = full_bqkv.astype(jnp.float32)
    bias_full = jnp.concatenate(
        [bias_qkv[:model_width], jnp.zeros((model_width,), jnp.float32), bias_qkv[model_width:]]
    )
    projected = (product(normed_a_low, full_qkv) + bias_full).astype(jnp.bfloat16)
    query_heads = projected[:, :model_width].reshape(row_count, head_count, head_dim)
    key_heads = projected[:, model_width : 2 * model_width].reshape(row_count, head_count, head_dim)
    value_heads = projected[:, 2 * model_width :].reshape(row_count, head_count, head_dim)
    query_blocks = query_heads.reshape(block_count, block_rows, head_count, head_dim)
    id_blocks = image_ids.reshape(block_count, block_rows)

    def scores_of(query_block, id_block):
        raw_scores = (
            jnp.einsum("qhd,khd->hqk", query_block, key_heads, preferred_element_type=jnp.float32)
            * scale_factor
        )
        same_image = id_block[:, None] == image_ids[None, :]
        return jnp.where(same_image[None], raw_scores, MASKED)

    def forward_block(block_item):
        query_block, id_block = block_item
        scores = scores_of(query_block, id_block)
        row_max = jnp.max(scores, axis=-1, keepdims=True)
        exponent = jnp.exp(scores - row_max)
        row_total = jnp.sum(exponent, axis=-1, keepdims=True)
        probabilities = (exponent / row_total).astype(jnp.bfloat16)
        attended_block = jnp.einsum(
            "hqk,khd->qhd", probabilities, value_heads, preferred_element_type=jnp.float32
        )
        return (attended_block.astype(jnp.bfloat16), (row_max + jnp.log(row_total))[:, :, 0])

    attended_blocks, lse_blocks = lax.map(forward_block, (query_blocks, id_blocks))
    attended = attended_blocks.reshape(row_count, model_width)
    full_out, full_bout = fetch_forward(w_out, b_out)
    branch_a = product(attended, full_out) + full_bout.astype(jnp.float32)
    middle = hidden + gate_a * branch_a
    normed_b, pull_b = jax.vjp(modulate, middle, shift_b, scale_b)
    normed_b_low = normed_b.astype(jnp.bfloat16)
    full_up, full_bup = fetch_forward(w_up, b_up)
    inner_pre = product(normed_b_low, full_up) + full_bup.astype(jnp.float32)
    activated, gelu_pull = jax.vjp(gelu_tanh, inner_pre)
    activated_low = activated.astype(jnp.bfloat16)
    full_down, full_bdown = fetch_forward(w_down, b_down)
    branch_b = product(activated_low, full_down) + full_bdown.astype(jnp.float32)
    output = (middle + gate_b * branch_b).astype(jnp.bfloat16)
    grad_out = cotangent.astype(jnp.float32)
    grad_gate_b = grad_out * branch_b
    grad_branch_b = (gate_b * grad_out).astype(jnp.bfloat16)
    grad_w_down, grad_b_down = reduce_grads(
        outer_sum(activated_low, grad_branch_b), jnp.sum(grad_branch_b.astype(jnp.float32), axis=0)
    )
    back_down = weights_again(w_down)
    grad_activated = product_back(grad_branch_b, back_down)
    (grad_inner,) = gelu_pull(grad_activated)
    grad_inner_low = grad_inner.astype(jnp.bfloat16)
    grad_w_up, grad_b_up = reduce_grads(
        outer_sum(normed_b_low, grad_inner_low), jnp.sum(grad_inner_low.astype(jnp.float32), axis=0)
    )
    back_up = weights_again(w_up)
    grad_normed_b = product_back(grad_inner_low, back_up)
    grad_middle_norm, grad_shift_b, grad_scale_b = pull_b(grad_normed_b)
    grad_middle = grad_out + grad_middle_norm
    grad_gate_a = grad_middle * branch_a
    grad_branch_a = (gate_a * grad_middle).astype(jnp.bfloat16)
    grad_w_out, grad_b_out = reduce_grads(
        outer_sum(attended, grad_branch_a), jnp.sum(grad_branch_a.astype(jnp.float32), axis=0)
    )
    back_out = weights_again(w_out)
    grad_attended = product_back(grad_branch_a, back_out).astype(jnp.bfloat16)
    grad_att_blocks = grad_attended.reshape(block_count, block_rows, head_count, head_dim)

    def backward_block(carried, block_item):
        key_grad, value_grad = carried
        query_block, id_block, grad_block, lse_block = block_item
        scores = scores_of(query_block, id_block)
        probabilities = jnp.exp(scores - lse_block[:, :, None])
        probabilities_low = probabilities.astype(jnp.bfloat16)
        grad_probs = jnp.einsum(
            "qhd,khd->hqk", grad_block, value_heads, preferred_element_type=jnp.float32
        )
        row_delta = jnp.sum(probabilities * grad_probs, axis=-1, keepdims=True)
        grad_scores = (probabilities * (grad_probs - row_delta)).astype(jnp.bfloat16)
        query_grad = (
            jnp.einsum("hqk,khd->qhd", grad_scores, key_heads, preferred_element_type=jnp.float32)
            * scale_factor
        )
        key_grad = (
            key_grad
            + jnp.einsum(
                "hqk,qhd->khd", grad_scores, query_block, preferred_element_type=jnp.float32
            )
            * scale_factor
        )
        value_grad = value_grad + jnp.einsum(
            "hqk,qhd->khd", probabilities_low, grad_block, preferred_element_type=jnp.float32
        )
        return ((key_grad, value_grad), query_grad)

    zero_heads = jnp.zeros((row_count, head_count, head_dim), jnp.float32)
    (grad_keys, grad_values), grad_query_blocks = lax.scan(
        backward_block,
        (zero_heads, zero_heads),
        (query_blocks, id_blocks, grad_att_blocks, lse_blocks),
    )
    grad_projected = jnp.concatenate(
        [
            grad_query_blocks.reshape(row_count, model_width),
            grad_keys.reshape(row_count, model_width),
            grad_values.reshape(row_count, model_width),
        ],
        axis=1,
    ).astype(jnp.bfloat16)
    column_sums = jnp.sum(grad_projected.astype(jnp.float32), axis=0)
    grad_bias_qkv = jnp.concatenate([column_sums[:model_width], column_sums[2 * model_width :]])
    grad_w_qkv, grad_b_qkv = reduce_grads(outer_sum(normed_a_low, grad_projected), grad_bias_qkv)
    back_qkv = weights_again(w_qkv)
    grad_normed_a = product_back(grad_projected, back_qkv)
    grad_hidden_norm, grad_shift_a, grad_scale_a = pull_a(grad_normed_a)
    grad_input = grad_middle + grad_hidden_norm
    grad_per_token = jnp.concatenate(
        [grad_shift_a, grad_scale_a, grad_gate_a, grad_shift_b, grad_scale_b, grad_gate_b], axis=1
    )
    grad_modulation = lax.dot_general(
        selector, grad_per_token, (((0,), (0,)), ((), ())), precision=HIGHEST
    ).astype(jnp.bfloat16)
    grad_w_ada, grad_b_ada = reduce_grads(
        outer_sum(activ_low, grad_modulation), jnp.sum(grad_modulation.astype(jnp.float32), axis=0)
    )
    back_ada = weights_again(w_ada)
    grad_activ = product_back(grad_modulation, back_ada)
    (grad_cond,) = silu_pull(grad_activ)
    return (
        output,
        grad_input,
        grad_cond,
        grad_w_ada,
        grad_b_ada,
        grad_w_qkv,
        grad_b_qkv,
        grad_w_out,
        grad_b_out,
        grad_w_up,
        grad_b_up,
        grad_w_down,
        grad_b_down,
    )


MESH = pl.DeviceIdType.MESH
F32, BF16 = jnp.float32, jnp.bfloat16


def flipped(offset):
    index = lax.axis_index("fsdp")
    y, x, core = index // 4, (index // 2) % 2, index % 2
    y = 1 - y if offset & 4 else y
    x = 1 - x if offset & 2 else x
    core = 1 - core if offset & 1 else core
    return y * 4 + x * 2 + core


def greet(offsets):
    barrier = pltpu.get_barrier_semaphore()
    for offset in offsets:
        pl.semaphore_signal(barrier, inc=1, device_id={"fsdp": flipped(offset)}, device_id_type=MESH)
    pl.semaphore_wait(barrier, len(offsets))


def remote(src, dst, send, recv, offset):
    return pltpu.make_async_remote_copy(
        src_ref=src, dst_ref=dst, send_sem=send, recv_sem=recv,
        device_id={"fsdp": flipped(offset)}, device_id_type=MESH,
    )


class Gather:
    def __init__(self, whole, send, recv, lead):
        rows = whole.shape[1]
        first, second = pl.ds(0, lead), pl.ds(lead, rows - lead)
        piece = {e: whole.at[flipped(e)] for e in (0, 2, 4, 6)}
        plan = (
            (piece[0], 1), (piece[0], 2), (piece[0], 4),
            (piece[2].at[first], 4), (piece[4].at[second], 2),
            (piece[2], 1), (piece[4], 1), (piece[6], 1),
        )
        self.copies = [remote(ref, ref, send.at[i], recv.at[i], e) for i, (ref, e) in enumerate(plan)]

    def own(self):
        for i in (1, 2, 0):
            self.copies[i].start()

    def along_x(self):
        self.copies[1].wait_recv()
        self.copies[3].start()
        self.copies[5].start()

    def along_y(self):
        self.copies[2].wait_recv()
        self.copies[4].start()
        self.copies[6].start()

    def across(self):
        self.copies[3].wait_recv()
        self.copies[4].wait_recv()
        self.copies[7].start()

    def finish(self, sends=True):
        for i in (0, 5, 6, 7):
            self.copies[i].wait_recv()

    def drain(self):
        for copy in self.copies:
            copy.wait_send()


def nt(a, b):
    return lax.dot_general(a, b, (((1,), (1,)), ((), ())), preferred_element_type=F32)


def tn(a, b):
    return lax.dot_general(a, b, (((0,), (0,)), ((), ())), preferred_element_type=F32)


def nn(a, b):
    return jnp.dot(a, b, preferred_element_type=F32)


def normalized(values):
    centered = values - jnp.mean(values, axis=-1, keepdims=True)
    variance = jnp.mean(centered * centered, axis=-1, keepdims=True)
    scale = lax.rsqrt(variance + EPSILON)
    return centered * scale, scale


def image_of(place, sizes_ref):
    end = jnp.int32(0)
    image = jnp.zeros(place.shape, jnp.int32)
    for j in range(sizes_ref.shape[0]):
        end = end + sizes_ref[j]
        image = image + (place >= end).astype(jnp.int32)
    return image


def per_row(selectors, modulation, part, width):
    total = None
    for j, chosen in enumerate(selectors):
        term = chosen * modulation[j : j + 1, part * width : (part + 1) * width]
        total = term if total is None else total + term
    return total


def head_window(head, head_dim):
    low = head * head_dim
    base = low // 128 * 128
    wide = 128 if low - base + head_dim <= 128 else 256
    lane = lax.broadcasted_iota(jnp.int32, (1, wide), 1) + (base - low)
    mask = jnp.where((lane >= 0) & (lane < head_dim), 1.0, 0.0)
    return base, wide, mask


def start_kernel(
    sizes_ref, tok_ref, cot_ref, cond_ref, wada_ref, bada_ref, obias_ref, wqkv_ref, wout_ref, wup_ref,
    mod_ref, na_ref, proj_ref, probs_ref, att_ref, bra_ref, mid_ref, nb_ref, gbb_all, wq_all, wo_all, wup_all, pick_ref,
    act_all, pm, mpair, mfar,
    loc_sem, act_send, act_recv, mp_send, mp_recv, mf_send, mf_recv, up_send, up_recv,
    q_send, q_recv, o_send, o_recv, g_send, g_recv,
):
    rows, width = tok_ref.shape
    head_dim = width // H
    slots = sizes_ref.shape[0]
    part = wada_ref.shape[0]
    wide = wup_all.shape[2]
    hid = (wup_ref.shape[1]) // 8
    me = flipped(0)
    others = range(1, 8)

    def up_piece(e):
        j = flipped(e)
        begin = pl.multiple_of(2 * hid * (j // 2) + (2 * hid - wide) * (j % 2), 128)
        return wup_ref.at[:, pl.ds(begin, wide)]

    local = [
        pltpu.make_async_copy(wqkv_ref, wq_all.at[me], loc_sem.at[0]),
        pltpu.make_async_copy(wout_ref, wo_all.at[me], loc_sem.at[1]),
        pltpu.make_async_copy(up_piece(0), wup_all.at[me], loc_sem.at[2]),
    ]
    for copy in local:
        copy.start()
    act = jax.nn.silu(cond_ref[...])
    act_all[me] = act
    qkv, out, gbb = (
        Gather(wq_all, q_send, q_recv, 80), Gather(wo_all, o_send, o_recv, 80), Gather(gbb_all, g_send, g_recv, rows // 2)
    )
    acts = [remote(act_all.at[me], act_all.at[me], act_send.at[e], act_recv.at[e], e) for e in others]
    ups = [remote(up_piece(e), wup_all.at[me], up_send.at[e], up_recv.at[e], e) for e in others]
    pairs = [remote(pm.at[flipped(2 * p + 1)], mpair.at[p], mp_send.at[p], mp_recv.at[p], 1) for p in range(4)]
    fars = [remote(pm.at[flipped(2 * p)], mfar.at[p], mf_send.at[p], mf_recv.at[p], 2 * p) for p in range(1, 4)]

    greet(others)
    for copy in acts:
        copy.start()
    local[0].wait()
    qkv.own()
    for copy in acts:
        copy.wait_recv()
    everyone = act_all[...].reshape(8 * act_all.shape[1], width).astype(BF16)
    pick = (
        lax.broadcasted_iota(jnp.int32, (width, part), 0) == lax.broadcasted_iota(jnp.int32, (width, part), 1) + me * part
    )
    chosen = nn(everyone, jnp.where(pick, 1.0, 0.0).astype(BF16)).astype(BF16)
    pick_ref[...] = chosen
    bias_row = lax.broadcasted_iota(jnp.int32, (8, 1), 0) == slots
    piece = nn(chosen, wada_ref[...]).reshape(pm.shape)
    pm[...] = jnp.where(bias_row[None], obias_ref[...][None], piece + bada_ref[...][None])
    for copy in pairs:
        copy.start()
    for p in range(4):
        pairs[p].wait_recv()
        pm[flipped(2 * p)] += mpair[p]
        if p:
            fars[p - 1].start()
    qkv.along_x()
    qkv.along_y()
    local[1].wait()
    out.own()
    for copy in fars:
        copy.wait_recv()
    modulation = pm[me] + (mfar[1] + mfar[2] + mfar[3])
    mod_ref[...] = modulation
    bias = modulation[slots : slots + 1]
    image = image_of(lax.broadcasted_iota(jnp.int32, (rows, 1), 0), sizes_ref)
    selectors = [jnp.where(image == j, 1.0, 0.0) for j in range(slots)]
    gate_b = per_row(selectors, mod_ref, 5, width)
    gbb_all[me] = (gate_b * cot_ref[...].astype(F32)).astype(BF16)
    hidden = tok_ref[...].astype(F32)
    na_ref[...] = (
        normalized(hidden)[0] * (1.0 + per_row(selectors, mod_ref, 1, width)) + per_row(selectors, mod_ref, 0, width)
    ).astype(BF16)
    qkv.across()
    gbb.own()
    for copy in ups:
        copy.start()
    qkv.finish()
    for i in range(3):
        block = wq_all[:, :, i * width : (i + 1) * width].reshape(width, width)
        value = nn(na_ref[...], block)
        if i == 0:
            value = value + bias[:, :width]
        if i == 2:
            value = value + bias[:, width : 2 * width]
        proj_ref[:, i * width : (i + 1) * width] = value.astype(BF16)
    out.along_x()
    out.along_y()
    att_ref[...] = jnp.zeros_like(att_ref)
    row_image = image_of(lax.broadcasted_iota(jnp.int32, (rows, rows), 0), sizes_ref)
    column_image = image_of(lax.broadcasted_iota(jnp.int32, (rows, rows), 1), sizes_ref)
    hidden_pairs = jnp.where(row_image == column_image, 0.0, -1e30)
    for head in range(H):
        base, window, mask = head_window(head, head_dim)
        mask = mask.astype(BF16)
        query = proj_ref[:, base : base + window] * mask
        key = proj_ref[:, width + base : width + base + window]
        value = proj_ref[:, 2 * width + base : 2 * width + base + window] * mask
        scores = nt(query, key) * head_dim ** (-0.5) + hidden_pairs
        exponent = jnp.exp(scores - jnp.max(scores, axis=-1, keepdims=True))
        probs = (exponent * (1.0 / jnp.sum(exponent, axis=-1, keepdims=True))).astype(BF16)
        probs_ref[head] = probs
        att_ref[:, base : base + window] += nn(probs, value).astype(BF16)
        if head == 3:
            out.across()
        if head == 7:
            gbb.along_x()
            gbb.along_y()
    out.finish()
    branch = nn(att_ref[...], wo_all[...].reshape(width, width)) + bias[:, 2 * width : 3 * width]
    bra_ref[...] = branch
    middle = tok_ref[...].astype(F32) + per_row(selectors, mod_ref, 2, width) * branch
    mid_ref[...] = middle
    nb_ref[...] = (
        normalized(middle)[0] * (1.0 + per_row(selectors, mod_ref, 4, width)) + per_row(selectors, mod_ref, 3, width)
    ).astype(BF16)
    gbb.across()
    gbb.finish()
    local[2].wait()
    for copy in ups:
        copy.wait()
    for copy in acts + pairs + fars:
        copy.wait_send()
    for gather in (qkv, out, gbb):
        gather.drain()


def start(sizes, tok, cot, cond, wada, bada, obias, wqkv, wout, wup, wide):
    rows, width = tok.shape
    part = wada.shape[0]
    columns = wada.shape[1]
    S = jax.ShapeDtypeStruct
    vm, hbm = pl.BlockSpec(memory_space=pltpu.VMEM), pl.BlockSpec(memory_space=pl.ANY)
    dma = pltpu.SemaphoreType.DMA
    shapes = (
        S((8, columns), F32), S((rows, width), BF16), S((rows, 3 * width), BF16), S((H, rows, rows), BF16),
        S((rows, width), BF16), S((rows, width), F32), S((rows, width), F32), S((rows, width), BF16),
        S((8, rows, width), BF16), S((8, part, 3 * width), BF16), S((8, part, width), BF16), S((8, part, wide), BF16),
        S((64, part), BF16),
    )
    return pl.pallas_call(
        start_kernel,
        out_shape=shapes,
        in_specs=[pl.BlockSpec(memory_space=pltpu.SMEM)] + [vm] * 6 + [hbm] * 3,
        out_specs=(vm,) * len(shapes),
        scratch_shapes=[
            pltpu.VMEM((8, 8, width), F32), pltpu.VMEM((8, 8, columns), F32), pltpu.VMEM((4, 8, columns), F32),
            pltpu.VMEM((4, 8, columns), F32),
            dma((3,)), dma((8,)), dma((8,)), dma((4,)), dma((4,)), dma((4,)), dma((4,)), dma((8,)), dma((8,)),
        ] + [dma((8,))] * 6,
        compiler_params=pltpu.CompilerParams(collective_id=0, has_side_effects=True, vmem_limit_bytes=60 << 20),
    )(sizes, tok, cot, cond, wada, bada, obias, wqkv, wout, wup)

GELU_RATE = 0.7978845608028654
GELU_CUBE = 0.044715


def gelu_parts(u):
    square = u * u
    bend = jnp.tanh(GELU_RATE * u * (1.0 + GELU_CUBE * square))
    half = 0.5 * (1.0 + bend)
    slope = half + 0.5 * u * (1.0 - bend * bend) * (GELU_RATE * (1.0 + 3.0 * GELU_CUBE * square))
    return u * half, slope


def mlp_kernel(
    nb_ref, gbb_all, wup_ref, bup_ref, wdn_ref,
    gnb_ref, bb_ref, gdn_ref, gup_ref, gbup_ref,
    nb_all, act_all, gi_all, out_pair, in_pair, in_far,
    n_send, n_recv, pr_send, pr_recv, far_send, far_recv, gnb_mine,
):
    rows, width = nb_ref.shape
    hid = wdn_ref.shape[0]
    me = flipped(0)
    nb = Gather(nb_all, n_send, n_recv, rows // 2)
    pairs = [[remote(out_pair.at[a, p], in_pair.at[a, p], pr_send.at[a, p], pr_recv.at[a, p], 1) for p in range(4)] for a in (0, 1)]
    mine = (gnb_mine, bb_ref)
    fars = [remote(gnb_mine.at[p], in_far.at[p], far_send.at[p], far_recv.at[p], 2 * p) for p in (1, 2, 3)]
    nb_all[me] = nb_ref[...]
    greet((1, 2, 4, 6))
    nb.own()

    def one(slot):
        inner = nn(nb_all[slot], wup_ref[...]) + bup_ref[...]
        act, slope = gelu_parts(inner)
        act_all[slot] = act.astype(BF16)
        gi_all[slot] = (slope * nt(gbb_all[slot], wdn_ref[...])).astype(BF16)

    def back(slot):
        return nt(gi_all[slot], wup_ref[...]).astype(BF16)

    def forth(slot):
        return nn(act_all[slot], wdn_ref[...]).astype(BF16)

    def combine(a, p):
        pairs[a][p].wait_recv()
        mine[a][p] = (mine[a][p].astype(F32) + in_pair[a, p].astype(F32)).astype(BF16)

    waits = {1: 0, 3: 5, 5: 6, 7: 7}
    for p in range(4):
        even, odd = flipped(2 * p), flipped(2 * p + 1)
        if p == 1:
            nb.along_x()
        if p == 2:
            nb.along_y()
        if p == 3:
            nb.across()
        one(even)
        gnb_mine[p] = back(even)
        nb.copies[waits[2 * p + 1]].wait_recv()
        one(odd)
        out_pair[0, p] = back(odd)
        pairs[0][p].start()
        bb_ref[p] = forth(even)
        out_pair[1, p] = forth(odd)
        pairs[1][p].start()
        combine(0, p)
        if p:
            fars[p - 1].start()
    gdn_ref[...] = tn(act_all[...].reshape(8 * rows, hid), gbb_all[...].reshape(8 * rows, width)).astype(BF16)
    inner_grads = gi_all[...].reshape(8 * rows, hid)
    gup_ref[...] = tn(nb_all[...].reshape(8 * rows, width), inner_grads).astype(BF16).reshape(gup_ref.shape)
    gbup_ref[...] = jnp.sum(inner_grads.astype(F32), axis=0, keepdims=True)
    for p in range(4):
        combine(1, p)
    total = gnb_mine[0].astype(F32)
    for p in (1, 2, 3):
        fars[p - 1].wait()
        total = total + in_far[p].astype(F32)
    gnb_ref[...] = total
    for a in (0, 1):
        for p in range(4):
            pairs[a][p].wait_send()
    nb.drain()


def mlp(nb, gbb_all, wup, bup, wdn):
    rows, width = nb.shape
    hid = wup.shape[1]
    S = jax.ShapeDtypeStruct
    vm = pl.BlockSpec(memory_space=pltpu.VMEM)
    dma = pltpu.SemaphoreType.DMA
    part = width // 8
    return pl.pallas_call(
        mlp_kernel,
        out_shape=(
            S((rows, width), F32), S((4, rows, width), BF16), S((hid, width), BF16), S((8, part, hid), BF16), S((1, hid), F32),
        ),
        in_specs=[vm] * 5,
        out_specs=(vm,) * 5,
        scratch_shapes=[
            pltpu.VMEM((8, rows, width), BF16), pltpu.VMEM((8, rows, hid), BF16), pltpu.VMEM((8, rows, hid), BF16),
            pltpu.VMEM((2, 4, rows, width), BF16), pltpu.VMEM((2, 4, rows, width), BF16), pltpu.VMEM((4, rows, width), BF16),
            dma((8,)), dma((8,)), dma((2, 4)), dma((2, 4)), dma((4,)), dma((4,)),
            pltpu.VMEM((4, rows, width), BF16),
        ],
        compiler_params=pltpu.CompilerParams(collective_id=1, has_side_effects=True, vmem_limit_bytes=60 << 20),
    )(nb, gbb_all, wup, bup, wdn)

def along(step):
    return lax.rem(lax.axis_index("rep") + step, 4)


def remote_z(src, dst, send, recv, z):
    return pltpu.make_async_remote_copy(
        src_ref=src, dst_ref=dst, send_sem=send, recv_sem=recv, device_id={"rep": z}, device_id_type=MESH
    )


class LineSum:
    def __init__(self, chunks, held, halves, send, recv, lead):
        self.chunks, self.held, self.halves, self.send, self.recv = chunks, held, halves, send, recv
        rows = chunks.shape[1]
        self.parts = (pl.ds(0, lead), pl.ds(lead, rows - lead))
        self.sizes = (lead, rows - lead)

    def on(self, roles, action):
        z = lax.axis_index("rep")
        for role in roles:
            pl.when(z == role)(functools.partial(action, role))

    def enter(self, c, role):
        mate = (1, 0, 3, 2)[role]
        return remote_z(self.chunks.at[c], self.held.at[c], self.send.at[0, c], self.recv.at[0, c], mate)

    def give(self, c, role):
        half = 2 - role
        space = self.halves.at[c, pl.ds(0, self.sizes[half])]
        return remote_z(self.chunks.at[c, self.parts[half]], space, self.send.at[1, c], self.recv.at[1, c], 3 - role)

    def result(self, c, half, kind, target):
        ref = self.held.at[c, self.parts[half]]
        return remote_z(ref, ref, self.send.at[kind, c], self.recv.at[kind, c], target)

    def begin(self, c):
        self.on((0, 3), lambda role: self.enter(c, role).start())

    def first(self, c):
        def action(role):
            self.enter(c, role).wait_recv()
            self.chunks[c] = (self.chunks[c].astype(F32) + self.held[c].astype(F32)).astype(BF16)
            self.give(c, role).start()

        self.on((1, 2), action)

    def second(self, c):
        def action(role):
            mine = role - 1
            self.give(c, 3 - role).wait_recv()
            part, size = self.parts[mine], self.sizes[mine]
            self.held[c, part] = (self.chunks[c, part].astype(F32) + self.halves[c, :size].astype(F32)).astype(BF16)
            self.result(c, mine, 2, 3 - role).start()
            self.result(c, mine, 3, (1, 0, 3, 2)[role]).start()

        self.on((1, 2), action)

    def third(self, c):
        def action(role):
            other = 2 - role
            self.result(c, other, 2, 3 - role).wait_recv()
            self.result(c, other, 4, (1, 0, 3, 2)[role]).start()

        self.on((1, 2), action)

    def tick(self, n):
        count = self.chunks.shape[0]
        for step, c in ((self.first, n), (self.second, n - 1), (self.third, n - 2)):
            if 0 <= c < count:
                step(c)

    def end(self):
        def outer(role):
            near = 0 if role == 0 else 1
            for c in range(self.chunks.shape[0]):
                self.result(c, near, 3, 1).wait_recv()
                self.result(c, 1 - near, 4, 1).wait_recv()
                self.enter(c, role).wait_send()

        def inner(role):
            for c in range(self.chunks.shape[0]):
                self.give(c, role).wait_send()
                self.result(c, role - 1, 2, 3 - role).wait_send()
                self.result(c, role - 1, 3, 3 - role).wait_send()
                self.result(c, 2 - role, 4, 3 - role).wait_send()

        self.on((0, 3), outer)
        self.on((1, 2), inner)


class PlaneSum:
    def __init__(self, blocks, pair_in, cross_a, cross_b, from_x, from_y, pair_send, pair_recv, send, recv, lead):
        rows = blocks.shape[1]
        a, b = pl.ds(0, lead), pl.ds(lead, rows - lead)
        self.a, self.b = a, b
        self.blocks, self.pair_in = blocks, pair_in
        self.cross_a, self.cross_b, self.from_x, self.from_y = cross_a, cross_b, from_x, from_y
        self.pairs = [
            remote(blocks.at[flipped(2 * p + 1)], pair_in.at[p], pair_send.at[p], pair_recv.at[p], 1) for p in range(4)
        ]
        self.copies = [
            remote(blocks.at[flipped(6), a], cross_a, send.at[0], recv.at[0], 2),
            remote(blocks.at[flipped(6), b], cross_b, send.at[1], recv.at[1], 4),
            remote(blocks.at[flipped(4)], from_y, send.at[2], recv.at[2], 4),
            remote(blocks.at[flipped(2)], from_x, send.at[3], recv.at[3], 2),
        ]

    def pair(self):
        for p in (3, 2, 1, 0):
            self.pairs[p].start()

    def combine(self):
        for p in (3, 2, 1, 0):
            self.pairs[p].wait_recv()
            block = flipped(2 * p)
            self.blocks[block] = (self.blocks[block].astype(F32) + self.pair_in[p].astype(F32)).astype(BF16)
            if p == 3:
                self.copies[0].start()
                self.copies[1].start()

    def relay(self):
        y, x = flipped(4), flipped(2)
        self.copies[0].wait_recv()
        self.blocks[y, self.a] = (self.blocks[y, self.a].astype(F32) + self.cross_a[...].astype(F32)).astype(BF16)
        self.copies[2].start()
        self.copies[1].wait_recv()
        self.blocks[x, self.b] = (self.blocks[x, self.b].astype(F32) + self.cross_b[...].astype(F32)).astype(BF16)
        self.copies[3].start()

    def total(self):
        self.copies[2].wait_recv()
        self.copies[3].wait_recv()
        return self.blocks[flipped(0)].astype(F32) + self.from_x[...].astype(F32) + self.from_y[...].astype(F32)

    def drain(self):
        for copy in self.pairs + self.copies:
            copy.wait_send()


def norm_back(values, scale_part, grad):
    normal, rate = normalized(values)
    inner = grad * (1.0 + scale_part)
    back = rate * (
        inner - jnp.mean(inner, axis=-1, keepdims=True) - normal * jnp.mean(inner * normal, axis=-1, keepdims=True)
    )
    return back, grad * normal


def back_kernel(
    sizes_ref, tok_ref, cot_ref, mod_ref, na_ref, proj_ref, probs_ref, att_ref, mid_ref, gbup_ref, wo_all,
    pick_ref, bra_hbm, gnb_hbm, bbs_hbm, gdn_hbm, gup_hbm, wq_hbm, wada_hbm,
    out_ref, gin_ref, sums, mods, gc_in, picks, bias_ref, gbup_out,
    gup_in, bb_in, zbuf, zhalf, gm_ref, gba_ref, gatt_ref, gp_ref, blocks, pair_in, cross_a, cross_b, from_x, from_y,
    wq_buf, wada_ref, modrow, modz, bias_z, bias_in, gc_out,
    loc_sem, up_send, up_recv, bb_send, bb_recv, z_send, z_recv, ps_send, ps_recv, pc_send, pc_recv,
    md_send, md_recv, mz_send, mz_recv, pk_send, pk_recv, bz_send, bz_recv, bi_send, bi_recv, gc_send, gc_recv,
):
    rows, width = tok_ref.shape
    head_dim = width // H
    slots = sizes_ref.shape[0]
    part = width // 8
    hid = 8 * part // 2
    me, z = flipped(0), lax.axis_index("rep")
    core = lax.rem(me, 2)
    others, steps = range(1, 8), range(1, 4)

    line = LineSum(zbuf, sums, zhalf, z_send, z_recv, 80)
    planes = [
        PlaneSum(
            blocks.at[i], pair_in.at[i], cross_a.at[i], cross_b.at[i], from_x.at[i], from_y.at[i],
            ps_send.at[i], ps_recv.at[i], pc_send.at[i], pc_recv.at[i], 80,
        )
        for i in range(4)
    ]
    ups = [remote(gup_hbm.at[flipped(e)], gup_in.at[me], up_send.at[e], up_recv.at[e], e) for e in others]
    fars = [remote(bbs_hbm.at[p], bb_in.at[p], bb_send.at[p], bb_recv.at[p], 2 * p) for p in (1, 2, 3)]
    shift = (gdn_hbm.shape[0] - hid) * core
    local = [pltpu.make_async_copy(gdn_hbm.at[pl.ds(pl.multiple_of(shift + part * c, 16), part)], zbuf.at[c], loc_sem.at[c]) for c in range(4)]
    local.append(pltpu.make_async_copy(gup_hbm.at[me], gup_in.at[me], loc_sem.at[4]))
    local.append(pltpu.make_async_copy(bbs_hbm.at[0], bb_in.at[0], loc_sem.at[5]))
    local.append(pltpu.make_async_copy(wada_hbm, wada_ref, loc_sem.at[6]))
    loads = [pltpu.make_async_copy(wq_hbm.at[:, :, pl.ds(i * width, width)], wq_buf, loc_sem.at[7 + i]) for i in range(3)]
    local.append(pltpu.make_async_copy(bra_hbm, gm_ref, loc_sem.at[10]))
    local.append(pltpu.make_async_copy(gnb_hbm, gin_ref, loc_sem.at[11]))
    for copy in local + loads[:1]:
        copy.start()
    picks[z] = pick_ref[...]

    barrier = pltpu.get_barrier_semaphore()
    for e in others:
        pl.semaphore_signal(barrier, inc=1, device_id={"fsdp": flipped(e)}, device_id_type=MESH)
    for s in steps:
        pl.semaphore_signal(barrier, inc=1, device_id={"rep": along(s)}, device_id_type=MESH)
    pl.semaphore_wait(barrier, 10)

    for copy in ups:
        copy.start()
    for c in range(4):
        local[c].wait()
        line.begin(c)
    send_picks = [remote_z(picks.at[z], picks.at[z], pk_send.at[s], pk_recv.at[s], along(s)) for s in steps]
    for copy in send_picks:
        copy.start()

    image = image_of(lax.broadcasted_iota(jnp.int32, (rows, 1), 0), sizes_ref)
    selectors = [jnp.where(image == j, 1.0, 0.0) for j in range(slots)]
    slot = lax.broadcasted_iota(jnp.int32, (8, rows), 0) - slots * lax.rem(z, 2)
    where = image_of(lax.broadcasted_iota(jnp.int32, (8, rows), 1), sizes_ref)
    gather_rows = jnp.where((where == slot) & (slot < slots), 1.0, 0.0)

    def to_slots(index, values):
        modrow[:, index * width : (index + 1) * width] = lax.dot_general(
            gather_rows, values, (((1,), (0,)), ((), ())), precision=lax.Precision.HIGHEST, preferred_element_type=F32
        )

    cot = cot_ref[...].astype(F32)
    local[7].wait()
    local[8].wait()
    back, grad_scale = norm_back(mid_ref[...], per_row(selectors, mod_ref, 4, width), gin_ref[...])
    to_slots(3, gin_ref[...])
    to_slots(4, grad_scale)
    gm = cot + back
    to_slots(2, gm * gm_ref[...])
    gm_ref[...] = gm
    gba = (per_row(selectors, mod_ref, 2, width) * gm).astype(BF16)
    gba_ref[...] = gba
    bias_z[0] = jnp.zeros(bias_z.shape[1:], F32)
    bias_z[0, 2:3] = jnp.sum(gba.astype(F32), axis=0, keepdims=True)
    gbb = (per_row(selectors, mod_ref, 5, width) * cot).astype(BF16)
    bias_z[0, 3:4] = jnp.sum(gbb.astype(F32), axis=0, keepdims=True)
    bias_z[0, 4:5, : gbup_ref.shape[1]] = gbup_ref[...]
    gatt_ref[...] = nt(gba_ref[...], wo_all[...].reshape(width, width)).astype(BF16)
    blocks[0] = tn(att_ref[...], gba_ref[...]).astype(BF16).reshape(8, part, width)
    planes[0].pair()
    for copy in fars:
        copy.start()
    line.tick(0)
    planes[0].combine()

    gp_ref[...] = jnp.zeros_like(gp_ref)
    rate = head_dim ** (-0.5)

    def head_back(head):
        base, window, mask = head_window(head, head_dim)
        mask = mask.astype(BF16)
        at = [pl.ds(i * width + base, window) for i in range(3)]
        query, key, value = proj_ref[:, at[0]] * mask, proj_ref[:, at[1]] * mask, proj_ref[:, at[2]]
        grad = gatt_ref[:, at[0]] * mask
        low = probs_ref[head]
        probs = low.astype(F32)
        grad_probs = nt(grad, value)
        delta = jnp.sum(probs * grad_probs, axis=-1, keepdims=True)
        grad_scores = (probs * (grad_probs - delta)).astype(BF16)
        gp_ref[:, at[0]] += (nn(grad_scores, key) * rate).astype(BF16)
        gp_ref[:, at[1]] += (tn(grad_scores, query) * rate).astype(BF16)
        gp_ref[:, at[2]] += tn(low, grad).astype(BF16)

    for head in range(8):
        head_back(head)
    line.tick(1)
    planes[0].relay()
    for head in range(8, 16):
        head_back(head)
    local[4].wait()
    for copy in ups:
        copy.wait_recv()
    lap = gup_in.shape[2] - hid
    for c in range(4):
        left, right = gup_in[2 * c].astype(F32), gup_in[2 * c + 1].astype(F32)
        zbuf[4 + c, :, : hid - lap] = left[:, : hid - lap].astype(BF16)
        zbuf[4 + c, :, hid - lap : hid + lap] = (left[:, hid - lap :] + right[:, : 2 * lap]).astype(BF16)
        zbuf[4 + c, :, hid + lap :] = right[:, 2 * lap :].astype(BF16)
        line.begin(4 + c)
    line.tick(2)

    def spread(i):
        blocks[i] = tn(na_ref[...], gp_ref[:, (i - 1) * width : i * width]).astype(BF16).reshape(8, part, width)
        planes[i].pair()

    def settle(i):
        zbuf[8 + i] = planes[i].total().astype(BF16)
        line.begin(8 + i)

    spread(1)
    settle(0)
    spread(2)
    planes[1].combine()
    line.tick(3)
    spread(3)
    planes[2].combine()
    planes[1].relay()
    line.tick(4)
    for i in range(3):
        loads[i].wait()
        term = nt(gp_ref[:, i * width : (i + 1) * width], wq_buf[...].reshape(width, width))
        gin_ref[...] = term if i == 0 else gin_ref[...] + term
        if i < 2:
            loads[i + 1].start()
    gna = gin_ref[...]
    planes[3].combine()
    planes[2].relay()
    line.tick(5)
    for i, c in ((0, 0), (2, 1)):
        bias_z[0, c : c + 1] = jnp.sum(gp_ref[:, i * width : (i + 1) * width].astype(F32), axis=0, keepdims=True)
    send_bias = [remote_z(bias_z.at[0], bias_z.at[s], bz_send.at[s], bz_recv.at[s], along(s)) for s in steps]
    for copy in send_bias:
        copy.start()
    back, grad_scale = norm_back(tok_ref[...].astype(F32), per_row(selectors, mod_ref, 1, width), gna)
    to_slots(0, gna)
    to_slots(1, grad_scale)
    gin_ref[...] = gm_ref[...] + back
    settle(1)
    planes[3].relay()
    line.tick(6)
    local[5].wait()
    for copy in fars:
        copy.wait_recv()
    branch = bb_in[0].astype(F32) + bb_in[1].astype(F32) + bb_in[2].astype(F32) + bb_in[3].astype(F32)
    branch = branch + mod_ref[slots : slots + 1, 3 * width : 4 * width]
    out_ref[...] = (mid_ref[...] + per_row(selectors, mod_ref, 5, width) * branch).astype(BF16)
    to_slots(5, cot_ref[...].astype(F32) * branch)
    modz[z] = modrow[...].astype(BF16)
    send_mods = [remote_z(modz.at[z], modz.at[z], mz_send.at[s], mz_recv.at[s], along(s)) for s in steps]
    for copy in send_mods:
        copy.start()
    settle(2)
    line.tick(7)
    settle(3)
    for copy in send_mods + send_bias:
        copy.wait_recv()
    gather = Gather(mods, md_send, md_recv, 8)
    for pair in range(2):
        mods[me, 8 * pair : 8 * pair + 8] = (modz[2 * pair].astype(F32) + modz[2 * pair + 1].astype(F32)).astype(BF16)
    gather.own()
    total = bias_z[0] + bias_z[1] + bias_z[2] + bias_z[3]
    gbup_out[...] = total[4:5, : gbup_out.shape[1]]
    bias_in[me] = total
    send_total = [remote(bias_in.at[me], bias_in.at[me], bi_send.at[e], bi_recv.at[e], e) for e in others]
    for copy in send_total:
        copy.start()
    line.tick(8)
    gather.along_x()
    gather.along_y()
    line.tick(9)
    gather.across()
    line.tick(10)
    gather.finish()
    local[6].wait()
    gc_out[...] = nt(mods[...].reshape(128, mods.shape[2]), wada_ref[...]).reshape(gc_out.shape)
    send_gc = [remote(gc_out.at[flipped(e)], gc_in.at[me], gc_send.at[e], gc_recv.at[e], e) for e in others]
    for copy in send_gc:
        copy.start()
    gc_in[me] = gc_out[me]
    line.tick(11)
    for copy in send_total:
        copy.wait_recv()
    total = bias_in[0]
    for j in others:
        total = total + bias_in[j]
    bias_ref[...] = total
    line.tick(12)
    line.tick(13)
    for copy in send_gc + send_picks:
        copy.wait_recv()
    line.end()
    for copy in ups + fars + send_picks + send_bias + send_mods + send_total + send_gc:
        copy.wait_send()
    for plane in planes:
        plane.drain()
    gather.drain()


def backward(sizes, tok, cot, mod, na, proj, probs, att, bra, mid, gnb, gbup, wo, pick, bbs, gdn, gup, wq, wada):
    rows, width = tok.shape
    part, columns = wada.shape
    wide = gdn.shape[0]
    S = jax.ShapeDtypeStruct
    vm, hbm = pl.BlockSpec(memory_space=pltpu.VMEM), pl.BlockSpec(memory_space=pl.ANY)
    dma = pltpu.SemaphoreType.DMA
    shapes = (
        S((rows, width), BF16), S((rows, width), F32), S((12, part, width), BF16), S((8, 16, columns), BF16),
        S((8, 16, part), F32), S((4, 64, part), BF16), S((8, width), F32), S((1, wide), F32),
    )
    V = pltpu.VMEM
    return pl.pallas_call(
        back_kernel,
        out_shape=shapes,
        in_specs=[pl.BlockSpec(memory_space=pltpu.SMEM)] + [vm] * 11 + [hbm] * 7,
        out_specs=(vm,) * len(shapes),
        scratch_shapes=[
            V((8, part, wide), BF16), V((4, rows, width), BF16), V((12, part, width), BF16), V((12, 80, width), BF16),
            V((rows, width), F32), V((rows, width), BF16), V((rows, width), BF16), V((rows, 3 * width), BF16),
            V((4, 8, part, width), BF16), V((4, 4, part, width), BF16), V((4, 80, width), BF16), V((4, part - 80, width), BF16),
            V((4, part, width), BF16), V((4, part, width), BF16), V((8, part, width), BF16), V((part, columns), BF16),
            V((8, columns), F32), V((4, 8, columns), BF16), V((4, 8, width), F32), V((8, 8, width), F32), V((8, 16, part), F32),
            dma((12,)), dma((8,)), dma((8,)), dma((4,)), dma((4,)), dma((5, 12)), dma((5, 12)), dma((4, 4)), dma((4, 4)),
            dma((4, 4)), dma((4, 4)), dma((8,)), dma((8,)), dma((4,)), dma((4,)), dma((4,)), dma((4,)), dma((4,)), dma((4,)),
            dma((8,)), dma((8,)), dma((8,)), dma((8,)),
        ],
        compiler_params=pltpu.CompilerParams(collective_id=2, has_side_effects=True, vmem_limit_bytes=61 << 20),
    )(sizes, tok, cot, mod, na, proj, probs, att, mid, gbup, wo, pick, bra, gnb, bbs, gdn, gup, wq, wada)

def fast(tokens, cond, image_sizes, w_ada, b_ada, w_qkv, b_qkv, w_out, b_out, w_up, b_up, w_down, b_down, cotangent):
    rows, width = tokens.shape
    slots = image_sizes.shape[0]
    part, columns = w_ada.shape
    hid = w_down.shape[0]
    wide = hid + 64
    index, z = lax.axis_index("fsdp"), lax.axis_index("rep")
    shift = (wide - hid) * (index % 2)

    def placed(row, starts, pieces):
        for begin, piece in zip(starts, pieces):
            row = lax.dynamic_update_slice(row, piece.astype(F32)[None], (0, begin + index * piece.shape[0]))
        return row

    blank = jnp.zeros((1, columns), F32)
    bada = placed(blank, (0,), (b_ada,))
    others = placed(blank, (0, 2 * width, 3 * width), (b_qkv, b_out, b_down))
    cond_float = cond.astype(F32)
    cond_rows = jnp.pad(cond_float, ((0, 8 - slots), (0, 0)))
    wdn = lax.dynamic_update_slice(jnp.zeros((wide, width), BF16), w_down, (shift, 0))
    bup = lax.dynamic_update_slice(jnp.zeros((1, wide), F32), b_up.astype(F32)[None], (0, shift))
    mod, na, proj, probs, att, bra, mid, nb, gbb, wq, wo, wup, pick = start(
        image_sizes, tokens, cotangent, cond_rows, w_ada, bada, others, w_qkv, w_out, w_up, wide
    )
    gnb, bbs, gdn, gup, gbup = mlp(nb, gbb, wup.reshape(width, wide), bup, wdn)
    output, grad_input, sums, mods, gc, picks, bias, gbup = backward(
        image_sizes, tokens, cotangent, mod, na, proj, probs, att, bra, mid, gnb, gbup, wo, pick, bbs, gdn, gup, wq, w_ada
    )
    acts = picks.reshape(2, 2, 8, 8, part)[:, :, :, :slots].transpose(2, 0, 1, 3, 4).reshape(32 * slots, part)
    flat = mods.reshape(32 * slots, columns)
    g_ada = tn(acts, flat)
    n_ada, n_qkv = b_ada.shape[0], b_qkv.shape[0]
    g_bada = lax.dynamic_slice(jnp.sum(flat.astype(F32), axis=0), (index * n_ada,), (n_ada,))
    g_bqkv = lax.dynamic_slice(bias[:2].reshape(-1), (index * n_qkv,), (n_qkv,))
    g_bout = lax.dynamic_slice(bias[2], (index * part,), (part,))
    g_bdown = lax.dynamic_slice(bias[3], (index * part,), (part,))
    g_bup = lax.dynamic_slice(gbup[0], (shift,), (hid,))
    rows_mine = lax.dynamic_slice(gc, (0, 8 * (z // 2) + slots * (z % 2), 0), (8, slots, part))
    grad_activ = rows_mine.transpose(1, 0, 2).reshape(slots, width)
    _, silu_pull = jax.vjp(jax.nn.silu, cond_float)
    (grad_cond,) = silu_pull(grad_activ)
    wide_sums = sums.astype(F32)
    g_down = wide_sums[:4].reshape(hid, width)
    g_up = wide_sums[4:8].transpose(1, 0, 2).reshape(part, 4 * width)
    g_out = wide_sums[8]
    g_qkv = wide_sums[9:].transpose(1, 0, 2).reshape(part, 3 * width)
    return (output, grad_input, grad_cond, g_ada, g_bada, g_qkv, g_bqkv, g_out, g_bout, g_up, g_bup, g_down, g_bdown)


def solution(mesh):
    placed = (
        P(("fsdp", "rep"), None),
        P(("fsdp", "rep"), None),
        P(("fsdp", "rep")),
        P("fsdp", None),
        P("fsdp"),
        P("fsdp", None),
        P("fsdp"),
        P("fsdp", None),
        P("fsdp"),
        P("fsdp", None),
        P("fsdp"),
        P("fsdp", None),
        P("fsdp"),
        P(("fsdp", "rep"), None),
    )
    fits = mesh.shape["fsdp"] == 8 and mesh.shape["rep"] == 4
    return jax.shard_map(
        fast if fits else local,
        mesh=mesh,
        in_specs=placed,
        out_specs=(
            P(("fsdp", "rep"), None),
            P(("fsdp", "rep"), None),
            P(("fsdp", "rep"), None),
            P("fsdp", None),
            P("fsdp"),
            P("fsdp", None),
            P("fsdp"),
            P("fsdp", None),
            P("fsdp"),
            P("fsdp", None),
            P("fsdp"),
            P("fsdp", None),
            P("fsdp"),
        ),
        check_vma=False,
    )
```

```python
import functools

import jax
import jax.numpy as jnp
from jax import lax
from jax.experimental import pallas as pl
from jax.experimental.pallas import tpu as pltpu
from jax.sharding import PartitionSpec as P

H = 16
EPSILON = 1e-06
HIGHEST = lax.Precision.HIGHEST
MASKED = -1e30


def layer_norm(inputs):
    average = jnp.mean(inputs, axis=-1, keepdims=True)
    centered = inputs - average
    variance = jnp.mean(centered * centered, axis=-1, keepdims=True)
    return centered * lax.rsqrt(variance + EPSILON)


def modulate(hidden, shift_part, scale_part):
    return layer_norm(hidden) * (1.0 + scale_part) + shift_part


def gelu_tanh(inputs):
    return jax.nn.gelu(inputs, approximate=True)


def product(first_operand, second_operand):
    return jnp.dot(first_operand, second_operand, preferred_element_type=jnp.float32)


def product_back(first_operand, second_operand):
    return lax.dot_general(
        first_operand, second_operand, (((1,), (1,)), ((), ())), preferred_element_type=jnp.float32
    )


def outer_sum(first_operand, second_operand):
    return lax.dot_general(
        first_operand, second_operand, (((0,), (0,)), ((), ())), preferred_element_type=jnp.float32
    )


def fetch_forward(weight, bias_piece):
    return (
        lax.all_gather(weight, "fsdp", axis=0, tiled=True),
        lax.all_gather(bias_piece, "fsdp", axis=0, tiled=True),
    )


def weights_again(weight):
    return lax.all_gather(weight, "fsdp", axis=0, tiled=True)


def reduce_grads(weight_grad, bias_grad):
    row_part, bias_part = (
        lax.psum_scatter(weight_grad, "fsdp", scatter_dimension=0, tiled=True),
        lax.psum_scatter(bias_grad, "fsdp", scatter_dimension=0, tiled=True),
    )
    column_part = lax.psum_scatter(row_part, "rep", scatter_dimension=1, tiled=True)
    whole_rows, bias_stack = (
        lax.all_gather(column_part, "rep", axis=1, tiled=True),
        lax.all_gather(bias_part[None], "rep", axis=0, tiled=True),
    )
    return (whole_rows, jnp.sum(bias_stack, axis=0))


def local(
    tokens,
    cond,
    image_sizes,
    w_ada,
    b_ada,
    w_qkv,
    b_qkv,
    w_out,
    b_out,
    w_up,
    b_up,
    w_down,
    b_down,
    cotangent,
):
    row_count, model_width = tokens.shape
    head_count = H
    head_dim = model_width // head_count
    slot_count = image_sizes.shape[0]
    scale_factor = head_dim ** (-0.5)
    block_rows = min(512, row_count)
    block_count = row_count // block_rows
    image_ends = jnp.sum(
        jnp.where(jnp.arange(slot_count)[:, None] >= jnp.arange(slot_count)[None, :], image_sizes[None, :], 0), axis=1
    )
    positions = jnp.arange(row_count, dtype=jnp.int32)
    image_ids = jnp.sum((positions[:, None] >= image_ends[None, :]).astype(jnp.int32), axis=1)
    selector = (image_ids[:, None] == jnp.arange(slot_count, dtype=jnp.int32)[None, :]).astype(
        jnp.float32
    )
    cond_float = cond.astype(jnp.float32)
    activ_float, silu_pull = jax.vjp(jax.nn.silu, cond_float)
    activ_low = activ_float.astype(jnp.bfloat16)
    full_ada, full_bada = fetch_forward(w_ada, b_ada)
    modulation = product(activ_low, full_ada) + full_bada.astype(jnp.float32)
    per_token = jnp.dot(selector, modulation, precision=HIGHEST)
    shift_a, scale_a, gate_a, shift_b, scale_b, gate_b = jnp.split(per_token, 6, axis=1)
    hidden = tokens.astype(jnp.float32)
    normed_a, pull_a = jax.vjp(modulate, hidden, shift_a, scale_a)
    normed_a_low = normed_a.astype(jnp.bfloat16)
    full_qkv, full_bqkv = fetch_forward(w_qkv, b_qkv)
    bias_qkv = full_bqkv.astype(jnp.float32)
    bias_full = jnp.concatenate(
        [bias_qkv[:model_width], jnp.zeros((model_width,), jnp.float32), bias_qkv[model_width:]]
    )
    projected = (product(normed_a_low, full_qkv) + bias_full).astype(jnp.bfloat16)
    query_heads = projected[:, :model_width].reshape(row_count, head_count, head_dim)
    key_heads = projected[:, model_width : 2 * model_width].reshape(row_count, head_count, head_dim)
    value_heads = projected[:, 2 * model_width :].reshape(row_count, head_count, head_dim)
    query_blocks = query_heads.reshape(block_count, block_rows, head_count, head_dim)
    id_blocks = image_ids.reshape(block_count, block_rows)

    def scores_of(query_block, id_block):
        raw_scores = (
            jnp.einsum("qhd,khd->hqk", query_block, key_heads, preferred_element_type=jnp.float32)
            * scale_factor
        )
        same_image = id_block[:, None] == image_ids[None, :]
        return jnp.where(same_image[None], raw_scores, MASKED)

    def forward_block(block_item):
        query_block, id_block = block_item
        scores = scores_of(query_block, id_block)
        row_max = jnp.max(scores, axis=-1, keepdims=True)
        exponent = jnp.exp(scores - row_max)
        row_total = jnp.sum(exponent, axis=-1, keepdims=True)
        probabilities = (exponent / row_total).astype(jnp.bfloat16)
        attended_block = jnp.einsum(
            "hqk,khd->qhd", probabilities, value_heads, preferred_element_type=jnp.float32
        )
        return (attended_block.astype(jnp.bfloat16), (row_max + jnp.log(row_total))[:, :, 0])

    attended_blocks, lse_blocks = lax.map(forward_block, (query_blocks, id_blocks))
    attended = attended_blocks.reshape(row_count, model_width)
    full_out, full_bout = fetch_forward(w_out, b_out)
    branch_a = product(attended, full_out) + full_bout.astype(jnp.float32)
    middle = hidden + gate_a * branch_a
    normed_b, pull_b = jax.vjp(modulate, middle, shift_b, scale_b)
    normed_b_low = normed_b.astype(jnp.bfloat16)
    full_up, full_bup = fetch_forward(w_up, b_up)
    inner_pre = product(normed_b_low, full_up) + full_bup.astype(jnp.float32)
    activated, gelu_pull = jax.vjp(gelu_tanh, inner_pre)
    activated_low = activated.astype(jnp.bfloat16)
    full_down, full_bdown = fetch_forward(w_down, b_down)
    branch_b = product(activated_low, full_down) + full_bdown.astype(jnp.float32)
    output = (middle + gate_b * branch_b).astype(jnp.bfloat16)
    grad_out = cotangent.astype(jnp.float32)
    grad_gate_b = grad_out * branch_b
    grad_branch_b = (gate_b * grad_out).astype(jnp.bfloat16)
    grad_w_down, grad_b_down = reduce_grads(
        outer_sum(activated_low, grad_branch_b), jnp.sum(grad_branch_b.astype(jnp.float32), axis=0)
    )
    back_down = weights_again(w_down)
    grad_activated = product_back(grad_branch_b, back_down)
    (grad_inner,) = gelu_pull(grad_activated)
    grad_inner_low = grad_inner.astype(jnp.bfloat16)
    grad_w_up, grad_b_up = reduce_grads(
        outer_sum(normed_b_low, grad_inner_low), jnp.sum(grad_inner_low.astype(jnp.float32), axis=0)
    )
    back_up = weights_again(w_up)
    grad_normed_b = product_back(grad_inner_low, back_up)
    grad_middle_norm, grad_shift_b, grad_scale_b = pull_b(grad_normed_b)
    grad_middle = grad_out + grad_middle_norm
    grad_gate_a = grad_middle * branch_a
    grad_branch_a = (gate_a * grad_middle).astype(jnp.bfloat16)
    grad_w_out, grad_b_out = reduce_grads(
        outer_sum(attended, grad_branch_a), jnp.sum(grad_branch_a.astype(jnp.float32), axis=0)
    )
    back_out = weights_again(w_out)
    grad_attended = product_back(grad_branch_a, back_out).astype(jnp.bfloat16)
    grad_att_blocks = grad_attended.reshape(block_count, block_rows, head_count, head_dim)

    def backward_block(carried, block_item):
        key_grad, value_grad = carried
        query_block, id_block, grad_block, lse_block = block_item
        scores = scores_of(query_block, id_block)
        probabilities = jnp.exp(scores - lse_block[:, :, None])
        probabilities_low = probabilities.astype(jnp.bfloat16)
        grad_probs = jnp.einsum(
            "qhd,khd->hqk", grad_block, value_heads, preferred_element_type=jnp.float32
        )
        row_delta = jnp.sum(probabilities * grad_probs, axis=-1, keepdims=True)
        grad_scores = (probabilities * (grad_probs - row_delta)).astype(jnp.bfloat16)
        query_grad = (
            jnp.einsum("hqk,khd->qhd", grad_scores, key_heads, preferred_element_type=jnp.float32)
            * scale_factor
        )
        key_grad = (
            key_grad
            + jnp.einsum(
                "hqk,qhd->khd", grad_scores, query_block, preferred_element_type=jnp.float32
            )
            * scale_factor
        )
        value_grad = value_grad + jnp.einsum(
            "hqk,qhd->khd", probabilities_low, grad_block, preferred_element_type=jnp.float32
        )
        return ((key_grad, value_grad), query_grad)

    zero_heads = jnp.zeros((row_count, head_count, head_dim), jnp.float32)
    (grad_keys, grad_values), grad_query_blocks = lax.scan(
        backward_block,
        (zero_heads, zero_heads),
        (query_blocks, id_blocks, grad_att_blocks, lse_blocks),
    )
    grad_projected = jnp.concatenate(
        [
            grad_query_blocks.reshape(row_count, model_width),
            grad_keys.reshape(row_count, model_width),
            grad_values.reshape(row_count, model_width),
        ],
        axis=1,
    ).astype(jnp.bfloat16)
    column_sums = jnp.sum(grad_projected.astype(jnp.float32), axis=0)
    grad_bias_qkv = jnp.concatenate([column_sums[:model_width], column_sums[2 * model_width :]])
    grad_w_qkv, grad_b_qkv = reduce_grads(outer_sum(normed_a_low, grad_projected), grad_bias_qkv)
    back_qkv = weights_again(w_qkv)
    grad_normed_a = product_back(grad_projected, back_qkv)
    grad_hidden_norm, grad_shift_a, grad_scale_a = pull_a(grad_normed_a)
    grad_input = grad_middle + grad_hidden_norm
    grad_per_token = jnp.concatenate(
        [grad_shift_a, grad_scale_a, grad_gate_a, grad_shift_b, grad_scale_b, grad_gate_b], axis=1
    )
    grad_modulation = lax.dot_general(
        selector, grad_per_token, (((0,), (0,)), ((), ())), precision=HIGHEST
    ).astype(jnp.bfloat16)
    grad_w_ada, grad_b_ada = reduce_grads(
        outer_sum(activ_low, grad_modulation), jnp.sum(grad_modulation.astype(jnp.float32), axis=0)
    )
    back_ada = weights_again(w_ada)
    grad_activ = product_back(grad_modulation, back_ada)
    (grad_cond,) = silu_pull(grad_activ)
    return (
        output,
        grad_input,
        grad_cond,
        grad_w_ada,
        grad_b_ada,
        grad_w_qkv,
        grad_b_qkv,
        grad_w_out,
        grad_b_out,
        grad_w_up,
        grad_b_up,
        grad_w_down,
        grad_b_down,
    )


MESH = pl.DeviceIdType.MESH
F32, BF16 = jnp.float32, jnp.bfloat16


def flipped(offset):
    index = lax.axis_index("fsdp")
    y, x, core = index // 4, (index // 2) % 2, index % 2
    y = 1 - y if offset & 4 else y
    x = 1 - x if offset & 2 else x
    core = 1 - core if offset & 1 else core
    return y * 4 + x * 2 + core


def greet(offsets):
    barrier = pltpu.get_barrier_semaphore()
    for offset in offsets:
        pl.semaphore_signal(barrier, inc=1, device_id={"fsdp": flipped(offset)}, device_id_type=MESH)
    pl.semaphore_wait(barrier, len(offsets))


def remote(src, dst, send, recv, offset):
    return pltpu.make_async_remote_copy(
        src_ref=src, dst_ref=dst, send_sem=send, recv_sem=recv,
        device_id={"fsdp": flipped(offset)}, device_id_type=MESH,
    )


class Gather:
    def __init__(self, whole, send, recv, lead):
        rows = whole.shape[1]
        first, second = pl.ds(0, lead), pl.ds(lead, rows - lead)
        piece = {e: whole.at[flipped(e)] for e in (0, 2, 4, 6)}
        plan = (
            (piece[0], 1), (piece[0], 2), (piece[0], 4),
            (piece[2].at[first], 4), (piece[4].at[second], 2),
            (piece[2], 1), (piece[4], 1), (piece[6], 1),
        )
        self.copies = [remote(ref, ref, send.at[i], recv.at[i], e) for i, (ref, e) in enumerate(plan)]

    def own(self):
        for i in (1, 2, 0):
            self.copies[i].start()

    def along_x(self):
        self.copies[1].wait_recv()
        self.copies[3].start()
        self.copies[5].start()

    def along_y(self):
        self.copies[2].wait_recv()
        self.copies[4].start()
        self.copies[6].start()

    def across(self):
        self.copies[3].wait_recv()
        self.copies[4].wait_recv()
        self.copies[7].start()

    def finish(self, sends=True):
        for i in (0, 5, 6, 7):
            self.copies[i].wait_recv()

    def drain(self):
        for copy in self.copies:
            copy.wait_send()


def nt(a, b):
    return lax.dot_general(a, b, (((1,), (1,)), ((), ())), preferred_element_type=F32)


def tn(a, b):
    return lax.dot_general(a, b, (((0,), (0,)), ((), ())), preferred_element_type=F32)


def nn(a, b):
    return jnp.dot(a, b, preferred_element_type=F32)


def normalized(values):
    centered = values - jnp.mean(values, axis=-1, keepdims=True)
    variance = jnp.mean(centered * centered, axis=-1, keepdims=True)
    scale = lax.rsqrt(variance + EPSILON)
    return centered * scale, scale


def image_of(place, sizes_ref):
    end = jnp.int32(0)
    image = jnp.zeros(place.shape, jnp.int32)
    for j in range(sizes_ref.shape[0]):
        end = end + sizes_ref[j]
        image = image + (place >= end).astype(jnp.int32)
    return image


def per_row(selectors, modulation, part, width):
    total = None
    for j, chosen in enumerate(selectors):
        term = chosen * modulation[j : j + 1, part * width : (part + 1) * width]
        total = term if total is None else total + term
    return total


def head_window(head, head_dim):
    low = head * head_dim
    base = low // 128 * 128
    wide = 128 if low - base + head_dim <= 128 else 256
    lane = lax.broadcasted_iota(jnp.int32, (1, wide), 1) + (base - low)
    mask = jnp.where((lane >= 0) & (lane < head_dim), 1.0, 0.0)
    return base, wide, mask


def start_kernel(
    sizes_ref, tok_ref, cot_ref, cond_ref, wada_ref, bada_ref, bqkv_ref, bout_ref, bdown_ref, wqkv_ref, wout_ref, wup_ref,
    mod_ref, nb_ref, gbb_all, wup_all, pick_ref, na_hbm, proj_hbm, probs_hbm, att_hbm, bra_hbm, mid_hbm, wq_hbm, wo_hbm,
    na_ref, proj_ref, probs_ref, att_ref, bra_ref, mid_ref, wq_all, wo_all,
    act_all, pm, mpair, mfar, lay, lay_b,
    loc_sem, save_sem, act_send, act_recv, mp_send, mp_recv, mf_send, mf_recv, up_send, up_recv,
    q_send, q_recv, o_send, o_recv, g_send, g_recv,
):
    rows, width = tok_ref.shape
    head_dim = width // H
    slots = sizes_ref.shape[0]
    part = wada_ref.shape[0]
    wide = wup_all.shape[2]
    hid = (wup_ref.shape[1]) // 8
    me = flipped(0)
    others = range(1, 8)

    def up_piece(e):
        j = flipped(e)
        begin = pl.multiple_of(2 * hid * (j // 2) + (2 * hid - wide) * (j % 2), 128)
        return wup_ref.at[:, pl.ds(begin, wide)]

    local = [
        pltpu.make_async_copy(wqkv_ref, wq_all.at[me], loc_sem.at[0]),
        pltpu.make_async_copy(wout_ref, wo_all.at[me], loc_sem.at[1]),
        pltpu.make_async_copy(up_piece(0), wup_all.at[me], loc_sem.at[2]),
    ]
    for copy in local:
        copy.start()
    act = jax.nn.silu(cond_ref[...].astype(F32))
    act_all[me, :slots] = act
    act_all[me, slots:] = act
    saves = [
        pltpu.make_async_copy(src, dst, save_sem.at[i])
        for i, (src, dst) in enumerate((
            (na_ref, na_hbm), (proj_ref, proj_hbm), (probs_ref, probs_hbm), (att_ref, att_hbm),
            (bra_ref, bra_hbm), (mid_ref, mid_hbm), (wq_all, wq_hbm), (wo_all, wo_hbm),
        ))
    ]
    qkv, out, gbb = (
        Gather(wq_all, q_send, q_recv, 80), Gather(wo_all, o_send, o_recv, 80), Gather(gbb_all, g_send, g_recv, rows // 2)
    )
    acts = [remote(act_all.at[me], act_all.at[me], act_send.at[e], act_recv.at[e], e) for e in others]
    ups = [remote(up_piece(e), wup_all.at[me], up_send.at[e], up_recv.at[e], e) for e in others]
    pairs = [remote(pm.at[flipped(2 * p + 1)], mpair.at[p], mp_send.at[p], mp_recv.at[p], 1) for p in range(4)]
    fars = [remote(pm.at[flipped(2 * p)], mfar.at[p], mf_send.at[p], mf_recv.at[p], 2 * p) for p in range(1, 4)]

    greet(others)
    for copy in acts:
        copy.start()
    local[0].wait()
    qkv.own()
    lay[...] = jnp.zeros_like(lay)
    lay_b[...] = jnp.zeros_like(lay_b)
    lay[0:1, : bada_ref.shape[1]] = bada_ref[...].astype(F32)
    bada = pltpu.roll(lay[...], me * bada_ref.shape[1], 1)[0:1]
    begin = 0
    for ref in (bqkv_ref, bout_ref, bdown_ref):
        size = ref.shape[1]
        lay_b[0:1, begin : begin + size] = ref[...].astype(F32)
        lay_b[0:1, begin : begin + 8 * size] = pltpu.roll(lay_b[:, begin : begin + 8 * size], me * size, 1)[0:1]
        begin += 8 * size
    for copy in acts:
        copy.wait_recv()
    everyone = act_all[...].reshape(8 * act_all.shape[1], width).astype(BF16)
    pick = (
        lax.broadcasted_iota(jnp.int32, (width, part), 0) == lax.broadcasted_iota(jnp.int32, (width, part), 1) + me * part
    )
    chosen = nn(everyone, jnp.where(pick, 1.0, 0.0).astype(BF16)).astype(BF16)
    pick_ref[...] = chosen
    bias_row = lax.broadcasted_iota(jnp.int32, (8, 1), 0) == slots
    piece = nn(chosen, wada_ref[...]).reshape(pm.shape)
    pm[...] = piece + bada[None]
    pm[:, :, : lay_b.shape[1]] = jnp.where(bias_row[None], lay_b[0:1][None], pm[:, :, : lay_b.shape[1]])
    for copy in pairs:
        copy.start()
    for p in range(4):
        pairs[p].wait_recv()
        pm[flipped(2 * p)] += mpair[p]
        if p:
            fars[p - 1].start()
    qkv.along_x()
    qkv.along_y()
    local[1].wait()
    out.own()
    for copy in fars:
        copy.wait_recv()
    modulation = pm[me] + (mfar[1] + mfar[2] + mfar[3])
    mod_ref[...] = modulation
    bias = modulation[slots : slots + 1]
    image = image_of(lax.broadcasted_iota(jnp.int32, (rows, 1), 0), sizes_ref)
    selectors = [jnp.where(image == j, 1.0, 0.0) for j in range(slots)]
    gate_b = per_row(selectors, mod_ref, 5, width)
    gbb_all[me] = (gate_b * cot_ref[...].astype(F32)).astype(BF16)
    hidden = tok_ref[...].astype(F32)
    na_ref[...] = (
        normalized(hidden)[0] * (1.0 + per_row(selectors, mod_ref, 1, width)) + per_row(selectors, mod_ref, 0, width)
    ).astype(BF16)
    saves[0].start()
    qkv.across()
    gbb.own()
    for copy in ups:
        copy.start()
    qkv.finish()
    for i in range(3):
        block = wq_all[:, :, i * width : (i + 1) * width].reshape(width, width)
        value = nn(na_ref[...], block)
        if i == 0:
            value = value + bias[:, :width]
        if i == 2:
            value = value + bias[:, width : 2 * width]
        proj_ref[:, i * width : (i + 1) * width] = value.astype(BF16)
    saves[1].start()
    saves[6].start()
    out.along_x()
    out.along_y()
    att_ref[...] = jnp.zeros_like(att_ref)
    row_image = image_of(lax.broadcasted_iota(jnp.int32, (rows, rows), 0), sizes_ref)
    column_image = image_of(lax.broadcasted_iota(jnp.int32, (rows, rows), 1), sizes_ref)
    hidden_pairs = jnp.where(row_image == column_image, 0.0, -1e30)
    for head in range(H):
        base, window, mask = head_window(head, head_dim)
        mask = mask.astype(BF16)
        query = proj_ref[:, base : base + window] * mask
        key = proj_ref[:, width + base : width + base + window]
        value = proj_ref[:, 2 * width + base : 2 * width + base + window] * mask
        scores = nt(query, key) * head_dim ** (-0.5) + hidden_pairs
        exponent = jnp.exp(scores - jnp.max(scores, axis=-1, keepdims=True))
        probs = (exponent * (1.0 / jnp.sum(exponent, axis=-1, keepdims=True))).astype(BF16)
        probs_ref[head] = probs
        att_ref[:, base : base + window] += nn(probs, value).astype(BF16)
        if head == 3:
            out.across()
        if head == 7:
            gbb.along_x()
            gbb.along_y()
    saves[2].start()
    saves[3].start()
    out.finish()
    saves[7].start()
    branch = nn(att_ref[...], wo_all[...].reshape(width, width)) + bias[:, 2 * width : 3 * width]
    bra_ref[...] = branch
    middle = tok_ref[...].astype(F32) + per_row(selectors, mod_ref, 2, width) * branch
    mid_ref[...] = middle
    nb_ref[...] = (
        normalized(middle)[0] * (1.0 + per_row(selectors, mod_ref, 4, width)) + per_row(selectors, mod_ref, 3, width)
    ).astype(BF16)
    saves[4].start()
    saves[5].start()
    gbb.across()
    gbb.finish()
    local[2].wait()
    for copy in ups:
        copy.wait()
    for copy in acts + pairs + fars:
        copy.wait_send()
    for gather in (qkv, out, gbb):
        gather.drain()
    for copy in saves:
        copy.wait()


def start(sizes, tok, cot, cond, wada, bada, bqkv, bout, bdown, wqkv, wout, wup, wide):
    rows, width = tok.shape
    part = wada.shape[0]
    columns = wada.shape[1]
    S, V = jax.ShapeDtypeStruct, pltpu.VMEM
    vm, hbm = pl.BlockSpec(memory_space=pltpu.VMEM), pl.BlockSpec(memory_space=pl.ANY)
    dma = pltpu.SemaphoreType.DMA
    kept = (
        ((rows, width), BF16), ((rows, 3 * width), BF16), ((H, rows, rows), BF16), ((rows, width), BF16),
        ((rows, width), F32), ((rows, width), F32), ((8, part, 3 * width), BF16), ((8, part, width), BF16),
    )
    shapes = (
        S((8, columns), F32), S((rows, width), BF16), S((8, rows, width), BF16), S((8, part, wide), BF16), S((64, part), BF16),
    ) + tuple(S(*pair) for pair in kept)
    return pl.pallas_call(
        start_kernel,
        out_shape=shapes,
        in_specs=[pl.BlockSpec(memory_space=pltpu.SMEM)] + [vm] * 8 + [hbm] * 3,
        out_specs=(vm,) * 5 + (hbm,) * 8,
        scratch_shapes=[V(*pair) for pair in kept] + [
            V((8, 8, width), F32), V((8, 8, columns), F32), V((4, 8, columns), F32),
            V((4, 8, columns), F32), V((8, columns), F32), V((8, 4 * width), F32),
            dma((3,)), dma((8,)), dma((8,)), dma((8,)), dma((4,)), dma((4,)), dma((4,)), dma((4,)), dma((8,)), dma((8,)),
        ] + [dma((8,))] * 6,
        compiler_params=pltpu.CompilerParams(collective_id=0, has_side_effects=True, vmem_limit_bytes=60 << 20),
    )(sizes, tok, cot, cond, wada, bada, bqkv, bout, bdown, wqkv, wout, wup)

GELU_RATE = 0.7978845608028654
GELU_CUBE = 0.044715


def gelu_parts(u):
    square = u * u
    bend = jnp.tanh(GELU_RATE * u * (1.0 + GELU_CUBE * square))
    half = 0.5 * (1.0 + bend)
    slope = half + 0.5 * u * (1.0 - bend * bend) * (GELU_RATE * (1.0 + 3.0 * GELU_CUBE * square))
    return u * half, slope


def mlp_kernel(
    nb_ref, bup_in, gbb_hbm, wup_hbm, wdn_hbm,
    gnb_ref, gbup_ref, bb_hbm, gdn_hbm, gup_hbm,
    nb_all, act_all, gi_all, out_pair, in_pair, in_far, gnb_mine, gbb_all, wup_ref, wdn_ref, bb_ref, gdn_ref, gup_ref, bup_ref,
    n_send, n_recv, pr_send, pr_recv, far_send, far_recv, loc_sem,
):
    rows, width = nb_ref.shape
    hid = wdn_ref.shape[0]
    me = flipped(0)
    own = wdn_hbm.shape[0]
    shift = lax.rem(me, 2) * (hid - own)
    blank = lax.rem(me + 1, 2) * own
    loads = [
        pltpu.make_async_copy(src, dst, loc_sem.at[i])
        for i, (src, dst) in enumerate((
            (wup_hbm, wup_ref), (gbb_hbm, gbb_all), (wdn_hbm, wdn_ref.at[pl.ds(pl.multiple_of(shift, 64), own)]),
            (bb_ref, bb_hbm), (gdn_ref, gdn_hbm), (gup_ref, gup_hbm),
        ))
    ]
    for copy in loads[:3]:
        copy.start()
    wdn_ref[pl.ds(pl.multiple_of(blank, 64), hid - own)] = jnp.zeros((hid - own, width), BF16)
    bup_ref[...] = jnp.zeros_like(bup_ref)
    bup_ref[0:1, :own] = bup_in[...].astype(F32)
    bup = pltpu.roll(bup_ref[...], shift, 1)[0:1]
    nb = Gather(nb_all, n_send, n_recv, rows // 2)
    pairs = [[remote(out_pair.at[a, p], in_pair.at[a, p], pr_send.at[a, p], pr_recv.at[a, p], 1) for p in range(4)] for a in (0, 1)]
    mine = (gnb_mine, bb_ref)
    fars = [remote(gnb_mine.at[p], in_far.at[p], far_send.at[p], far_recv.at[p], 2 * p) for p in (1, 2, 3)]
    nb_all[me] = nb_ref[...]
    greet((1, 2, 4, 6))
    nb.own()
    for copy in loads[:3]:
        copy.wait()

    def one(slot):
        inner = nn(nb_all[slot], wup_ref[...]) + bup
        act, slope = gelu_parts(inner)
        act_all[slot] = act.astype(BF16)
        gi_all[slot] = (slope * nt(gbb_all[slot], wdn_ref[...])).astype(BF16)

    def back(slot):
        return nt(gi_all[slot], wup_ref[...]).astype(BF16)

    def forth(slot):
        return nn(act_all[slot], wdn_ref[...]).astype(BF16)

    def combine(a, p):
        pairs[a][p].wait_recv()
        mine[a][p] = (mine[a][p].astype(F32) + in_pair[a, p].astype(F32)).astype(BF16)

    waits = {1: 0, 3: 5, 5: 6, 7: 7}
    for p in range(4):
        even, odd = flipped(2 * p), flipped(2 * p + 1)
        if p == 1:
            nb.along_x()
        if p == 2:
            nb.along_y()
        if p == 3:
            nb.across()
        one(even)
        gnb_mine[p] = back(even)
        nb.copies[waits[2 * p + 1]].wait_recv()
        one(odd)
        out_pair[0, p] = back(odd)
        pairs[0][p].start()
        bb_ref[p] = forth(even)
        out_pair[1, p] = forth(odd)
        pairs[1][p].start()
        combine(0, p)
        if p:
            fars[p - 1].start()
    gdn_ref[...] = tn(act_all[...].reshape(8 * rows, hid), gbb_all[...].reshape(8 * rows, width)).astype(BF16)
    loads[4].start()
    inner_grads = gi_all[...].reshape(8 * rows, hid)
    gup_ref[...] = tn(nb_all[...].reshape(8 * rows, width), inner_grads).astype(BF16).reshape(gup_ref.shape)
    loads[5].start()
    gbup_ref[...] = jnp.sum(inner_grads.astype(F32), axis=0, keepdims=True)
    for p in range(4):
        combine(1, p)
    loads[3].start()
    total = gnb_mine[0].astype(F32)
    for p in (1, 2, 3):
        fars[p - 1].wait()
        total = total + in_far[p].astype(F32)
    gnb_ref[...] = total
    for a in (0, 1):
        for p in range(4):
            pairs[a][p].wait_send()
    nb.drain()
    for copy in loads[3:]:
        copy.wait()


def mlp(nb, bup, gbb_all, wup, wdn):
    rows, width = nb.shape
    hid = wup.shape[1]
    part = width // 8
    S, V = jax.ShapeDtypeStruct, pltpu.VMEM
    vm, hbm = pl.BlockSpec(memory_space=pltpu.VMEM), pl.BlockSpec(memory_space=pl.ANY)
    dma = pltpu.SemaphoreType.DMA
    kept = (((4, rows, width), BF16), ((hid, width), BF16), ((8, part, hid), BF16))
    return pl.pallas_call(
        mlp_kernel,
        out_shape=(S((rows, width), F32), S((1, hid), F32)) + tuple(S(*pair) for pair in kept),
        in_specs=[vm] * 2 + [hbm] * 3,
        out_specs=(vm,) * 2 + (hbm,) * 3,
        scratch_shapes=[
            V((8, rows, width), BF16), V((8, rows, hid), BF16), V((8, rows, hid), BF16),
            V((2, 4, rows, width), BF16), V((2, 4, rows, width), BF16), V((4, rows, width), BF16), V((4, rows, width), BF16),
            V((8, rows, width), BF16), V((width, hid), BF16), V((hid, width), BF16),
        ] + [V(*pair) for pair in kept] + [
            V((8, hid), F32),
            dma((8,)), dma((8,)), dma((2, 4)), dma((2, 4)), dma((4,)), dma((4,)), dma((6,)),
        ],
        compiler_params=pltpu.CompilerParams(collective_id=1, has_side_effects=True, vmem_limit_bytes=60 << 20),
    )(nb, bup, gbb_all, wup, wdn)

def along(step):
    return lax.rem(lax.axis_index("rep") + step, 4)


def remote_z(src, dst, send, recv, z):
    return pltpu.make_async_remote_copy(
        src_ref=src, dst_ref=dst, send_sem=send, recv_sem=recv, device_id={"rep": z}, device_id_type=MESH
    )


class LineSum:
    def __init__(self, chunks, held, halves, send, recv, lead):
        self.chunks, self.held, self.halves, self.send, self.recv = chunks, held, halves, send, recv
        rows = chunks.shape[1]
        self.parts = (pl.ds(0, lead), pl.ds(lead, rows - lead))
        self.sizes = (lead, rows - lead)

    def on(self, roles, action):
        z = lax.axis_index("rep")
        for role in roles:
            pl.when(z == role)(functools.partial(action, role))

    def enter(self, c, role):
        mate = (1, 0, 3, 2)[role]
        return remote_z(self.chunks.at[c], self.held.at[c], self.send.at[0, c], self.recv.at[0, c], mate)

    def give(self, c, role):
        half = 2 - role
        space = self.halves.at[c, pl.ds(0, self.sizes[half])]
        return remote_z(self.chunks.at[c, self.parts[half]], space, self.send.at[1, c], self.recv.at[1, c], 3 - role)

    def result(self, c, half, kind, target):
        ref = self.held.at[c, self.parts[half]]
        return remote_z(ref, ref, self.send.at[kind, c], self.recv.at[kind, c], target)

    def begin(self, c):
        def action(role):
            if c >= 2:
                self.enter(c - 2, role).wait_send()
            self.enter(c, role).start()

        self.on((0, 3), action)

    def first(self, c):
        def action(role):
            self.enter(c, role).wait_recv()
            self.chunks[c] = (self.chunks[c].astype(F32) + self.held[c].astype(F32)).astype(BF16)
            self.give(c, role).start()

        self.on((1, 2), action)

    def second(self, c):
        def action(role):
            mine = role - 1
            self.give(c, 3 - role).wait_recv()
            part, size = self.parts[mine], self.sizes[mine]
            self.held[c, part] = (self.chunks[c, part].astype(F32) + self.halves[c, :size].astype(F32)).astype(BF16)
            self.result(c, mine, 2, 3 - role).start()
            self.result(c, mine, 3, (1, 0, 3, 2)[role]).start()

        self.on((1, 2), action)

    def third(self, c):
        def action(role):
            other = 2 - role
            self.result(c, other, 2, 3 - role).wait_recv()
            self.result(c, other, 4, (1, 0, 3, 2)[role]).start()

        self.on((1, 2), action)

    def tick(self, n):
        count = self.chunks.shape[0]
        for step, c in ((self.begin, n + 2), (self.first, n), (self.second, n - 1), (self.third, n - 2)):
            if 0 <= c < count:
                step(c)

    def end(self):
        def outer(role):
            near = 0 if role == 0 else 1
            for c in range(self.chunks.shape[0]):
                self.result(c, near, 3, 1).wait_recv()
                self.result(c, 1 - near, 4, 1).wait_recv()
                if c >= self.chunks.shape[0] - 2:
                    self.enter(c, role).wait_send()

        def inner(role):
            for c in range(self.chunks.shape[0]):
                self.give(c, role).wait_send()
                self.result(c, role - 1, 2, 3 - role).wait_send()
                self.result(c, role - 1, 3, 3 - role).wait_send()
                self.result(c, 2 - role, 4, 3 - role).wait_send()

        self.on((0, 3), outer)
        self.on((1, 2), inner)


class PlaneSum:
    def __init__(self, blocks, pair_in, cross_a, cross_b, from_x, from_y, pair_send, pair_recv, send, recv, lead):
        rows = blocks.shape[1]
        a, b = pl.ds(0, lead), pl.ds(lead, rows - lead)
        self.a, self.b = a, b
        self.blocks, self.pair_in = blocks, pair_in
        self.cross_a, self.cross_b, self.from_x, self.from_y = cross_a, cross_b, from_x, from_y
        self.pairs = [
            remote(blocks.at[flipped(2 * p + 1)], pair_in.at[p], pair_send.at[p], pair_recv.at[p], 1) for p in range(4)
        ]
        self.copies = [
            remote(blocks.at[flipped(6), a], cross_a, send.at[0], recv.at[0], 2),
            remote(blocks.at[flipped(6), b], cross_b, send.at[1], recv.at[1], 4),
            remote(blocks.at[flipped(4)], from_y, send.at[2], recv.at[2], 4),
            remote(blocks.at[flipped(2)], from_x, send.at[3], recv.at[3], 2),
        ]

    def pair(self):
        for p in (3, 2, 1, 0):
            self.pairs[p].start()

    def combine(self):
        for p in (3, 2, 1, 0):
            self.pairs[p].wait_recv()
            block = flipped(2 * p)
            self.blocks[block] = (self.blocks[block].astype(F32) + self.pair_in[p].astype(F32)).astype(BF16)
            if p == 3:
                self.copies[0].start()
                self.copies[1].start()

    def relay(self):
        y, x = flipped(4), flipped(2)
        self.copies[0].wait_recv()
        self.blocks[y, self.a] = (self.blocks[y, self.a].astype(F32) + self.cross_a[...].astype(F32)).astype(BF16)
        self.copies[2].start()
        self.copies[1].wait_recv()
        self.blocks[x, self.b] = (self.blocks[x, self.b].astype(F32) + self.cross_b[...].astype(F32)).astype(BF16)
        self.copies[3].start()

    def total(self):
        self.copies[2].wait_recv()
        self.copies[3].wait_recv()
        return self.blocks[flipped(0)].astype(F32) + self.from_x[...].astype(F32) + self.from_y[...].astype(F32)

    def drain(self):
        for copy in self.pairs + self.copies:
            copy.wait_send()


def norm_back(values, scale_part, grad):
    normal, rate = normalized(values)
    inner = grad * (1.0 + scale_part)
    back = rate * (
        inner - jnp.mean(inner, axis=-1, keepdims=True) - normal * jnp.mean(inner * normal, axis=-1, keepdims=True)
    )
    return back, grad * normal


def back_kernel(
    sizes_ref, tok_ref, cot_ref, mod_ref, mid_ref, gbup_ref, pick_ref, na_hbm, proj_hbm, probs_hbm, att_hbm, wo_hbm,
    bra_hbm, gnb_hbm, bbs_hbm, gdn_hbm, gup_hbm, wq_hbm, wada_hbm,
    out_ref, gin_ref, sums, mods, gc_in, picks, bias_ref, gbup_out,
    na_ref, proj_ref, probs_ref, att_ref, wo_all,
    gup_in, bb_in, zbuf, zhalf, gm_ref, gba_ref, gatt_ref, gp_ref, blocks, pair_in, cross_a, cross_b, from_x, from_y,
    wq_buf, wada_ref, modrow, bias_z, bias_in, gc_out,
    loc_sem, up_send, up_recv, bb_send, bb_recv, z_send, z_recv, ps_send, ps_recv, pc_send, pc_recv,
    md_send, md_recv, mz_send, mz_recv, pk_send, pk_recv, bz_send, bz_recv, bi_send, bi_recv, gc_send, gc_recv,
):
    rows, width = tok_ref.shape
    head_dim = width // H
    slots = sizes_ref.shape[0]
    part = width // 8
    hid = 8 * part // 2
    me, z = flipped(0), lax.axis_index("rep")
    core = lax.rem(me, 2)
    others, steps = range(1, 8), range(1, 4)

    line = LineSum(zbuf, sums, zhalf, z_send, z_recv, 80)
    planes = [
        PlaneSum(
            blocks.at[i], pair_in.at[i], cross_a.at[i], cross_b.at[i], from_x.at[i], from_y.at[i],
            ps_send.at[i], ps_recv.at[i], pc_send.at[i], pc_recv.at[i], 80,
        )
        for i in range(4)
    ]
    ups = [remote(gup_hbm.at[flipped(e)], gup_in.at[me], up_send.at[e], up_recv.at[e], e) for e in others]
    fars = [remote(bbs_hbm.at[p], bb_in.at[p], bb_send.at[p], bb_recv.at[p], 2 * p) for p in (1, 2, 3)]
    shift = (gdn_hbm.shape[0] - hid) * core
    local = [pltpu.make_async_copy(gdn_hbm.at[pl.ds(pl.multiple_of(shift + part * c, 16), part)], zbuf.at[c], loc_sem.at[c]) for c in range(4)]
    local.append(pltpu.make_async_copy(gup_hbm.at[me], gup_in.at[me], loc_sem.at[4]))
    local.append(pltpu.make_async_copy(bbs_hbm.at[0], bb_in.at[0], loc_sem.at[5]))
    local.append(pltpu.make_async_copy(wada_hbm, wada_ref, loc_sem.at[6]))
    loads = [pltpu.make_async_copy(wq_hbm.at[:, :, pl.ds(i * width, width)], wq_buf, loc_sem.at[7 + i]) for i in range(3)]
    local.append(pltpu.make_async_copy(bra_hbm, gm_ref, loc_sem.at[10]))
    local.append(pltpu.make_async_copy(gnb_hbm, gin_ref, loc_sem.at[11]))
    local += [
        pltpu.make_async_copy(src, dst, loc_sem.at[12 + i])
        for i, (src, dst) in enumerate((
            (wo_hbm, wo_all), (att_hbm, att_ref), (proj_hbm, proj_ref), (probs_hbm, probs_ref), (na_hbm, na_ref),
        ))
    ]
    for i in (7, 8, 0, 1, 9, 10, 2, 3, 11, 12, 4, 5, 13, 6):
        local[i].start()
    loads[0].start()
    picks[z] = pick_ref[...]

    barrier = pltpu.get_barrier_semaphore()
    for e in others:
        pl.semaphore_signal(barrier, inc=1, device_id={"fsdp": flipped(e)}, device_id_type=MESH)
    for s in steps:
        pl.semaphore_signal(barrier, inc=1, device_id={"rep": along(s)}, device_id_type=MESH)
    pl.semaphore_wait(barrier, 10)

    for copy in ups:
        copy.start()
    for c in range(4):
        local[c].wait()
    line.begin(0)
    line.begin(1)
    send_picks = [remote_z(picks.at[z], picks.at[z], pk_send.at[s], pk_recv.at[s], along(s)) for s in steps]
    for copy in send_picks:
        copy.start()

    image = image_of(lax.broadcasted_iota(jnp.int32, (rows, 1), 0), sizes_ref)
    selectors = [jnp.where(image == j, 1.0, 0.0) for j in range(slots)]
    slot = lax.broadcasted_iota(jnp.int32, (8, rows), 0)
    where = image_of(lax.broadcasted_iota(jnp.int32, (8, rows), 1), sizes_ref)
    gather_rows = (jnp.where((where == slot) & (slot < slots), 1.0, 0.0), jnp.where((where == slot - slots) & (where < slots), 1.0, 0.0))
    modrow[...] = jnp.zeros_like(modrow)

    def to_slots(index, values):
        modrow[:, (index % 3) * width : (index % 3 + 1) * width] += lax.dot_general(
            gather_rows[index // 3], values, (((1,), (0,)), ((), ())), precision=lax.Precision.HIGHEST, preferred_element_type=F32
        )

    cot = cot_ref[...].astype(F32)
    local[7].wait()
    local[8].wait()
    back, grad_scale = norm_back(mid_ref[...], per_row(selectors, mod_ref, 4, width), gin_ref[...])
    to_slots(3, gin_ref[...])
    to_slots(4, grad_scale)
    gm = cot + back
    to_slots(2, gm * gm_ref[...])
    gm_ref[...] = gm
    gba = (per_row(selectors, mod_ref, 2, width) * gm).astype(BF16)
    gba_ref[...] = gba
    bias_z[0] = jnp.zeros(bias_z.shape[1:], F32)
    bias_z[0, 2:3] = jnp.sum(gba.astype(F32), axis=0, keepdims=True)
    gbb = (per_row(selectors, mod_ref, 5, width) * cot).astype(BF16)
    bias_z[0, 3:4] = jnp.sum(gbb.astype(F32), axis=0, keepdims=True)
    bias_z[0, 4:5, : gbup_ref.shape[1]] = gbup_ref[...]
    local[9].wait()
    gatt_ref[...] = nt(gba_ref[...], wo_all[...].reshape(width, width)).astype(BF16)
    local[10].wait()
    blocks[0] = tn(att_ref[...], gba_ref[...]).astype(BF16).reshape(8, part, width)
    planes[0].pair()
    line.tick(0)

    gp_ref[...] = jnp.zeros_like(gp_ref)
    rate = head_dim ** (-0.5)

    def head_back(head):
        base, window, mask = head_window(head, head_dim)
        mask = mask.astype(BF16)
        at = [pl.ds(i * width + base, window) for i in range(3)]
        query, key, value = proj_ref[:, at[0]] * mask, proj_ref[:, at[1]] * mask, proj_ref[:, at[2]]
        grad = gatt_ref[:, at[0]] * mask
        low = probs_ref[head]
        probs = low.astype(F32)
        grad_probs = nt(grad, value)
        delta = jnp.sum(probs * grad_probs, axis=-1, keepdims=True)
        grad_scores = (probs * (grad_probs - delta)).astype(BF16)
        gp_ref[:, at[0]] += (nn(grad_scores, key) * rate).astype(BF16)
        gp_ref[:, at[1]] += (tn(grad_scores, query) * rate).astype(BF16)
        gp_ref[:, at[2]] += tn(low, grad).astype(BF16)

    local[11].wait()
    local[12].wait()
    for head in range(3):
        head_back(head)
    planes[0].combine()
    fars[0].start()
    fars[1].start()
    for head in range(3, 10):
        head_back(head)
    line.tick(1)
    for head in range(10, 16):
        head_back(head)
    local[4].wait()
    for copy in ups:
        copy.wait_recv()
    lap = gup_in.shape[2] - hid
    for c in range(4):
        left, right = gup_in[2 * c].astype(F32), gup_in[2 * c + 1].astype(F32)
        zbuf[4 + c, :, : hid - lap] = left[:, : hid - lap].astype(BF16)
        zbuf[4 + c, :, hid - lap : hid + lap] = (left[:, hid - lap :] + right[:, : 2 * lap]).astype(BF16)
        zbuf[4 + c, :, hid + lap :] = right[:, 2 * lap :].astype(BF16)
    line.tick(2)

    def spread(i):
        blocks[i] = tn(na_ref[...], gp_ref[:, (i - 1) * width : i * width]).astype(BF16).reshape(8, part, width)
        planes[i].pair()

    def settle(i):
        zbuf[8 + i] = planes[i].total().astype(BF16)

    local[13].wait()
    spread(1)
    spread(2)
    planes[1].combine()
    spread(3)
    planes[2].combine()
    planes[0].relay()
    line.tick(3)
    planes[3].combine()
    for i in range(3):
        loads[i].wait()
        term = nt(gp_ref[:, i * width : (i + 1) * width], wq_buf[...].reshape(width, width))
        gin_ref[...] = term if i == 0 else gin_ref[...] + term
        if i < 2:
            loads[i + 1].start()
    gna = gin_ref[...]
    planes[1].relay()
    fars[2].start()
    line.tick(4)
    for i, c in ((0, 0), (2, 1)):
        bias_z[0, c : c + 1] = jnp.sum(gp_ref[:, i * width : (i + 1) * width].astype(F32), axis=0, keepdims=True)
    send_bias = [remote_z(bias_z.at[0], bias_z.at[s], bz_send.at[s], bz_recv.at[s], along(s)) for s in steps]
    for copy in send_bias:
        copy.start()
    back, grad_scale = norm_back(tok_ref[...].astype(F32), per_row(selectors, mod_ref, 1, width), gna)
    to_slots(0, gna)
    to_slots(1, grad_scale)
    gin_ref[...] = gm_ref[...] + back
    line.tick(5)
    planes[2].relay()
    settle(0)
    line.tick(6)
    planes[3].relay()
    settle(1)
    line.tick(7)
    local[5].wait()
    for copy in fars:
        copy.wait_recv()
    branch = bb_in[0].astype(F32) + bb_in[1].astype(F32) + bb_in[2].astype(F32) + bb_in[3].astype(F32)
    branch = branch + mod_ref[slots : slots + 1, 3 * width : 4 * width]
    out_ref[...] = (mid_ref[...] + per_row(selectors, mod_ref, 5, width) * branch).astype(BF16)
    to_slots(5, cot_ref[...].astype(F32) * branch)
    mine = mods.at[me, pl.ds(pl.multiple_of(8 * z, 8), 8)]
    mine[...] = modrow[...].astype(BF16)
    send_mods = [remote_z(mine, mine, mz_send.at[s], mz_recv.at[s], along(s)) for s in steps]
    for copy in send_mods:
        copy.start()
    settle(2)
    line.tick(8)
    settle(3)
    line.tick(9)
    for copy in send_mods + send_bias:
        copy.wait_recv()
    gather = Gather(mods, md_send, md_recv, 16)
    gather.own()
    total = bias_z[0] + bias_z[1] + bias_z[2] + bias_z[3]
    gbup_out[...] = total[4:5, : gbup_out.shape[1]]
    bias_in[me] = total
    send_total = [remote(bias_in.at[me], bias_in.at[me], bi_send.at[e], bi_recv.at[e], e) for e in others]
    for copy in send_total:
        copy.start()
    line.tick(10)
    gather.along_x()
    gather.along_y()
    line.tick(11)
    gather.across()
    gather.finish()
    local[6].wait()
    plane_rows = mods[:, pl.ds(pl.multiple_of(8 * z, 8), 8), :].reshape(64, mods.shape[2])
    half = mods.shape[2]
    first, second = nt(plane_rows, wada_ref[:, :half]), nt(plane_rows, wada_ref[:, half:])
    upper = lax.rem(lax.broadcasted_iota(jnp.int32, (64, 1), 0), 8) < slots
    gc_out[...] = jnp.where(upper, first, second).reshape(gc_out.shape)
    send_gc = [remote(gc_out.at[flipped(e)], gc_in.at[me], gc_send.at[e], gc_recv.at[e], e) for e in others]
    for copy in send_gc:
        copy.start()
    gc_in[me] = gc_out[me]
    line.tick(12)
    for copy in send_total:
        copy.wait_recv()
    total = bias_in[0]
    for j in others:
        total = total + bias_in[j]
    bias_ref[...] = total
    line.tick(13)
    for copy in send_gc + send_picks:
        copy.wait_recv()
    line.end()
    for copy in ups + fars + send_picks + send_bias + send_mods + send_total + send_gc:
        copy.wait_send()
    for plane in planes:
        plane.drain()
    gather.drain()


def backward(sizes, tok, cot, mod, mid, gbup, pick, na, proj, probs, att, wo, bra, gnb, bbs, gdn, gup, wq, wada):
    rows, width = tok.shape
    part, columns = wada.shape
    wide = gdn.shape[0]
    S, V = jax.ShapeDtypeStruct, pltpu.VMEM
    vm, hbm = pl.BlockSpec(memory_space=pltpu.VMEM), pl.BlockSpec(memory_space=pl.ANY)
    dma = pltpu.SemaphoreType.DMA
    shapes = (
        S((rows, width), BF16), S((rows, width), F32), S((12, part, width), BF16), S((8, 32, columns // 2), BF16),
        S((8, 8, part), F32), S((4, 64, part), BF16), S((8, width), F32), S((1, wide), F32),
    )
    return pl.pallas_call(
        back_kernel,
        out_shape=shapes,
        in_specs=[pl.BlockSpec(memory_space=pltpu.SMEM)] + [vm] * 6 + [hbm] * 12,
        out_specs=(vm,) * len(shapes),
        scratch_shapes=[
            V((rows, width), BF16), V((rows, 3 * width), BF16), V((H, rows, rows), BF16), V((rows, width), BF16), V((8, part, width), BF16),
            V((8, part, wide), BF16), V((4, rows, width), BF16), V((12, part, width), BF16), V((12, 80, width), BF16),
            V((rows, width), F32), V((rows, width), BF16), V((rows, width), BF16), V((rows, 3 * width), BF16),
            V((4, 8, part, width), BF16), V((4, 4, part, width), BF16), V((4, 80, width), BF16), V((4, part - 80, width), BF16),
            V((4, part, width), BF16), V((4, part, width), BF16), V((8, part, width), BF16), V((part, columns), BF16),
            V((8, columns // 2), F32), V((4, 8, width), F32), V((8, 8, width), F32), V((8, 8, part), F32),
            dma((17,)), dma((8,)), dma((8,)), dma((4,)), dma((4,)), dma((5, 12)), dma((5, 12)), dma((4, 4)), dma((4, 4)),
            dma((4, 4)), dma((4, 4)), dma((8,)), dma((8,)), dma((4,)), dma((4,)), dma((4,)), dma((4,)), dma((4,)), dma((4,)),
            dma((8,)), dma((8,)), dma((8,)), dma((8,)),
        ],
        compiler_params=pltpu.CompilerParams(collective_id=2, has_side_effects=True, vmem_limit_bytes=61 << 20),
    )(sizes, tok, cot, mod, mid, gbup, pick, na, proj, probs, att, wo, bra, gnb, bbs, gdn, gup, wq, wada)

def finish_kernel(
    sums_ref, mods_ref, picks_ref, gc_ref, bias_ref, gbup_ref, cond_ref,
    gcond_ref, gada_ref, gbada_ref, gqkv_ref, gbqkv_ref, gout_ref, gbout_ref, gup_ref, gbup_out, gdown_ref, gbdown_ref,
    lanes,
):
    slots, width = cond_ref.shape
    part = width // 8
    half = mods_ref.shape[2]
    me, z = lax.axis_index("fsdp"), lax.axis_index("rep")
    for c in range(4):
        gdown_ref[c * part : (c + 1) * part] = sums_ref[c].astype(F32)
        gup_ref[:, c * width : (c + 1) * width] = sums_ref[4 + c].astype(F32)
    gout_ref[...] = sums_ref[8].astype(F32)
    for c in range(3):
        gqkv_ref[:, c * width : (c + 1) * width] = sums_ref[9 + c].astype(F32)
    rows = mods_ref[...].reshape(256, half)
    acts = jnp.stack([picks_ref[i] for i in range(4)], axis=0).reshape(4, 8, 8, part)
    acts = jnp.stack([acts[:, f] for f in range(8)], axis=0).reshape(256, part).astype(F32)
    upper = lax.rem(lax.broadcasted_iota(jnp.int32, (256, 1), 0), 8) < slots
    first, second = jnp.where(upper, acts, 0.0).astype(BF16), jnp.where(upper, 0.0, acts).astype(BF16)
    gada_ref[:, :half] = tn(first, rows)
    gada_ref[:, half:] = tn(second, rows)
    floats = rows.astype(F32)
    lanes[...] = jnp.zeros_like(lanes)

    def own(row, size):
        total = row.shape[1]
        lanes[0:1, :total] = row
        return pltpu.roll(lanes[:, :total], lax.rem(total - me * size, total), 1)[0, :size]

    column = jnp.concatenate(
        [
            jnp.sum(jnp.where(upper, floats, 0.0), axis=0, keepdims=True),
            jnp.sum(jnp.where(upper, 0.0, floats), axis=0, keepdims=True),
        ],
        axis=1,
    )
    gbada_ref[...] = own(column, gbada_ref.shape[0])
    gbqkv_ref[...] = own(jnp.concatenate([bias_ref[0:1], bias_ref[1:2]], axis=1), gbqkv_ref.shape[0])
    gbout_ref[...] = own(bias_ref[2:3], part)
    gbdown_ref[...] = own(bias_ref[3:4], part)
    wide, hid = gbup_ref.shape[1], gbup_out.shape[0]
    lanes[0:1, :wide] = gbup_ref[...]
    gbup_out[...] = pltpu.roll(lanes[:, :wide], lax.rem(wide - lax.rem(me, 2) * (wide - hid), wide), 1)[0, :hid]
    grad = None
    for j in range(8):
        lanes[:, :width] = jnp.zeros((8, width), F32)
        lanes[0:slots, :part] = gc_ref[j, 0:slots] + gc_ref[j, slots : 2 * slots]
        term = pltpu.roll(lanes[:, :width], j * part, 1) if j else lanes[:, :width]
        grad = term if grad is None else grad + term
    cond = cond_ref[...].astype(F32)
    gate = jax.nn.sigmoid(cond)
    gcond_ref[...] = grad[0:slots] * (gate * (1.0 + cond * (1.0 - gate)))


def finish(sums, mods, picks, gc, bias, gbup, cond, sizes):
    S = jax.ShapeDtypeStruct
    vm = pl.BlockSpec(memory_space=pltpu.VMEM)
    return pl.pallas_call(
        finish_kernel,
        out_shape=tuple(S(size, F32) for size in sizes),
        in_specs=[vm] * 7,
        out_specs=(vm,) * len(sizes),
        scratch_shapes=[pltpu.VMEM((8, 2 * mods.shape[2]), F32)],
        compiler_params=pltpu.CompilerParams(vmem_limit_bytes=56 << 20),
    )(sums, mods, picks, gc, bias, gbup, cond)

def fast(tokens, cond, image_sizes, w_ada, b_ada, w_qkv, b_qkv, w_out, b_out, w_up, b_up, w_down, b_down, cotangent):
    width = tokens.shape[1]
    part, columns = w_ada.shape
    hid = w_down.shape[0]
    wide = hid + 64
    mod, nb, gbb, wup, pick, na, proj, probs, att, bra, mid, wq, wo = start(
        image_sizes, tokens, cotangent, cond, w_ada, b_ada[None], b_qkv[None], b_out[None], b_down[None], w_qkv, w_out, w_up, wide
    )
    gnb, gbup, bbs, gdn, gup = mlp(nb, b_up[None], gbb, wup.reshape(width, wide), w_down)
    output, grad_input, sums, mods, gc, picks, bias, gbup = backward(
        image_sizes, tokens, cotangent, mod, mid, gbup, pick, na, proj, probs, att, wo, bra, gnb, bbs, gdn, gup, wq, w_ada
    )
    sizes = tuple(
        leaf.shape for leaf in (cond, w_ada, b_ada, w_qkv, b_qkv, w_out, b_out, w_up, b_up, w_down, b_down)
    )
    return (output, grad_input, *finish(sums, mods, picks, gc, bias, gbup, cond, sizes))


def solution(mesh):
    placed = (
        P(("fsdp", "rep"), None),
        P(("fsdp", "rep"), None),
        P(("fsdp", "rep")),
        P("fsdp", None),
        P("fsdp"),
        P("fsdp", None),
        P("fsdp"),
        P("fsdp", None),
        P("fsdp"),
        P("fsdp", None),
        P("fsdp"),
        P("fsdp", None),
        P("fsdp"),
        P(("fsdp", "rep"), None),
    )
    fits = mesh.shape["fsdp"] == 8 and mesh.shape["rep"] == 4
    return jax.shard_map(
        fast if fits else local,
        mesh=mesh,
        in_specs=placed,
        out_specs=(
            P(("fsdp", "rep"), None),
            P(("fsdp", "rep"), None),
            P(("fsdp", "rep"), None),
            P("fsdp", None),
            P("fsdp"),
            P("fsdp", None),
            P("fsdp"),
            P("fsdp", None),
            P("fsdp"),
            P("fsdp", None),
            P("fsdp"),
            P("fsdp", None),
            P("fsdp"),
        ),
        check_vma=False,
    )
```

```python
import functools

import jax
import jax.numpy as jnp
from jax import lax
from jax.experimental import pallas as pl
from jax.experimental.pallas import tpu as pltpu
from jax.sharding import PartitionSpec as P

H = 16
EPSILON = 1e-06
HIGHEST = lax.Precision.HIGHEST
MASKED = -1e30


def layer_norm(inputs):
    average = jnp.mean(inputs, axis=-1, keepdims=True)
    centered = inputs - average
    variance = jnp.mean(centered * centered, axis=-1, keepdims=True)
    return centered * lax.rsqrt(variance + EPSILON)


def modulate(hidden, shift_part, scale_part):
    return layer_norm(hidden) * (1.0 + scale_part) + shift_part


def gelu_tanh(inputs):
    return jax.nn.gelu(inputs, approximate=True)


def product(first_operand, second_operand):
    return jnp.dot(first_operand, second_operand, preferred_element_type=jnp.float32)


def product_back(first_operand, second_operand):
    return lax.dot_general(
        first_operand, second_operand, (((1,), (1,)), ((), ())), preferred_element_type=jnp.float32
    )


def outer_sum(first_operand, second_operand):
    return lax.dot_general(
        first_operand, second_operand, (((0,), (0,)), ((), ())), preferred_element_type=jnp.float32
    )


def fetch_forward(weight, bias_piece):
    return (
        lax.all_gather(weight, "fsdp", axis=0, tiled=True),
        lax.all_gather(bias_piece, "fsdp", axis=0, tiled=True),
    )


def weights_again(weight):
    return lax.all_gather(weight, "fsdp", axis=0, tiled=True)


def reduce_grads(weight_grad, bias_grad):
    row_part, bias_part = (
        lax.psum_scatter(weight_grad, "fsdp", scatter_dimension=0, tiled=True),
        lax.psum_scatter(bias_grad, "fsdp", scatter_dimension=0, tiled=True),
    )
    column_part = lax.psum_scatter(row_part, "rep", scatter_dimension=1, tiled=True)
    whole_rows, bias_stack = (
        lax.all_gather(column_part, "rep", axis=1, tiled=True),
        lax.all_gather(bias_part[None], "rep", axis=0, tiled=True),
    )
    return (whole_rows, jnp.sum(bias_stack, axis=0))


def local(
    tokens,
    cond,
    image_sizes,
    w_ada,
    b_ada,
    w_qkv,
    b_qkv,
    w_out,
    b_out,
    w_up,
    b_up,
    w_down,
    b_down,
    cotangent,
):
    row_count, model_width = tokens.shape
    head_count = H
    head_dim = model_width // head_count
    slot_count = image_sizes.shape[0]
    scale_factor = head_dim ** (-0.5)
    block_rows = min(512, row_count)
    block_count = row_count // block_rows
    image_ends = jnp.sum(
        jnp.where(jnp.arange(slot_count)[:, None] >= jnp.arange(slot_count)[None, :], image_sizes[None, :], 0), axis=1
    )
    positions = jnp.arange(row_count, dtype=jnp.int32)
    image_ids = jnp.sum((positions[:, None] >= image_ends[None, :]).astype(jnp.int32), axis=1)
    selector = (image_ids[:, None] == jnp.arange(slot_count, dtype=jnp.int32)[None, :]).astype(
        jnp.float32
    )
    cond_float = cond.astype(jnp.float32)
    activ_float, silu_pull = jax.vjp(jax.nn.silu, cond_float)
    activ_low = activ_float.astype(jnp.bfloat16)
    full_ada, full_bada = fetch_forward(w_ada, b_ada)
    modulation = product(activ_low, full_ada) + full_bada.astype(jnp.float32)
    per_token = jnp.dot(selector, modulation, precision=HIGHEST)
    shift_a, scale_a, gate_a, shift_b, scale_b, gate_b = jnp.split(per_token, 6, axis=1)
    hidden = tokens.astype(jnp.float32)
    normed_a, pull_a = jax.vjp(modulate, hidden, shift_a, scale_a)
    normed_a_low = normed_a.astype(jnp.bfloat16)
    full_qkv, full_bqkv = fetch_forward(w_qkv, b_qkv)
    bias_qkv = full_bqkv.astype(jnp.float32)
    bias_full = jnp.concatenate(
        [bias_qkv[:model_width], jnp.zeros((model_width,), jnp.float32), bias_qkv[model_width:]]
    )
    projected = (product(normed_a_low, full_qkv) + bias_full).astype(jnp.bfloat16)
    query_heads = projected[:, :model_width].reshape(row_count, head_count, head_dim)
    key_heads = projected[:, model_width : 2 * model_width].reshape(row_count, head_count, head_dim)
    value_heads = projected[:, 2 * model_width :].reshape(row_count, head_count, head_dim)
    query_blocks = query_heads.reshape(block_count, block_rows, head_count, head_dim)
    id_blocks = image_ids.reshape(block_count, block_rows)

    def scores_of(query_block, id_block):
        raw_scores = (
            jnp.einsum("qhd,khd->hqk", query_block, key_heads, preferred_element_type=jnp.float32)
            * scale_factor
        )
        same_image = id_block[:, None] == image_ids[None, :]
        return jnp.where(same_image[None], raw_scores, MASKED)

    def forward_block(block_item):
        query_block, id_block = block_item
        scores = scores_of(query_block, id_block)
        row_max = jnp.max(scores, axis=-1, keepdims=True)
        exponent = jnp.exp(scores - row_max)
        row_total = jnp.sum(exponent, axis=-1, keepdims=True)
        probabilities = (exponent / row_total).astype(jnp.bfloat16)
        attended_block = jnp.einsum(
            "hqk,khd->qhd", probabilities, value_heads, preferred_element_type=jnp.float32
        )
        return (attended_block.astype(jnp.bfloat16), (row_max + jnp.log(row_total))[:, :, 0])

    attended_blocks, lse_blocks = lax.map(forward_block, (query_blocks, id_blocks))
    attended = attended_blocks.reshape(row_count, model_width)
    full_out, full_bout = fetch_forward(w_out, b_out)
    branch_a = product(attended, full_out) + full_bout.astype(jnp.float32)
    middle = hidden + gate_a * branch_a
    normed_b, pull_b = jax.vjp(modulate, middle, shift_b, scale_b)
    normed_b_low = normed_b.astype(jnp.bfloat16)
    full_up, full_bup = fetch_forward(w_up, b_up)
    inner_pre = product(normed_b_low, full_up) + full_bup.astype(jnp.float32)
    activated, gelu_pull = jax.vjp(gelu_tanh, inner_pre)
    activated_low = activated.astype(jnp.bfloat16)
    full_down, full_bdown = fetch_forward(w_down, b_down)
    branch_b = product(activated_low, full_down) + full_bdown.astype(jnp.float32)
    output = (middle + gate_b * branch_b).astype(jnp.bfloat16)
    grad_out = cotangent.astype(jnp.float32)
    grad_gate_b = grad_out * branch_b
    grad_branch_b = (gate_b * grad_out).astype(jnp.bfloat16)
    grad_w_down, grad_b_down = reduce_grads(
        outer_sum(activated_low, grad_branch_b), jnp.sum(grad_branch_b.astype(jnp.float32), axis=0)
    )
    back_down = weights_again(w_down)
    grad_activated = product_back(grad_branch_b, back_down)
    (grad_inner,) = gelu_pull(grad_activated)
    grad_inner_low = grad_inner.astype(jnp.bfloat16)
    grad_w_up, grad_b_up = reduce_grads(
        outer_sum(normed_b_low, grad_inner_low), jnp.sum(grad_inner_low.astype(jnp.float32), axis=0)
    )
    back_up = weights_again(w_up)
    grad_normed_b = product_back(grad_inner_low, back_up)
    grad_middle_norm, grad_shift_b, grad_scale_b = pull_b(grad_normed_b)
    grad_middle = grad_out + grad_middle_norm
    grad_gate_a = grad_middle * branch_a
    grad_branch_a = (gate_a * grad_middle).astype(jnp.bfloat16)
    grad_w_out, grad_b_out = reduce_grads(
        outer_sum(attended, grad_branch_a), jnp.sum(grad_branch_a.astype(jnp.float32), axis=0)
    )
    back_out = weights_again(w_out)
    grad_attended = product_back(grad_branch_a, back_out).astype(jnp.bfloat16)
    grad_att_blocks = grad_attended.reshape(block_count, block_rows, head_count, head_dim)

    def backward_block(carried, block_item):
        key_grad, value_grad = carried
        query_block, id_block, grad_block, lse_block = block_item
        scores = scores_of(query_block, id_block)
        probabilities = jnp.exp(scores - lse_block[:, :, None])
        probabilities_low = probabilities.astype(jnp.bfloat16)
        grad_probs = jnp.einsum(
            "qhd,khd->hqk", grad_block, value_heads, preferred_element_type=jnp.float32
        )
        row_delta = jnp.sum(probabilities * grad_probs, axis=-1, keepdims=True)
        grad_scores = (probabilities * (grad_probs - row_delta)).astype(jnp.bfloat16)
        query_grad = (
            jnp.einsum("hqk,khd->qhd", grad_scores, key_heads, preferred_element_type=jnp.float32)
            * scale_factor
        )
        key_grad = (
            key_grad
            + jnp.einsum(
                "hqk,qhd->khd", grad_scores, query_block, preferred_element_type=jnp.float32
            )
            * scale_factor
        )
        value_grad = value_grad + jnp.einsum(
            "hqk,qhd->khd", probabilities_low, grad_block, preferred_element_type=jnp.float32
        )
        return ((key_grad, value_grad), query_grad)

    zero_heads = jnp.zeros((row_count, head_count, head_dim), jnp.float32)
    (grad_keys, grad_values), grad_query_blocks = lax.scan(
        backward_block,
        (zero_heads, zero_heads),
        (query_blocks, id_blocks, grad_att_blocks, lse_blocks),
    )
    grad_projected = jnp.concatenate(
        [
            grad_query_blocks.reshape(row_count, model_width),
            grad_keys.reshape(row_count, model_width),
            grad_values.reshape(row_count, model_width),
        ],
        axis=1,
    ).astype(jnp.bfloat16)
    column_sums = jnp.sum(grad_projected.astype(jnp.float32), axis=0)
    grad_bias_qkv = jnp.concatenate([column_sums[:model_width], column_sums[2 * model_width :]])
    grad_w_qkv, grad_b_qkv = reduce_grads(outer_sum(normed_a_low, grad_projected), grad_bias_qkv)
    back_qkv = weights_again(w_qkv)
    grad_normed_a = product_back(grad_projected, back_qkv)
    grad_hidden_norm, grad_shift_a, grad_scale_a = pull_a(grad_normed_a)
    grad_input = grad_middle + grad_hidden_norm
    grad_per_token = jnp.concatenate(
        [grad_shift_a, grad_scale_a, grad_gate_a, grad_shift_b, grad_scale_b, grad_gate_b], axis=1
    )
    grad_modulation = lax.dot_general(
        selector, grad_per_token, (((0,), (0,)), ((), ())), precision=HIGHEST
    ).astype(jnp.bfloat16)
    grad_w_ada, grad_b_ada = reduce_grads(
        outer_sum(activ_low, grad_modulation), jnp.sum(grad_modulation.astype(jnp.float32), axis=0)
    )
    back_ada = weights_again(w_ada)
    grad_activ = product_back(grad_modulation, back_ada)
    (grad_cond,) = silu_pull(grad_activ)
    return (
        output,
        grad_input,
        grad_cond,
        grad_w_ada,
        grad_b_ada,
        grad_w_qkv,
        grad_b_qkv,
        grad_w_out,
        grad_b_out,
        grad_w_up,
        grad_b_up,
        grad_w_down,
        grad_b_down,
    )


MESH = pl.DeviceIdType.MESH
F32, BF16 = jnp.float32, jnp.bfloat16


def flipped(offset):
    index = lax.axis_index("fsdp")
    y, x, core = index // 4, (index // 2) % 2, index % 2
    y = 1 - y if offset & 4 else y
    x = 1 - x if offset & 2 else x
    core = 1 - core if offset & 1 else core
    return y * 4 + x * 2 + core


def greet(offsets):
    barrier = pltpu.get_barrier_semaphore()
    for offset in offsets:
        pl.semaphore_signal(barrier, inc=1, device_id={"fsdp": flipped(offset)}, device_id_type=MESH)
    pl.semaphore_wait(barrier, len(offsets))


def remote(src, dst, send, recv, offset):
    return pltpu.make_async_remote_copy(
        src_ref=src, dst_ref=dst, send_sem=send, recv_sem=recv,
        device_id={"fsdp": flipped(offset)}, device_id_type=MESH,
    )


def lead(rows):
    return -(-rows // 32) * 16


class Gather:
    def __init__(self, shard, rows, send, recv, lead):
        first, second = pl.ds(0, lead), pl.ds(lead, rows - lead)
        piece = {e: shard(flipped(e)) for e in (0, 2, 4, 6)}
        plan = (
            (piece[0], 1), (piece[0], 2), (piece[0], 4),
            (piece[2].at[first], 4), (piece[4].at[second], 2),
            (piece[2], 1), (piece[4], 1), (piece[6], 1),
        )
        self.copies = [remote(ref, ref, send.at[i], recv.at[i], e) for i, (ref, e) in enumerate(plan)]

    def own(self):
        for i in (1, 2, 0):
            self.copies[i].start()

    def along(self):
        self.copies[1].wait_recv()
        self.copies[3].start()
        self.copies[5].start()
        self.copies[2].wait_recv()
        self.copies[4].start()
        self.copies[6].start()

    def across(self):
        self.copies[3].wait_recv()
        self.copies[4].wait_recv()
        self.copies[7].start()

    def sibling(self, p):
        self.copies[(0, 5, 6, 7)[p]].wait_recv()

    def finish(self):
        for p in range(4):
            self.sibling(p)

    def drain(self):
        for copy in self.copies:
            copy.wait_send()


class PlaneSum:
    def __init__(self, held, odd, pair_in, cross_a, cross_b, from_x, from_y, pair_send, pair_recv, send, recv, rows, lead):
        self.a, self.b = a, b = pl.ds(0, lead), pl.ds(lead, rows - lead)
        self.held, self.pair_in, self.cross_a, self.cross_b = held, pair_in, cross_a, cross_b
        self.from_x, self.from_y = from_x, from_y
        self.pairs = [] if odd is None else [
            remote(odd[p], pair_in[p], pair_send.at[p], pair_recv.at[p], 1) for p in range(4)
        ]
        plan = (
            (held[3].at[a], cross_a, 2), (held[3].at[b], cross_b, 4),
            (held[2].at[b], from_y.at[b], 4), (held[1].at[a], from_x.at[a], 2),
            (held[2].at[a], from_y.at[a], 4), (held[1].at[b], from_x.at[b], 2),
        )
        self.copies = [remote(src, dst, send.at[i], recv.at[i], e) for i, (src, dst, e) in enumerate(plan)]

    def pair(self):
        for p in (3, 2, 1, 0):
            self.pairs[p].start()

    def leave(self, p):
        if p == 3:
            self.copies[0].start()
            self.copies[1].start()
        elif p:
            self.copies[(None, 3, 2)[p]].start()

    def join(self, p):
        self.pairs[p].wait_recv()
        self.held[p][...] = (self.held[p][...].astype(F32) + self.pair_in[p][...].astype(F32)).astype(BF16)
        self.leave(p)

    def combine(self):
        for p in (3, 2, 1, 0):
            self.join(p)

    def relay(self):
        for i, p, part, came in ((0, 2, self.a, self.cross_a), (1, 1, self.b, self.cross_b)):
            self.copies[i].wait_recv()
            ref = self.held[p].at[part]
            ref[...] = (ref[...].astype(F32) + came[...].astype(F32)).astype(BF16)
            self.copies[4 + i].start()

    def total(self):
        for i in (2, 3, 4, 5):
            self.copies[i].wait_recv()
        return self.held[0][...].astype(F32) + self.from_x[...].astype(F32) + self.from_y[...].astype(F32)

    def drain(self):
        for copy in self.pairs + self.copies:
            copy.wait_send()


def nt(a, b):
    return lax.dot_general(a, b, (((1,), (1,)), ((), ())), preferred_element_type=F32)


def tn(a, b):
    return lax.dot_general(a, b, (((0,), (0,)), ((), ())), preferred_element_type=F32)


def nn(a, b):
    return jnp.dot(a, b, preferred_element_type=F32)


def normalized(values):
    centered = values - jnp.mean(values, axis=-1, keepdims=True)
    variance = jnp.mean(centered * centered, axis=-1, keepdims=True)
    scale = lax.rsqrt(variance + EPSILON)
    return centered * scale, scale


def image_of(place, sizes_ref):
    end = jnp.int32(0)
    image = jnp.zeros(place.shape, jnp.int32)
    for j in range(sizes_ref.shape[0]):
        end = end + sizes_ref[j]
        image = image + (place >= end).astype(jnp.int32)
    return image


def per_row(selectors, modulation, part, width):
    total = None
    for j, chosen in enumerate(selectors):
        term = chosen * modulation[j : j + 1, part * width : (part + 1) * width]
        total = term if total is None else total + term
    return total


def head_window(head, head_dim):
    low = head * head_dim
    base = low // 128 * 128
    wide = 128 if low - base + head_dim <= 128 else 256
    lane = lax.broadcasted_iota(jnp.int32, (1, wide), 1) + (base - low)
    mask = jnp.where((lane >= 0) & (lane < head_dim), 1.0, 0.0)
    return base, wide, mask


GELU_RATE = 0.7978845608028654
GELU_CUBE = 0.044715


def gelu_parts(u):
    square = u * u
    bend = jnp.tanh(GELU_RATE * u * (1.0 + GELU_CUBE * square))
    half = 0.5 * (1.0 + bend)
    slope = half + 0.5 * u * (1.0 - bend * bend) * (GELU_RATE * (1.0 + 3.0 * GELU_CUBE * square))
    return u * half, slope


def front_kernel(
    sizes_ref, tok_ref, cot_ref, cond_ref, wada_ref, bada_ref, bqkv_ref, bout_ref, bdown_ref, bup_in,
    wqkv_hbm, wout_hbm, wup_hbm, wdn_hbm,
    mod_ref, gnb_ref, gbup_ref, pick_ref, na_hbm, proj_hbm, probs_hbm, att_hbm, bra_hbm, mid_hbm, wq_hbm, wo_hbm,
    bb_hbm, gdn_hbm, gup_hbm,
    na_ref, proj_ref, probs_ref, att_ref, bra_ref, mid_ref, arena, wo_all, bb_ref, gdn_ref, gup_ref,
    cond_all, pm, mpair, mfar, lay, lay_b, nb_all, gbb_all, wup_all, wdn_ref, act_all, gi_all, in_pair, cross_a, cross_b, from_x, from_y,
    loc_sem, save_sem, c_send, c_recv, mp_send, mp_recv, mf_send, mf_recv, up_send, up_recv,
    q_send, q_recv, o_send, o_recv, g_send, g_recv, n_send, n_recv, pr_send, pr_recv, far_send, far_recv,
):
    rows, width = tok_ref.shape
    head_dim = width // H
    slots = sizes_ref.shape[0]
    part = wada_ref.shape[0]
    own, wide = wdn_hbm.shape[0], wup_all.shape[1]
    me = flipped(0)
    others = range(1, 8)

    def strip(ref, size):
        return lambda j: ref.at[pl.ds(pl.multiple_of(j * size, 8), size)]

    def up_piece(e):
        j = flipped(e)
        begin = pl.multiple_of(2 * own * (j // 2) + (2 * own - wide) * (j % 2), 128)
        return wup_hbm.at[:, pl.ds(begin, wide)]

    shift = lax.rem(me, 2) * (wide - own)
    blank = lax.rem(me + 1, 2) * own
    wq_strip, wup_strip = strip(arena, 3 * part), strip(wup_all, part)
    sources = [
        (wqkv_hbm.at[:, pl.ds(i * width, width)], arena.at[pl.ds(pl.multiple_of(me * 3 * part + i * part, 8), part)]) for i in range(3)
    ] + [
        (wout_hbm, strip(wo_all, part)(me)), (up_piece(0), wup_strip(me)),
        (wdn_hbm, wdn_ref.at[pl.ds(pl.multiple_of(shift, 8), own)]),
    ]
    local = [pltpu.make_async_copy(src, dst, loc_sem.at[i]) for i, (src, dst) in enumerate(sources)]
    for copy in local:
        copy.start()
    saves = [
        pltpu.make_async_copy(src, dst, save_sem.at[i])
        for i, (src, dst) in enumerate((
            (na_ref, na_hbm), (proj_ref, proj_hbm), (probs_ref, probs_hbm), (att_ref, att_hbm),
            (bra_ref, bra_hbm), (mid_ref, mid_hbm), (arena, wq_hbm), (wo_all, wo_hbm),
            (bb_ref, bb_hbm), (gdn_ref, gdn_hbm), (gup_ref, gup_hbm),
        ))
    ]
    act = jax.nn.silu(cond_ref[...].astype(F32))
    cond_all[me, :slots] = act
    cond_all[me, slots:] = act
    qkv = Gather(wq_strip, 3 * part, q_send, q_recv, lead(3 * part))
    out = Gather(strip(wo_all, part), part, o_send, o_recv, lead(part))
    gbb = Gather(lambda j: gbb_all.at[j], rows, g_send, g_recv, rows // 2)
    nb = Gather(lambda j: nb_all.at[j], rows, n_send, n_recv, rows // 2)
    conds = [remote(cond_all.at[me], cond_all.at[me], c_send.at[e], c_recv.at[e], e) for e in others]
    ups = [remote(up_piece(e), wup_strip(me), up_send.at[e], up_recv.at[e], e) for e in others]
    pairs = [remote(pm.at[flipped(2 * p + 1)], mpair.at[p], mp_send.at[p], mp_recv.at[p], 1) for p in range(4)]
    fars = [remote(pm.at[flipped(2 * p)], mfar.at[p], mf_send.at[p], mf_recv.at[p], 2 * p) for p in range(1, 4)]
    block = [arena.at[pl.ds(i * rows, rows)] for i in range(12)]
    gnb = PlaneSum(
        block[8:], block[:4], [in_pair.at[p] for p in range(4)], cross_a, cross_b, from_x, from_y,
        pr_send, pr_recv, far_send, far_recv, rows, rows // 2,
    )
    bb_pairs = [remote(block[4 + p], in_pair.at[4 + p], pr_send.at[4 + p], pr_recv.at[4 + p], 1) for p in range(4)]

    greet(others)
    for copy in conds:
        copy.start()
    for copy in local[:3]:
        copy.wait()
    qkv.own()
    lay[...] = jnp.zeros_like(lay)
    lay_b[...] = jnp.zeros_like(lay_b)
    lay[0:1, : bada_ref.shape[0]] = bada_ref[...].astype(F32)[None]
    bada = pltpu.roll(lay[...], me * bada_ref.shape[0], 1)[0:1]
    begin = 0
    for ref in (bqkv_ref, bout_ref, bdown_ref):
        size = ref.shape[0]
        lay_b[0:1, begin : begin + size] = ref[...].astype(F32)[None]
        lay_b[0:1, begin : begin + 8 * size] = pltpu.roll(lay_b[:, begin : begin + 8 * size], me * size, 1)[0:1]
        begin += 8 * size
    for copy in conds:
        copy.wait_recv()
    everyone = cond_all[...].reshape(8 * cond_all.shape[1], width).astype(BF16)
    pick = (
        lax.broadcasted_iota(jnp.int32, (width, part), 0) == lax.broadcasted_iota(jnp.int32, (width, part), 1) + me * part
    )
    chosen = nn(everyone, jnp.where(pick, 1.0, 0.0).astype(BF16)).astype(BF16)
    pick_ref[...] = chosen
    bias_row = lax.broadcasted_iota(jnp.int32, (8, 1), 0) == slots
    piece = nn(chosen, wada_ref[...]).reshape(pm.shape)
    pm[...] = piece + bada[None]
    pm[:, :, : lay_b.shape[1]] = jnp.where(bias_row[None], lay_b[0:1][None], pm[:, :, : lay_b.shape[1]])
    for copy in pairs:
        copy.start()
    for p in (3, 2, 1, 0):
        pairs[p].wait_recv()
        pm[flipped(2 * p)] += mpair[p]
        if p:
            fars[p - 1].start()
    qkv.along()
    local[3].wait()
    out.own()
    lay[...] = jnp.zeros_like(lay)
    lay[0:1, :own] = bup_in[...].astype(F32)[None]
    bup = pltpu.roll(lay[:, :wide], shift, 1)[0:1]
    wdn_ref[pl.ds(pl.multiple_of(blank, 8), wide - own)] = jnp.zeros((wide - own, width), BF16)
    for copy in fars:
        copy.wait_recv()
    modulation = pm[me] + (mfar[1] + mfar[2] + mfar[3])
    mod_ref[...] = modulation
    bias = modulation[slots : slots + 1]
    image = image_of(lax.broadcasted_iota(jnp.int32, (rows, 1), 0), sizes_ref)
    selectors = [jnp.where(image == j, 1.0, 0.0) for j in range(slots)]
    gbb_all[me] = (per_row(selectors, mod_ref, 5, width) * cot_ref[...].astype(F32)).astype(BF16)
    gbb.own()
    hidden = tok_ref[...].astype(F32)
    na_ref[...] = (
        normalized(hidden)[0] * (1.0 + per_row(selectors, mod_ref, 1, width)) + per_row(selectors, mod_ref, 0, width)
    ).astype(BF16)
    saves[0].start()
    qkv.across()
    for copy in ups:
        copy.start()
    out.along()
    qkv.finish()
    saves[6].start()
    for i in range(3):
        strips = [arena[3 * part * j + i * part : 3 * part * j + (i + 1) * part] for j in range(8)]
        value = nn(na_ref[...], jnp.concatenate(strips, axis=0))
        if i == 0:
            value = value + bias[:, :width]
        if i == 2:
            value = value + bias[:, width : 2 * width]
        proj_ref[:, i * width : (i + 1) * width] = value.astype(BF16)
    saves[1].start()
    att_ref[...] = jnp.zeros_like(att_ref)
    row_image = image_of(lax.broadcasted_iota(jnp.int32, (rows, rows), 0), sizes_ref)
    column_image = image_of(lax.broadcasted_iota(jnp.int32, (rows, rows), 1), sizes_ref)
    hidden_pairs = jnp.where(row_image == column_image, 0.0, -1e30)
    for head in range(H):
        base, window, mask = head_window(head, head_dim)
        mask = mask.astype(BF16)
        query = proj_ref[:, base : base + window] * mask
        key = proj_ref[:, width + base : width + base + window]
        value = proj_ref[:, 2 * width + base : 2 * width + base + window] * mask
        scores = nt(query, key) * head_dim ** (-0.5) + hidden_pairs
        exponent = jnp.exp(scores - jnp.max(scores, axis=-1, keepdims=True))
        probs = (exponent * (1.0 / jnp.sum(exponent, axis=-1, keepdims=True))).astype(BF16)
        probs_ref[head] = probs
        att_ref[:, base : base + window] += nn(probs, value).astype(BF16)
        if head == 5:
            out.across()
    saves[2].start()
    saves[3].start()
    gbb.along()
    out.finish()
    saves[7].start()
    branch = nn(att_ref[...], wo_all[...]) + bias[:, 2 * width : 3 * width]
    bra_ref[...] = branch
    middle = tok_ref[...].astype(F32) + per_row(selectors, mod_ref, 2, width) * branch
    mid_ref[...] = middle
    nb_all[me] = (
        normalized(middle)[0] * (1.0 + per_row(selectors, mod_ref, 4, width)) + per_row(selectors, mod_ref, 3, width)
    ).astype(BF16)
    nb.own()
    saves[4].start()
    saves[5].start()

    qkv.drain()
    saves[6].wait()
    local[4].wait()
    local[5].wait()
    for copy in ups:
        copy.wait_recv()
    gbb.across()

    def one(slot):
        inner = nn(nb_all[slot], wup_all[...]) + bup
        act, slope = gelu_parts(inner)
        act_all[slot] = act.astype(BF16)
        gi_all[slot] = (slope * nt(gbb_all[slot], wdn_ref[...])).astype(BF16)

    for p in range(4):
        even, odd = flipped(2 * p), flipped(2 * p + 1)
        if p == 1:
            nb.along()
        if p == 3:
            nb.across()
        one(even)
        block[8 + p][...] = nt(gi_all[even], wup_all[...]).astype(BF16)
        gbb.sibling(p)
        nb.sibling(p)
        one(odd)
        block[p][...] = nt(gi_all[odd], wup_all[...]).astype(BF16)
        gnb.pairs[p].start()
        gnb.join(p)

    def forth(p):
        even, odd = flipped(2 * p), flipped(2 * p + 1)
        block[4 + p][...] = nn(act_all[odd], wdn_ref[...]).astype(BF16)
        bb_pairs[p].start()
        bb_ref[p] = nn(act_all[even], wdn_ref[...]).astype(BF16)

    forth(0)
    forth(1)
    forth(2)
    forth(3)
    gnb.relay()
    gdn_ref[...] = tn(act_all[...].reshape(8 * rows, wide), gbb_all[...].reshape(8 * rows, width)).astype(BF16)
    saves[9].start()
    inner_grads = gi_all[...].reshape(8 * rows, wide)
    gup_ref[...] = tn(nb_all[...].reshape(8 * rows, width), inner_grads).astype(BF16).reshape(gup_ref.shape)
    saves[10].start()
    gbup_ref[...] = jnp.sum(inner_grads.astype(F32), axis=0, keepdims=True)
    for p in range(4):
        bb_pairs[p].wait_recv()
        bb_ref[p] = (bb_ref[p].astype(F32) + in_pair[4 + p].astype(F32)).astype(BF16)
    saves[8].start()
    gnb_ref[...] = gnb.total()
    for copy in conds + pairs + fars + ups + bb_pairs:
        copy.wait_send()
    for gather in (out, gbb, nb, gnb):
        gather.drain()
    for i, copy in enumerate(saves):
        if i != 6:
            copy.wait()


def front(sizes, tok, cot, cond, wada, bada, bqkv, bout, bdown, bup, wqkv, wout, wup, wdn):
    rows, width = tok.shape
    part, columns = wada.shape
    wide = wdn.shape[0] + 64
    S, V = jax.ShapeDtypeStruct, pltpu.VMEM
    vm, hbm = pl.BlockSpec(memory_space=pltpu.VMEM), pl.BlockSpec(memory_space=pl.ANY)
    dma = pltpu.SemaphoreType.DMA
    kept = (
        ((rows, width), BF16), ((rows, 3 * width), BF16), ((H, rows, rows), BF16), ((rows, width), BF16),
        ((rows, width), F32), ((rows, width), F32), ((24 * part, width), BF16), ((8 * part, width), BF16),
        ((4, rows, width), BF16), ((wide, width), BF16), ((8, part, wide), BF16),
    )
    shapes = (S((8, columns), F32), S((rows, width), F32), S((1, wide), F32), S((64, part), BF16)) + tuple(S(*pair) for pair in kept)
    return pl.pallas_call(
        front_kernel,
        out_shape=shapes,
        in_specs=[pl.BlockSpec(memory_space=pltpu.SMEM)] + [vm] * 9 + [hbm] * 4,
        out_specs=(vm,) * 4 + (hbm,) * 11,
        scratch_shapes=[V(*pair) for pair in kept] + [
            V((8, 8, width), F32), V((8, 8, columns), F32), V((4, 8, columns), F32),
            V((4, 8, columns), F32), V((8, columns), F32), V((8, 4 * width), F32),
            V((8, rows, width), BF16), V((8, rows, width), BF16), V((8 * part, wide), BF16), V((wide, width), BF16),
            V((8, rows, wide), BF16), V((8, rows, wide), BF16), V((8, rows, width), BF16),
            V((rows // 2, width), BF16), V((rows // 2, width), BF16), V((rows, width), BF16), V((rows, width), BF16),
            dma((6,)), dma((11,)), dma((8,)), dma((8,)), dma((4,)), dma((4,)), dma((4,)), dma((4,)),
        ] + [dma((8,))] * 14,
        compiler_params=pltpu.CompilerParams(collective_id=0, has_side_effects=True, vmem_limit_bytes=61 << 20),
    )(sizes, tok, cot, cond, wada, bada, bqkv, bout, bdown, bup, wqkv, wout, wup, wdn)

def along(step):
    return lax.rem(lax.axis_index("rep") + step, 4)


def remote_z(src, dst, send, recv, z):
    return pltpu.make_async_remote_copy(
        src_ref=src, dst_ref=dst, send_sem=send, recv_sem=recv, device_id={"rep": z}, device_id_type=MESH
    )


class LineSum:
    def __init__(self, chunks, held, halves, send, recv, lead):
        self.chunks, self.held, self.halves, self.send, self.recv = chunks, held, halves, send, recv
        rows = chunks.shape[1]
        self.parts = (pl.ds(0, lead), pl.ds(lead, rows - lead))
        self.sizes = (lead, rows - lead)

    def on(self, roles, action):
        z = lax.axis_index("rep")
        for role in roles:
            pl.when(z == role)(functools.partial(action, role))

    def enter(self, c, role):
        mate = (1, 0, 3, 2)[role]
        return remote_z(self.chunks.at[c], self.held.at[c], self.send.at[0, c], self.recv.at[0, c], mate)

    def give(self, c, role):
        half = 2 - role
        space = self.halves.at[c, pl.ds(0, self.sizes[half])]
        return remote_z(self.chunks.at[c, self.parts[half]], space, self.send.at[1, c], self.recv.at[1, c], 3 - role)

    def result(self, c, half, kind, target):
        ref = self.held.at[c, self.parts[half]]
        return remote_z(ref, ref, self.send.at[kind, c], self.recv.at[kind, c], target)

    def begin(self, c):
        def action(role):
            if c >= 2:
                self.enter(c - 2, role).wait_send()
            self.enter(c, role).start()

        self.on((0, 3), action)

    def first(self, c):
        def action(role):
            self.enter(c, role).wait_recv()
            self.chunks[c] = (self.chunks[c].astype(F32) + self.held[c].astype(F32)).astype(BF16)
            self.give(c, role).start()

        self.on((1, 2), action)

    def second(self, c):
        def action(role):
            mine = role - 1
            self.give(c, 3 - role).wait_recv()
            part, size = self.parts[mine], self.sizes[mine]
            self.held[c, part] = (self.chunks[c, part].astype(F32) + self.halves[c, :size].astype(F32)).astype(BF16)
            self.result(c, mine, 2, 3 - role).start()
            self.result(c, mine, 3, (1, 0, 3, 2)[role]).start()

        self.on((1, 2), action)

    def third(self, c):
        def action(role):
            other = 2 - role
            self.result(c, other, 2, 3 - role).wait_recv()
            self.result(c, other, 4, (1, 0, 3, 2)[role]).start()

        self.on((1, 2), action)

    def tick(self, n):
        count = self.chunks.shape[0]
        for step, c in ((self.begin, n + 2), (self.first, n), (self.second, n - 1), (self.third, n - 2)):
            if 0 <= c < count:
                step(c)

    def end(self):
        def outer(role):
            near = 0 if role == 0 else 1
            for c in range(self.chunks.shape[0]):
                self.result(c, near, 3, 1).wait_recv()
                self.result(c, 1 - near, 4, 1).wait_recv()
                if c >= self.chunks.shape[0] - 2:
                    self.enter(c, role).wait_send()

        def inner(role):
            for c in range(self.chunks.shape[0]):
                self.give(c, role).wait_send()
                self.result(c, role - 1, 2, 3 - role).wait_send()
                self.result(c, role - 1, 3, 3 - role).wait_send()
                self.result(c, 2 - role, 4, 3 - role).wait_send()

        self.on((0, 3), outer)
        self.on((1, 2), inner)


def norm_back(values, scale_part, grad):
    normal, rate = normalized(values)
    inner = grad * (1.0 + scale_part)
    back = rate * (
        inner - jnp.mean(inner, axis=-1, keepdims=True) - normal * jnp.mean(inner * normal, axis=-1, keepdims=True)
    )
    return back, grad * normal


def back_kernel(
    sizes_ref, tok_ref, cot_ref, mod_ref, mid_ref, gbup_ref, pick_ref, na_hbm, proj_hbm, probs_hbm, att_hbm, wo_hbm,
    bra_hbm, gnb_hbm, bbs_hbm, gdn_hbm, gup_hbm, wq_hbm, wada_hbm,
    out_ref, gin_ref, sums, mods, gc_in, picks, bias_ref, gbup_out,
    na_ref, proj_ref, probs_ref, att_ref, wo_all,
    gup_in, bb_in, zbuf, zhalf, gm_ref, gba_ref, gatt_ref, gp_ref, blocks, pair_in, cross_a, cross_b, from_x, from_y,
    wq_buf, wada_ref, modrow, bias_z, bias_in, gc_out,
    loc_sem, up_send, up_recv, bb_send, bb_recv, z_send, z_recv, ps_send, ps_recv, pc_send, pc_recv,
    md_send, md_recv, mz_send, mz_recv, pk_send, pk_recv, bz_send, bz_recv, bi_send, bi_recv, gc_send, gc_recv,
):
    rows, width = tok_ref.shape
    head_dim = width // H
    slots = sizes_ref.shape[0]
    part = width // 8
    hid = 8 * part // 2
    me, z = flipped(0), lax.axis_index("rep")
    core = lax.rem(me, 2)
    others, steps = range(1, 8), range(1, 4)

    line = LineSum(zbuf, sums, zhalf, z_send, z_recv, lead(part))
    planes = [
        PlaneSum(
            [blocks.at[i, flipped(2 * p)] for p in range(4)], [blocks.at[i, flipped(2 * p + 1)] for p in range(4)],
            [pair_in.at[i, p] for p in range(4)], cross_a.at[i], cross_b.at[i], from_x.at[i], from_y.at[i],
            ps_send.at[i], ps_recv.at[i], pc_send.at[i], pc_recv.at[i], part, lead(part),
        )
        for i in range(4)
    ]
    ups = [remote(gup_hbm.at[flipped(e)], gup_in.at[me], up_send.at[e], up_recv.at[e], e) for e in others]
    fars = [remote(bbs_hbm.at[p], bb_in.at[p], bb_send.at[p], bb_recv.at[p], 2 * p) for p in (1, 2, 3)]
    shift = (gdn_hbm.shape[0] - hid) * core
    local = [pltpu.make_async_copy(gdn_hbm.at[pl.ds(pl.multiple_of(shift + part * c, 16), part)], zbuf.at[c], loc_sem.at[c]) for c in range(4)]
    local.append(pltpu.make_async_copy(gup_hbm.at[me], gup_in.at[me], loc_sem.at[4]))
    local.append(pltpu.make_async_copy(bbs_hbm.at[0], bb_in.at[0], loc_sem.at[5]))
    local.append(pltpu.make_async_copy(wada_hbm, wada_ref, loc_sem.at[6]))
    loads = [pltpu.make_async_copy(wq_hbm.at[:, pl.ds(i * part, part)], wq_buf, loc_sem.at[7 + i]) for i in range(3)]
    local.append(pltpu.make_async_copy(bra_hbm, gm_ref, loc_sem.at[10]))
    local.append(pltpu.make_async_copy(gnb_hbm, gin_ref, loc_sem.at[11]))
    local += [
        pltpu.make_async_copy(src, dst, loc_sem.at[12 + i])
        for i, (src, dst) in enumerate((
            (wo_hbm, wo_all), (att_hbm, att_ref), (proj_hbm, proj_ref), (probs_hbm, probs_ref), (na_hbm, na_ref),
        ))
    ]
    for i in (7, 8, 0, 1, 9, 10, 2, 3, 11, 12, 4, 5, 13, 6):
        local[i].start()
    loads[0].start()
    picks[z] = pick_ref[...]

    barrier = pltpu.get_barrier_semaphore()
    for e in others:
        pl.semaphore_signal(barrier, inc=1, device_id={"fsdp": flipped(e)}, device_id_type=MESH)
    for s in steps:
        pl.semaphore_signal(barrier, inc=1, device_id={"rep": along(s)}, device_id_type=MESH)
    pl.semaphore_wait(barrier, 10)

    for copy in ups:
        copy.start()
    for c in range(4):
        local[c].wait()
    line.begin(0)
    line.begin(1)
    send_picks = [remote_z(picks.at[z], picks.at[z], pk_send.at[s], pk_recv.at[s], along(s)) for s in steps]
    for copy in send_picks:
        copy.start()

    image = image_of(lax.broadcasted_iota(jnp.int32, (rows, 1), 0), sizes_ref)
    selectors = [jnp.where(image == j, 1.0, 0.0) for j in range(slots)]
    slot = lax.broadcasted_iota(jnp.int32, (8, rows), 0)
    where = image_of(lax.broadcasted_iota(jnp.int32, (8, rows), 1), sizes_ref)
    gather_rows = (jnp.where((where == slot) & (slot < slots), 1.0, 0.0), jnp.where((where == slot - slots) & (where < slots), 1.0, 0.0))
    modrow[...] = jnp.zeros_like(modrow)

    def to_slots(index, values):
        modrow[:, (index % 3) * width : (index % 3 + 1) * width] += lax.dot_general(
            gather_rows[index // 3], values, (((1,), (0,)), ((), ())), precision=lax.Precision.HIGHEST, preferred_element_type=F32
        )

    cot = cot_ref[...].astype(F32)
    local[7].wait()
    local[8].wait()
    back, grad_scale = norm_back(mid_ref[...], per_row(selectors, mod_ref, 4, width), gin_ref[...])
    to_slots(3, gin_ref[...])
    to_slots(4, grad_scale)
    gm = cot + back
    to_slots(2, gm * gm_ref[...])
    gm_ref[...] = gm
    gba = (per_row(selectors, mod_ref, 2, width) * gm).astype(BF16)
    gba_ref[...] = gba
    bias_z[0] = jnp.zeros(bias_z.shape[1:], F32)
    bias_z[0, 2:3] = jnp.sum(gba.astype(F32), axis=0, keepdims=True)
    gbb = (per_row(selectors, mod_ref, 5, width) * cot).astype(BF16)
    bias_z[0, 3:4] = jnp.sum(gbb.astype(F32), axis=0, keepdims=True)
    bias_z[0, 4:5, : gbup_ref.shape[1]] = gbup_ref[...]
    local[9].wait()
    gatt_ref[...] = nt(gba_ref[...], wo_all[...].reshape(width, width)).astype(BF16)
    local[10].wait()
    blocks[0] = tn(att_ref[...], gba_ref[...]).astype(BF16).reshape(8, part, width)
    planes[0].pair()
    line.tick(0)

    gp_ref[...] = jnp.zeros_like(gp_ref)
    rate = head_dim ** (-0.5)

    def head_back(head):
        base, window, mask = head_window(head, head_dim)
        mask = mask.astype(BF16)
        at = [pl.ds(i * width + base, window) for i in range(3)]
        query, key, value = proj_ref[:, at[0]] * mask, proj_ref[:, at[1]] * mask, proj_ref[:, at[2]]
        grad = gatt_ref[:, at[0]] * mask
        low = probs_ref[head]
        probs = low.astype(F32)
        grad_probs = nt(grad, value)
        delta = jnp.sum(probs * grad_probs, axis=-1, keepdims=True)
        grad_scores = (probs * (grad_probs - delta)).astype(BF16)
        gp_ref[:, at[0]] += (nn(grad_scores, key) * rate).astype(BF16)
        gp_ref[:, at[1]] += (tn(grad_scores, query) * rate).astype(BF16)
        gp_ref[:, at[2]] += tn(low, grad).astype(BF16)

    local[11].wait()
    local[12].wait()
    for head in range(3):
        head_back(head)
    planes[0].combine()
    fars[0].start()
    fars[1].start()
    for head in range(3, 10):
        head_back(head)
    line.tick(1)
    for head in range(10, 16):
        head_back(head)
    local[4].wait()
    for copy in ups:
        copy.wait_recv()
    lap = gup_in.shape[2] - hid
    for c in range(4):
        left, right = gup_in[2 * c].astype(F32), gup_in[2 * c + 1].astype(F32)
        zbuf[4 + c, :, : hid - lap] = left[:, : hid - lap].astype(BF16)
        zbuf[4 + c, :, hid - lap : hid + lap] = (left[:, hid - lap :] + right[:, : 2 * lap]).astype(BF16)
        zbuf[4 + c, :, hid + lap :] = right[:, 2 * lap :].astype(BF16)
    line.tick(2)

    def spread(i):
        blocks[i] = tn(na_ref[...], gp_ref[:, (i - 1) * width : i * width]).astype(BF16).reshape(8, part, width)
        planes[i].pair()

    def settle(i):
        zbuf[8 + i] = planes[i].total().astype(BF16)

    local[13].wait()
    spread(1)
    spread(2)
    planes[1].combine()
    spread(3)
    planes[2].combine()
    planes[0].relay()
    line.tick(3)
    planes[3].combine()
    for i in range(3):
        loads[i].wait()
        term = nt(gp_ref[:, i * width : (i + 1) * width], wq_buf[...].reshape(width, width))
        gin_ref[...] = term if i == 0 else gin_ref[...] + term
        if i < 2:
            loads[i + 1].start()
    gna = gin_ref[...]
    planes[1].relay()
    fars[2].start()
    line.tick(4)
    for i, c in ((0, 0), (2, 1)):
        bias_z[0, c : c + 1] = jnp.sum(gp_ref[:, i * width : (i + 1) * width].astype(F32), axis=0, keepdims=True)
    send_bias = [remote_z(bias_z.at[0], bias_z.at[s], bz_send.at[s], bz_recv.at[s], along(s)) for s in steps]
    for copy in send_bias:
        copy.start()
    back, grad_scale = norm_back(tok_ref[...].astype(F32), per_row(selectors, mod_ref, 1, width), gna)
    to_slots(0, gna)
    to_slots(1, grad_scale)
    gin_ref[...] = gm_ref[...] + back
    line.tick(5)
    planes[2].relay()
    settle(0)
    line.tick(6)
    planes[3].relay()
    settle(1)
    line.tick(7)
    local[5].wait()
    for copy in fars:
        copy.wait_recv()
    branch = bb_in[0].astype(F32) + bb_in[1].astype(F32) + bb_in[2].astype(F32) + bb_in[3].astype(F32)
    branch = branch + mod_ref[slots : slots + 1, 3 * width : 4 * width]
    out_ref[...] = (mid_ref[...] + per_row(selectors, mod_ref, 5, width) * branch).astype(BF16)
    to_slots(5, cot_ref[...].astype(F32) * branch)
    mine = mods.at[me, pl.ds(pl.multiple_of(8 * z, 8), 8)]
    mine[...] = modrow[...].astype(BF16)
    send_mods = [remote_z(mine, mine, mz_send.at[s], mz_recv.at[s], along(s)) for s in steps]
    for copy in send_mods:
        copy.start()
    settle(2)
    line.tick(8)
    settle(3)
    line.tick(9)
    for copy in send_mods + send_bias:
        copy.wait_recv()
    gather = Gather(lambda j: mods.at[j], mods.shape[1], md_send, md_recv, mods.shape[1] // 2)
    gather.own()
    total = bias_z[0] + bias_z[1] + bias_z[2] + bias_z[3]
    gbup_out[...] = total[4:5, : gbup_out.shape[1]]
    bias_in[me] = total
    send_total = [remote(bias_in.at[me], bias_in.at[me], bi_send.at[e], bi_recv.at[e], e) for e in others]
    for copy in send_total:
        copy.start()
    line.tick(10)
    gather.along()
    line.tick(11)
    gather.across()
    gather.finish()
    local[6].wait()
    plane_rows = mods[:, pl.ds(pl.multiple_of(8 * z, 8), 8), :].reshape(64, mods.shape[2])
    half = mods.shape[2]
    first, second = nt(plane_rows, wada_ref[:, :half]), nt(plane_rows, wada_ref[:, half:])
    upper = lax.rem(lax.broadcasted_iota(jnp.int32, (64, 1), 0), 8) < slots
    gc_out[...] = jnp.where(upper, first, second).reshape(gc_out.shape)
    send_gc = [remote(gc_out.at[flipped(e)], gc_in.at[me], gc_send.at[e], gc_recv.at[e], e) for e in others]
    for copy in send_gc:
        copy.start()
    gc_in[me] = gc_out[me]
    line.tick(12)
    for copy in send_total:
        copy.wait_recv()
    total = bias_in[0]
    for j in others:
        total = total + bias_in[j]
    bias_ref[...] = total
    line.tick(13)
    for copy in send_gc + send_picks:
        copy.wait_recv()
    line.end()
    for copy in ups + fars + send_picks + send_bias + send_mods + send_total + send_gc:
        copy.wait_send()
    for plane in planes:
        plane.drain()
    gather.drain()


def backward(sizes, tok, cot, mod, mid, gbup, pick, na, proj, probs, att, wo, bra, gnb, bbs, gdn, gup, wq, wada):
    rows, width = tok.shape
    part, columns = wada.shape
    wide = gdn.shape[0]
    S, V = jax.ShapeDtypeStruct, pltpu.VMEM
    vm, hbm = pl.BlockSpec(memory_space=pltpu.VMEM), pl.BlockSpec(memory_space=pl.ANY)
    dma = pltpu.SemaphoreType.DMA
    shapes = (
        S((rows, width), BF16), S((rows, width), F32), S((12, part, width), BF16), S((8, 32, columns // 2), BF16),
        S((8, 8, part), F32), S((4, 64, part), BF16), S((8, width), F32), S((1, wide), F32),
    )
    return pl.pallas_call(
        back_kernel,
        out_shape=shapes,
        in_specs=[pl.BlockSpec(memory_space=pltpu.SMEM)] + [vm] * 6 + [hbm] * 12,
        out_specs=(vm,) * len(shapes),
        scratch_shapes=[
            V((rows, width), BF16), V((rows, 3 * width), BF16), V((H, rows, rows), BF16), V((rows, width), BF16), V((8, part, width), BF16),
            V((8, part, wide), BF16), V((4, rows, width), BF16), V((12, part, width), BF16), V((12, lead(part), width), BF16),
            V((rows, width), F32), V((rows, width), BF16), V((rows, width), BF16), V((rows, 3 * width), BF16),
            V((4, 8, part, width), BF16), V((4, 4, part, width), BF16), V((4, lead(part), width), BF16), V((4, part - lead(part), width), BF16),
            V((4, part, width), BF16), V((4, part, width), BF16), V((8, part, width), BF16), V((part, columns), BF16),
            V((8, columns // 2), F32), V((4, 8, width), F32), V((8, 8, width), F32), V((8, 8, part), F32),
            dma((17,)), dma((8,)), dma((8,)), dma((4,)), dma((4,)), dma((5, 12)), dma((5, 12)), dma((4, 4)), dma((4, 4)),
            dma((4, 6)), dma((4, 6)), dma((8,)), dma((8,)), dma((4,)), dma((4,)), dma((4,)), dma((4,)), dma((4,)), dma((4,)),
            dma((8,)), dma((8,)), dma((8,)), dma((8,)),
        ],
        compiler_params=pltpu.CompilerParams(collective_id=2, has_side_effects=True, vmem_limit_bytes=61 << 20),
    )(sizes, tok, cot, mod, mid, gbup, pick, na, proj, probs, att, wo, bra, gnb, bbs, gdn, gup, wq, wada)

def finish_kernel(
    sums_ref, mods_ref, picks_ref, gc_ref, bias_ref, gbup_ref, cond_ref,
    gcond_ref, gada_ref, gbada_ref, gqkv_ref, gbqkv_ref, gout_ref, gbout_ref, gup_ref, gbup_out, gdown_ref, gbdown_ref,
    lanes,
):
    slots, width = cond_ref.shape
    part = width // 8
    half = mods_ref.shape[2]
    me, z = lax.axis_index("fsdp"), lax.axis_index("rep")
    for c in range(4):
        gdown_ref[c * part : (c + 1) * part] = sums_ref[c].astype(F32)
        gup_ref[:, c * width : (c + 1) * width] = sums_ref[4 + c].astype(F32)
    gout_ref[...] = sums_ref[8].astype(F32)
    for c in range(3):
        gqkv_ref[:, c * width : (c + 1) * width] = sums_ref[9 + c].astype(F32)
    rows = mods_ref[...].reshape(256, half)
    acts = jnp.stack([picks_ref[i] for i in range(4)], axis=0).reshape(4, 8, 8, part)
    acts = jnp.stack([acts[:, f] for f in range(8)], axis=0).reshape(256, part).astype(F32)
    upper = lax.rem(lax.broadcasted_iota(jnp.int32, (256, 1), 0), 8) < slots
    first, second = jnp.where(upper, acts, 0.0).astype(BF16), jnp.where(upper, 0.0, acts).astype(BF16)
    gada_ref[:, :half] = tn(first, rows)
    gada_ref[:, half:] = tn(second, rows)
    floats = rows.astype(F32)
    lanes[...] = jnp.zeros_like(lanes)

    def own(row, size):
        total = row.shape[1]
        lanes[0:1, :total] = row
        return pltpu.roll(lanes[:, :total], lax.rem(total - me * size, total), 1)[0, :size]

    column = jnp.concatenate(
        [
            jnp.sum(jnp.where(upper, floats, 0.0), axis=0, keepdims=True),
            jnp.sum(jnp.where(upper, 0.0, floats), axis=0, keepdims=True),
        ],
        axis=1,
    )
    gbada_ref[...] = own(column, gbada_ref.shape[0])
    gbqkv_ref[...] = own(jnp.concatenate([bias_ref[0:1], bias_ref[1:2]], axis=1), gbqkv_ref.shape[0])
    gbout_ref[...] = own(bias_ref[2:3], part)
    gbdown_ref[...] = own(bias_ref[3:4], part)
    wide, hid = gbup_ref.shape[1], gbup_out.shape[0]
    lanes[0:1, :wide] = gbup_ref[...]
    gbup_out[...] = pltpu.roll(lanes[:, :wide], lax.rem(wide - lax.rem(me, 2) * (wide - hid), wide), 1)[0, :hid]
    grad = None
    for j in range(8):
        lanes[:, :width] = jnp.zeros((8, width), F32)
        lanes[0:slots, :part] = gc_ref[j, 0:slots] + gc_ref[j, slots : 2 * slots]
        term = pltpu.roll(lanes[:, :width], j * part, 1) if j else lanes[:, :width]
        grad = term if grad is None else grad + term
    cond = cond_ref[...].astype(F32)
    gate = jax.nn.sigmoid(cond)
    gcond_ref[...] = grad[0:slots] * (gate * (1.0 + cond * (1.0 - gate)))


def finish(sums, mods, picks, gc, bias, gbup, cond, sizes):
    S = jax.ShapeDtypeStruct
    vm = pl.BlockSpec(memory_space=pltpu.VMEM)
    return pl.pallas_call(
        finish_kernel,
        out_shape=tuple(S(size, F32) for size in sizes),
        in_specs=[vm] * 7,
        out_specs=(vm,) * len(sizes),
        scratch_shapes=[pltpu.VMEM((8, 2 * mods.shape[2]), F32)],
        compiler_params=pltpu.CompilerParams(vmem_limit_bytes=56 << 20),
    )(sums, mods, picks, gc, bias, gbup, cond)

def fast(tokens, cond, image_sizes, w_ada, b_ada, w_qkv, b_qkv, w_out, b_out, w_up, b_up, w_down, b_down, cotangent):
    width = tokens.shape[1]
    part, columns = w_ada.shape
    mod, gnb, gbup, pick, na, proj, probs, att, bra, mid, wq, wo, bbs, gdn, gup = front(
        image_sizes, tokens, cotangent, cond, w_ada, b_ada, b_qkv, b_out, b_down, b_up,
        w_qkv, w_out, w_up, w_down,
    )
    wq, wo = wq.reshape(8, 3 * part, width), wo.reshape(8, part, width)
    output, grad_input, sums, mods, gc, picks, bias, gbup = backward(
        image_sizes, tokens, cotangent, mod, mid, gbup, pick, na, proj, probs, att, wo, bra, gnb, bbs, gdn, gup, wq, w_ada
    )
    sizes = tuple(
        leaf.shape for leaf in (cond, w_ada, b_ada, w_qkv, b_qkv, w_out, b_out, w_up, b_up, w_down, b_down)
    )
    return (output, grad_input, *finish(sums, mods, picks, gc, bias, gbup, cond, sizes))


def solution(mesh):
    placed = (
        P(("fsdp", "rep"), None),
        P(("fsdp", "rep"), None),
        P(("fsdp", "rep")),
        P("fsdp", None),
        P("fsdp"),
        P("fsdp", None),
        P("fsdp"),
        P("fsdp", None),
        P("fsdp"),
        P("fsdp", None),
        P("fsdp"),
        P("fsdp", None),
        P("fsdp"),
        P(("fsdp", "rep"), None),
    )
    fits = mesh.shape["fsdp"] == 8 and mesh.shape["rep"] == 4
    return jax.shard_map(
        fast if fits else local,
        mesh=mesh,
        in_specs=placed,
        out_specs=(
            P(("fsdp", "rep"), None),
            P(("fsdp", "rep"), None),
            P(("fsdp", "rep"), None),
            P("fsdp", None),
            P("fsdp"),
            P("fsdp", None),
            P("fsdp"),
            P("fsdp", None),
            P("fsdp"),
            P("fsdp", None),
            P("fsdp"),
            P("fsdp", None),
            P("fsdp"),
        ),
        check_vma=False,
    )
```

```python
import functools

import jax
import jax.numpy as jnp
from jax import lax
from jax.experimental import pallas as pl
from jax.experimental.pallas import tpu as pltpu
from jax.sharding import PartitionSpec as P

H = 16
EPSILON = 1e-06
HIGHEST = lax.Precision.HIGHEST
MASKED = -1e30


def layer_norm(inputs):
    average = jnp.mean(inputs, axis=-1, keepdims=True)
    centered = inputs - average
    variance = jnp.mean(centered * centered, axis=-1, keepdims=True)
    return centered * lax.rsqrt(variance + EPSILON)


def modulate(hidden, shift_part, scale_part):
    return layer_norm(hidden) * (1.0 + scale_part) + shift_part


def gelu_tanh(inputs):
    return jax.nn.gelu(inputs, approximate=True)


def product(first_operand, second_operand):
    return jnp.dot(first_operand, second_operand, preferred_element_type=jnp.float32)


def product_back(first_operand, second_operand):
    return lax.dot_general(
        first_operand, second_operand, (((1,), (1,)), ((), ())), preferred_element_type=jnp.float32
    )


def outer_sum(first_operand, second_operand):
    return lax.dot_general(
        first_operand, second_operand, (((0,), (0,)), ((), ())), preferred_element_type=jnp.float32
    )


def fetch_forward(weight, bias_piece):
    return (
        lax.all_gather(weight, "fsdp", axis=0, tiled=True),
        lax.all_gather(bias_piece, "fsdp", axis=0, tiled=True),
    )


def weights_again(weight):
    return lax.all_gather(weight, "fsdp", axis=0, tiled=True)


def reduce_grads(weight_grad, bias_grad):
    row_part, bias_part = (
        lax.psum_scatter(weight_grad, "fsdp", scatter_dimension=0, tiled=True),
        lax.psum_scatter(bias_grad, "fsdp", scatter_dimension=0, tiled=True),
    )
    column_part = lax.psum_scatter(row_part, "rep", scatter_dimension=1, tiled=True)
    whole_rows, bias_stack = (
        lax.all_gather(column_part, "rep", axis=1, tiled=True),
        lax.all_gather(bias_part[None], "rep", axis=0, tiled=True),
    )
    return (whole_rows, jnp.sum(bias_stack, axis=0))


def local(
    tokens,
    cond,
    image_sizes,
    w_ada,
    b_ada,
    w_qkv,
    b_qkv,
    w_out,
    b_out,
    w_up,
    b_up,
    w_down,
    b_down,
    cotangent,
):
    row_count, model_width = tokens.shape
    head_count = H
    head_dim = model_width // head_count
    slot_count = image_sizes.shape[0]
    scale_factor = head_dim ** (-0.5)
    block_rows = min(512, row_count)
    block_count = row_count // block_rows
    image_ends = jnp.sum(
        jnp.where(jnp.arange(slot_count)[:, None] >= jnp.arange(slot_count)[None, :], image_sizes[None, :], 0), axis=1
    )
    positions = jnp.arange(row_count, dtype=jnp.int32)
    image_ids = jnp.sum((positions[:, None] >= image_ends[None, :]).astype(jnp.int32), axis=1)
    selector = (image_ids[:, None] == jnp.arange(slot_count, dtype=jnp.int32)[None, :]).astype(
        jnp.float32
    )
    cond_float = cond.astype(jnp.float32)
    activ_float, silu_pull = jax.vjp(jax.nn.silu, cond_float)
    activ_low = activ_float.astype(jnp.bfloat16)
    full_ada, full_bada = fetch_forward(w_ada, b_ada)
    modulation = product(activ_low, full_ada) + full_bada.astype(jnp.float32)
    per_token = jnp.dot(selector, modulation, precision=HIGHEST)
    shift_a, scale_a, gate_a, shift_b, scale_b, gate_b = jnp.split(per_token, 6, axis=1)
    hidden = tokens.astype(jnp.float32)
    normed_a, pull_a = jax.vjp(modulate, hidden, shift_a, scale_a)
    normed_a_low = normed_a.astype(jnp.bfloat16)
    full_qkv, full_bqkv = fetch_forward(w_qkv, b_qkv)
    bias_qkv = full_bqkv.astype(jnp.float32)
    bias_full = jnp.concatenate(
        [bias_qkv[:model_width], jnp.zeros((model_width,), jnp.float32), bias_qkv[model_width:]]
    )
    projected = (product(normed_a_low, full_qkv) + bias_full).astype(jnp.bfloat16)
    query_heads = projected[:, :model_width].reshape(row_count, head_count, head_dim)
    key_heads = projected[:, model_width : 2 * model_width].reshape(row_count, head_count, head_dim)
    value_heads = projected[:, 2 * model_width :].reshape(row_count, head_count, head_dim)
    query_blocks = query_heads.reshape(block_count, block_rows, head_count, head_dim)
    id_blocks = image_ids.reshape(block_count, block_rows)

    def scores_of(query_block, id_block):
        raw_scores = (
            jnp.einsum("qhd,khd->hqk", query_block, key_heads, preferred_element_type=jnp.float32)
            * scale_factor
        )
        same_image = id_block[:, None] == image_ids[None, :]
        return jnp.where(same_image[None], raw_scores, MASKED)

    def forward_block(block_item):
        query_block, id_block = block_item
        scores = scores_of(query_block, id_block)
        row_max = jnp.max(scores, axis=-1, keepdims=True)
        exponent = jnp.exp(scores - row_max)
        row_total = jnp.sum(exponent, axis=-1, keepdims=True)
        probabilities = (exponent / row_total).astype(jnp.bfloat16)
        attended_block = jnp.einsum(
            "hqk,khd->qhd", probabilities, value_heads, preferred_element_type=jnp.float32
        )
        return (attended_block.astype(jnp.bfloat16), (row_max + jnp.log(row_total))[:, :, 0])

    attended_blocks, lse_blocks = lax.map(forward_block, (query_blocks, id_blocks))
    attended = attended_blocks.reshape(row_count, model_width)
    full_out, full_bout = fetch_forward(w_out, b_out)
    branch_a = product(attended, full_out) + full_bout.astype(jnp.float32)
    middle = hidden + gate_a * branch_a
    normed_b, pull_b = jax.vjp(modulate, middle, shift_b, scale_b)
    normed_b_low = normed_b.astype(jnp.bfloat16)
    full_up, full_bup = fetch_forward(w_up, b_up)
    inner_pre = product(normed_b_low, full_up) + full_bup.astype(jnp.float32)
    activated, gelu_pull = jax.vjp(gelu_tanh, inner_pre)
    activated_low = activated.astype(jnp.bfloat16)
    full_down, full_bdown = fetch_forward(w_down, b_down)
    branch_b = product(activated_low, full_down) + full_bdown.astype(jnp.float32)
    output = (middle + gate_b * branch_b).astype(jnp.bfloat16)
    grad_out = cotangent.astype(jnp.float32)
    grad_gate_b = grad_out * branch_b
    grad_branch_b = (gate_b * grad_out).astype(jnp.bfloat16)
    grad_w_down, grad_b_down = reduce_grads(
        outer_sum(activated_low, grad_branch_b), jnp.sum(grad_branch_b.astype(jnp.float32), axis=0)
    )
    back_down = weights_again(w_down)
    grad_activated = product_back(grad_branch_b, back_down)
    (grad_inner,) = gelu_pull(grad_activated)
    grad_inner_low = grad_inner.astype(jnp.bfloat16)
    grad_w_up, grad_b_up = reduce_grads(
        outer_sum(normed_b_low, grad_inner_low), jnp.sum(grad_inner_low.astype(jnp.float32), axis=0)
    )
    back_up = weights_again(w_up)
    grad_normed_b = product_back(grad_inner_low, back_up)
    grad_middle_norm, grad_shift_b, grad_scale_b = pull_b(grad_normed_b)
    grad_middle = grad_out + grad_middle_norm
    grad_gate_a = grad_middle * branch_a
    grad_branch_a = (gate_a * grad_middle).astype(jnp.bfloat16)
    grad_w_out, grad_b_out = reduce_grads(
        outer_sum(attended, grad_branch_a), jnp.sum(grad_branch_a.astype(jnp.float32), axis=0)
    )
    back_out = weights_again(w_out)
    grad_attended = product_back(grad_branch_a, back_out).astype(jnp.bfloat16)
    grad_att_blocks = grad_attended.reshape(block_count, block_rows, head_count, head_dim)

    def backward_block(carried, block_item):
        key_grad, value_grad = carried
        query_block, id_block, grad_block, lse_block = block_item
        scores = scores_of(query_block, id_block)
        probabilities = jnp.exp(scores - lse_block[:, :, None])
        probabilities_low = probabilities.astype(jnp.bfloat16)
        grad_probs = jnp.einsum(
            "qhd,khd->hqk", grad_block, value_heads, preferred_element_type=jnp.float32
        )
        row_delta = jnp.sum(probabilities * grad_probs, axis=-1, keepdims=True)
        grad_scores = (probabilities * (grad_probs - row_delta)).astype(jnp.bfloat16)
        query_grad = (
            jnp.einsum("hqk,khd->qhd", grad_scores, key_heads, preferred_element_type=jnp.float32)
            * scale_factor
        )
        key_grad = (
            key_grad
            + jnp.einsum(
                "hqk,qhd->khd", grad_scores, query_block, preferred_element_type=jnp.float32
            )
            * scale_factor
        )
        value_grad = value_grad + jnp.einsum(
            "hqk,qhd->khd", probabilities_low, grad_block, preferred_element_type=jnp.float32
        )
        return ((key_grad, value_grad), query_grad)

    zero_heads = jnp.zeros((row_count, head_count, head_dim), jnp.float32)
    (grad_keys, grad_values), grad_query_blocks = lax.scan(
        backward_block,
        (zero_heads, zero_heads),
        (query_blocks, id_blocks, grad_att_blocks, lse_blocks),
    )
    grad_projected = jnp.concatenate(
        [
            grad_query_blocks.reshape(row_count, model_width),
            grad_keys.reshape(row_count, model_width),
            grad_values.reshape(row_count, model_width),
        ],
        axis=1,
    ).astype(jnp.bfloat16)
    column_sums = jnp.sum(grad_projected.astype(jnp.float32), axis=0)
    grad_bias_qkv = jnp.concatenate([column_sums[:model_width], column_sums[2 * model_width :]])
    grad_w_qkv, grad_b_qkv = reduce_grads(outer_sum(normed_a_low, grad_projected), grad_bias_qkv)
    back_qkv = weights_again(w_qkv)
    grad_normed_a = product_back(grad_projected, back_qkv)
    grad_hidden_norm, grad_shift_a, grad_scale_a = pull_a(grad_normed_a)
    grad_input = grad_middle + grad_hidden_norm
    grad_per_token = jnp.concatenate(
        [grad_shift_a, grad_scale_a, grad_gate_a, grad_shift_b, grad_scale_b, grad_gate_b], axis=1
    )
    grad_modulation = lax.dot_general(
        selector, grad_per_token, (((0,), (0,)), ((), ())), precision=HIGHEST
    ).astype(jnp.bfloat16)
    grad_w_ada, grad_b_ada = reduce_grads(
        outer_sum(activ_low, grad_modulation), jnp.sum(grad_modulation.astype(jnp.float32), axis=0)
    )
    back_ada = weights_again(w_ada)
    grad_activ = product_back(grad_modulation, back_ada)
    (grad_cond,) = silu_pull(grad_activ)
    return (
        output,
        grad_input,
        grad_cond,
        grad_w_ada,
        grad_b_ada,
        grad_w_qkv,
        grad_b_qkv,
        grad_w_out,
        grad_b_out,
        grad_w_up,
        grad_b_up,
        grad_w_down,
        grad_b_down,
    )


MESH = pl.DeviceIdType.MESH
F32, BF16 = jnp.float32, jnp.bfloat16


def flipped(offset):
    index = lax.axis_index("fsdp")
    y, x, core = index // 4, (index // 2) % 2, index % 2
    y = 1 - y if offset & 4 else y
    x = 1 - x if offset & 2 else x
    core = 1 - core if offset & 1 else core
    return y * 4 + x * 2 + core


def greet(offsets):
    barrier = pltpu.get_barrier_semaphore()
    for offset in offsets:
        pl.semaphore_signal(barrier, inc=1, device_id={"fsdp": flipped(offset)}, device_id_type=MESH)
    pl.semaphore_wait(barrier, len(offsets))


def remote(src, dst, send, recv, offset):
    return pltpu.make_async_remote_copy(
        src_ref=src, dst_ref=dst, send_sem=send, recv_sem=recv,
        device_id={"fsdp": flipped(offset)}, device_id_type=MESH,
    )


def lead(rows):
    return -(-rows // 32) * 16


class Gather:
    def __init__(self, shard, rows, send, recv, lead):
        first, second = pl.ds(0, lead), pl.ds(lead, rows - lead)
        piece = {e: shard(flipped(e)) for e in (0, 2, 4, 6)}
        plan = (
            (piece[0], 1), (piece[0], 2), (piece[0], 4),
            (piece[2].at[first], 4), (piece[4].at[second], 2),
            (piece[2], 1), (piece[4], 1), (piece[6], 1),
        )
        self.copies = [remote(ref, ref, send.at[i], recv.at[i], e) for i, (ref, e) in enumerate(plan)]

    def own(self):
        for i in (1, 2, 0):
            self.copies[i].start()

    def along(self):
        self.copies[1].wait_recv()
        self.copies[3].start()
        self.copies[5].start()
        self.copies[2].wait_recv()
        self.copies[4].start()
        self.copies[6].start()

    def across(self):
        self.copies[3].wait_recv()
        self.copies[4].wait_recv()
        self.copies[7].start()

    def sibling(self, p):
        self.copies[(0, 5, 6, 7)[p]].wait_recv()

    def finish(self):
        for p in range(4):
            self.sibling(p)

    def drain(self):
        for copy in self.copies:
            copy.wait_send()


class PlaneSum:
    def __init__(self, held, odd, pair_in, cross_a, cross_b, from_x, from_y, pair_send, pair_recv, send, recv, rows, lead):
        self.a, self.b = a, b = pl.ds(0, lead), pl.ds(lead, rows - lead)
        self.held, self.pair_in, self.cross_a, self.cross_b = held, pair_in, cross_a, cross_b
        self.from_x, self.from_y = from_x, from_y
        self.pairs = [] if odd is None else [
            remote(odd[p], pair_in[p], pair_send.at[p], pair_recv.at[p], 1) for p in range(4)
        ]
        plan = (
            (held[3].at[a], cross_a, 2), (held[3].at[b], cross_b, 4),
            (held[2].at[b], from_y.at[b], 4), (held[1].at[a], from_x.at[a], 2),
            (held[2].at[a], from_y.at[a], 4), (held[1].at[b], from_x.at[b], 2),
        )
        self.copies = [remote(src, dst, send.at[i], recv.at[i], e) for i, (src, dst, e) in enumerate(plan)]

    def pair(self):
        for p in (3, 2, 1, 0):
            self.pairs[p].start()

    def leave(self, p):
        if p == 3:
            self.copies[0].start()
            self.copies[1].start()
        elif p:
            self.copies[(None, 3, 2)[p]].start()

    def join(self, p):
        self.pairs[p].wait_recv()
        self.held[p][...] += self.pair_in[p][...]
        self.leave(p)

    def combine(self):
        for p in (3, 2, 1, 0):
            self.join(p)

    def relay(self):
        for i, p, part, came in ((0, 2, self.a, self.cross_a), (1, 1, self.b, self.cross_b)):
            self.copies[i].wait_recv()
            ref = self.held[p].at[part]
            ref[...] += came[...]
            self.copies[4 + i].start()

    def total(self):
        for i in (2, 3, 4, 5):
            self.copies[i].wait_recv()
        return self.held[0][...].astype(F32) + self.from_x[...].astype(F32) + self.from_y[...].astype(F32)

    def drain(self):
        for copy in self.pairs + self.copies:
            copy.wait_send()


def nt(a, b):
    return lax.dot_general(a, b, (((1,), (1,)), ((), ())), preferred_element_type=F32)


def tn(a, b):
    return lax.dot_general(a, b, (((0,), (0,)), ((), ())), preferred_element_type=F32)


def nn(a, b):
    return jnp.dot(a, b, preferred_element_type=F32)


def normalized(values):
    centered = values - jnp.mean(values, axis=-1, keepdims=True)
    variance = jnp.mean(centered * centered, axis=-1, keepdims=True)
    scale = lax.rsqrt(variance + EPSILON)
    return centered * scale, scale


def image_of(place, sizes_ref):
    end = jnp.int32(0)
    image = jnp.zeros(place.shape, jnp.int32)
    for j in range(sizes_ref.shape[0]):
        end = end + sizes_ref[j]
        image = image + (place >= end).astype(jnp.int32)
    return image


def per_row(selectors, modulation, part, width):
    total = None
    for j, chosen in enumerate(selectors):
        term = chosen * modulation[j : j + 1, part * width : (part + 1) * width]
        total = term if total is None else total + term
    return total


def head_window(head, head_dim):
    low = head * head_dim
    base = low // 128 * 128
    wide = 128 if low - base + head_dim <= 128 else 256
    lane = lax.broadcasted_iota(jnp.int32, (1, wide), 1) + (base - low)
    mask = jnp.where((lane >= 0) & (lane < head_dim), 1.0, 0.0)
    return base, wide, mask


GELU_RATE = 0.7978845608028654
GELU_CUBE = 0.044715


def gelu_parts(u):
    square = u * u
    bend = jnp.tanh(GELU_RATE * u * (1.0 + GELU_CUBE * square))
    half = 0.5 * (1.0 + bend)
    slope = half + 0.5 * u * (1.0 - bend * bend) * (GELU_RATE * (1.0 + 3.0 * GELU_CUBE * square))
    return u * half, slope


def front_kernel(
    sizes_ref, tok_ref, cot_ref, cond_ref, wada_ref, bada_ref, bqkv_ref, bout_ref, bdown_ref, bup_in,
    wqkv_hbm, wout_hbm, wup_hbm, wdn_hbm,
    mod_ref, gnb_ref, gbup_ref, pick_ref, na_hbm, proj_hbm, probs_hbm, att_hbm, bra_hbm, mid_hbm, wq_hbm, wo_hbm,
    bb_hbm, gdn_hbm, gup_hbm,
    na_ref, proj_ref, probs_ref, att_ref, bra_ref, mid_ref, arena, wo_all, bb_ref, gdn_ref, gup_ref,
    cond_all, pm, mpair, mfar, lay, lay_b, nb_all, gbb_all, wup_all, wdn_ref, act_all, gi_all, in_pair, cross_a, cross_b, from_x, from_y,
    loc_sem, save_sem, c_send, c_recv, mp_send, mp_recv, mf_send, mf_recv, up_send, up_recv,
    q_send, q_recv, o_send, o_recv, g_send, g_recv, n_send, n_recv, pr_send, pr_recv, far_send, far_recv,
):
    rows, width = tok_ref.shape
    head_dim = width // H
    slots = sizes_ref.shape[0]
    part = wada_ref.shape[0]
    own, wide = wdn_hbm.shape[0], wup_all.shape[1]
    me = flipped(0)
    others = range(1, 8)

    def strip(ref, size):
        return lambda j: ref.at[pl.ds(pl.multiple_of(j * size, 8), size)]

    def up_piece(e):
        j = flipped(e)
        begin = pl.multiple_of(2 * own * (j // 2) + (2 * own - wide) * (j % 2), 128)
        return wup_hbm.at[:, pl.ds(begin, wide)]

    shift = lax.rem(me, 2) * (wide - own)
    blank = lax.rem(me + 1, 2) * own
    wq_strip, wup_strip = strip(arena, 3 * part), strip(wup_all, part)
    sources = [
        (wqkv_hbm.at[:, pl.ds(i * width, width)], arena.at[pl.ds(pl.multiple_of(me * 3 * part + i * part, 8), part)]) for i in range(3)
    ] + [
        (wout_hbm, strip(wo_all, part)(me)), (up_piece(0), wup_strip(me)),
        (wdn_hbm, wdn_ref.at[pl.ds(pl.multiple_of(shift, 8), own)]),
    ]
    local = [pltpu.make_async_copy(src, dst, loc_sem.at[i]) for i, (src, dst) in enumerate(sources)]
    for copy in local:
        copy.start()
    saves = [
        pltpu.make_async_copy(src, dst, save_sem.at[i])
        for i, (src, dst) in enumerate((
            (na_ref, na_hbm), (proj_ref, proj_hbm), (probs_ref, probs_hbm), (att_ref, att_hbm),
            (bra_ref, bra_hbm), (mid_ref, mid_hbm), (arena, wq_hbm), (wo_all, wo_hbm),
            (bb_ref, bb_hbm), (gdn_ref, gdn_hbm), (gup_ref, gup_hbm),
        ))
    ]
    act = jax.nn.silu(cond_ref[...].astype(F32))
    cond_all[me, :slots] = act
    cond_all[me, slots:] = act
    qkv = Gather(wq_strip, 3 * part, q_send, q_recv, lead(3 * part))
    out = Gather(strip(wo_all, part), part, o_send, o_recv, lead(part))
    gbb = Gather(lambda j: gbb_all.at[j], rows, g_send, g_recv, rows // 2)
    nb = Gather(lambda j: nb_all.at[j], rows, n_send, n_recv, rows // 2)
    conds = [remote(cond_all.at[me], cond_all.at[me], c_send.at[e], c_recv.at[e], e) for e in others]
    ups = [remote(up_piece(e), wup_strip(me), up_send.at[e], up_recv.at[e], e) for e in others]
    pairs = [remote(pm.at[flipped(2 * p + 1)], mpair.at[p], mp_send.at[p], mp_recv.at[p], 1) for p in range(4)]
    fars = [remote(pm.at[flipped(2 * p)], mfar.at[p], mf_send.at[p], mf_recv.at[p], 2 * p) for p in range(1, 4)]
    block = [arena.at[pl.ds(i * rows, rows)] for i in range(12)]
    gnb = PlaneSum(
        block[8:], block[:4], [in_pair.at[p] for p in range(4)], cross_a, cross_b, from_x, from_y,
        pr_send, pr_recv, far_send, far_recv, rows, rows // 2,
    )
    bb_pairs = [remote(block[4 + p], in_pair.at[4 + p], pr_send.at[4 + p], pr_recv.at[4 + p], 1) for p in range(4)]

    greet(others)
    for copy in conds:
        copy.start()
    for copy in local[:3]:
        copy.wait()
    qkv.own()
    lay[...] = jnp.zeros_like(lay)
    lay_b[...] = jnp.zeros_like(lay_b)
    lay[0:1, : bada_ref.shape[0]] = bada_ref[...].astype(F32)[None]
    bada = pltpu.roll(lay[...], me * bada_ref.shape[0], 1)[0:1]
    begin = 0
    for ref in (bqkv_ref, bout_ref, bdown_ref):
        size = ref.shape[0]
        lay_b[0:1, begin : begin + size] = ref[...].astype(F32)[None]
        lay_b[0:1, begin : begin + 8 * size] = pltpu.roll(lay_b[:, begin : begin + 8 * size], me * size, 1)[0:1]
        begin += 8 * size
    for copy in conds:
        copy.wait_recv()
    everyone = cond_all[...].reshape(8 * cond_all.shape[1], width).astype(BF16)
    pick = (
        lax.broadcasted_iota(jnp.int32, (width, part), 0) == lax.broadcasted_iota(jnp.int32, (width, part), 1) + me * part
    )
    chosen = nn(everyone, jnp.where(pick, 1.0, 0.0).astype(BF16)).astype(BF16)
    pick_ref[...] = chosen
    bias_row = lax.broadcasted_iota(jnp.int32, (8, 1), 0) == slots
    piece = nn(chosen, wada_ref[...]).reshape(pm.shape)
    pm[...] = piece + bada[None]
    pm[:, :, : lay_b.shape[1]] = jnp.where(bias_row[None], lay_b[0:1][None], pm[:, :, : lay_b.shape[1]])
    for copy in pairs:
        copy.start()
    for p in (3, 2, 1, 0):
        pairs[p].wait_recv()
        pm[flipped(2 * p)] += mpair[p]
        if p:
            fars[p - 1].start()
    qkv.along()
    local[3].wait()
    out.own()
    lay[...] = jnp.zeros_like(lay)
    lay[0:1, :own] = bup_in[...].astype(F32)[None]
    bup = pltpu.roll(lay[:, :wide], shift, 1)[0:1]
    wdn_ref[pl.ds(pl.multiple_of(blank, 8), wide - own)] = jnp.zeros((wide - own, width), BF16)
    for copy in fars:
        copy.wait_recv()
    modulation = pm[me] + (mfar[1] + mfar[2] + mfar[3])
    mod_ref[...] = modulation
    bias = modulation[slots : slots + 1]
    image = image_of(lax.broadcasted_iota(jnp.int32, (rows, 1), 0), sizes_ref)
    selectors = [jnp.where(image == j, 1.0, 0.0) for j in range(slots)]
    gbb_all[me] = (per_row(selectors, mod_ref, 5, width) * cot_ref[...].astype(F32)).astype(BF16)
    gbb.own()
    hidden = tok_ref[...].astype(F32)
    na_ref[...] = (
        normalized(hidden)[0] * (1.0 + per_row(selectors, mod_ref, 1, width)) + per_row(selectors, mod_ref, 0, width)
    ).astype(BF16)
    saves[0].start()
    qkv.across()
    qkv.finish()
    saves[6].start()
    for i in range(3):
        strips = [arena[3 * part * j + i * part : 3 * part * j + (i + 1) * part] for j in range(8)]
        value = nn(na_ref[...], jnp.concatenate(strips, axis=0))
        if i == 0:
            value = value + bias[:, :width]
        if i == 2:
            value = value + bias[:, width : 2 * width]
        proj_ref[:, i * width : (i + 1) * width] = value.astype(BF16)
    saves[1].start()
    out.along()
    for copy in ups:
        copy.start()
    att_ref[...] = jnp.zeros_like(att_ref)
    row_image = image_of(lax.broadcasted_iota(jnp.int32, (rows, rows), 0), sizes_ref)
    column_image = image_of(lax.broadcasted_iota(jnp.int32, (rows, rows), 1), sizes_ref)
    hidden_pairs = jnp.where(row_image == column_image, 0.0, -1e30)
    for head in range(H):
        base, window, mask = head_window(head, head_dim)
        mask = mask.astype(BF16)
        query = proj_ref[:, base : base + window] * mask
        key = proj_ref[:, width + base : width + base + window]
        value = proj_ref[:, 2 * width + base : 2 * width + base + window] * mask
        scores = nt(query, key) * head_dim ** (-0.5) + hidden_pairs
        exponent = jnp.exp(scores - jnp.max(scores, axis=-1, keepdims=True))
        probs = (exponent * (1.0 / jnp.sum(exponent, axis=-1, keepdims=True))).astype(BF16)
        probs_ref[head] = probs
        att_ref[:, base : base + window] += nn(probs, value).astype(BF16)
        if head == 5:
            out.across()
    saves[2].start()
    saves[3].start()
    gbb.along()
    out.finish()
    saves[7].start()
    branch = nn(att_ref[...], wo_all[...]) + bias[:, 2 * width : 3 * width]
    bra_ref[...] = branch
    middle = tok_ref[...].astype(F32) + per_row(selectors, mod_ref, 2, width) * branch
    mid_ref[...] = middle
    nb_all[me] = (
        normalized(middle)[0] * (1.0 + per_row(selectors, mod_ref, 4, width)) + per_row(selectors, mod_ref, 3, width)
    ).astype(BF16)
    nb.own()
    saves[4].start()
    saves[5].start()

    qkv.drain()
    saves[6].wait()
    local[4].wait()
    local[5].wait()
    for copy in ups:
        copy.wait_recv()
    gbb.across()

    def one(slot):
        inner = nn(nb_all[slot], wup_all[...]) + bup
        act, slope = gelu_parts(inner)
        act_all[slot] = act.astype(BF16)
        gi_all[slot] = (slope * nt(gbb_all[slot], wdn_ref[...])).astype(BF16)

    for p in range(4):
        even, odd = flipped(2 * p), flipped(2 * p + 1)
        if p == 1:
            nb.along()
        if p == 3:
            nb.across()
        one(even)
        block[8 + p][...] = nt(gi_all[even], wup_all[...]).astype(BF16)
        gbb.sibling(p)
        nb.sibling(p)
        one(odd)
        block[p][...] = nt(gi_all[odd], wup_all[...]).astype(BF16)
        gnb.pairs[p].start()
        gnb.join(p)

    def forth(p):
        even, odd = flipped(2 * p), flipped(2 * p + 1)
        block[4 + p][...] = nn(act_all[odd], wdn_ref[...]).astype(BF16)
        bb_pairs[p].start()
        bb_ref[p] = nn(act_all[even], wdn_ref[...]).astype(BF16)

    forth(0)
    forth(1)
    forth(2)
    forth(3)
    gnb.relay()
    gdn_ref[...] = tn(act_all[...].reshape(8 * rows, wide), gbb_all[...].reshape(8 * rows, width)).astype(BF16)
    saves[9].start()
    inner_grads = gi_all[...].reshape(8 * rows, wide)
    gup_ref[...] = tn(nb_all[...].reshape(8 * rows, width), inner_grads).astype(BF16).reshape(gup_ref.shape)
    saves[10].start()
    gbup_ref[...] = jnp.sum(inner_grads.astype(F32), axis=0, keepdims=True)
    for p in range(4):
        bb_pairs[p].wait_recv()
        bb_ref[p] += in_pair[4 + p]
    saves[8].start()
    gnb_ref[...] = gnb.total()
    for copy in conds + pairs + fars + ups + bb_pairs:
        copy.wait_send()
    for gather in (out, gbb, nb, gnb):
        gather.drain()
    for i, copy in enumerate(saves):
        if i != 6:
            copy.wait()


def front(sizes, tok, cot, cond, wada, bada, bqkv, bout, bdown, bup, wqkv, wout, wup, wdn):
    rows, width = tok.shape
    part, columns = wada.shape
    wide = wdn.shape[0] + 64
    S, V = jax.ShapeDtypeStruct, pltpu.VMEM
    vm, hbm = pl.BlockSpec(memory_space=pltpu.VMEM), pl.BlockSpec(memory_space=pl.ANY)
    dma = pltpu.SemaphoreType.DMA
    kept = (
        ((rows, width), BF16), ((rows, 3 * width), BF16), ((H, rows, rows), BF16), ((rows, width), BF16),
        ((rows, width), F32), ((rows, width), F32), ((24 * part, width), BF16), ((8 * part, width), BF16),
        ((4, rows, width), BF16), ((wide, width), BF16), ((8, part, wide), BF16),
    )
    shapes = (S((8, columns), F32), S((rows, width), F32), S((1, wide), F32), S((64, part), BF16)) + tuple(S(*pair) for pair in kept)
    return pl.pallas_call(
        front_kernel,
        out_shape=shapes,
        in_specs=[pl.BlockSpec(memory_space=pltpu.SMEM)] + [vm] * 9 + [hbm] * 4,
        out_specs=(vm,) * 4 + (hbm,) * 11,
        scratch_shapes=[V(*pair) for pair in kept] + [
            V((8, 8, width), F32), V((8, 8, columns), F32), V((4, 8, columns), F32),
            V((4, 8, columns), F32), V((8, columns), F32), V((8, 4 * width), F32),
            V((8, rows, width), BF16), V((8, rows, width), BF16), V((8 * part, wide), BF16), V((wide, width), BF16),
            V((8, rows, wide), BF16), V((8, rows, wide), BF16), V((8, rows, width), BF16),
            V((rows // 2, width), BF16), V((rows // 2, width), BF16), V((rows, width), BF16), V((rows, width), BF16),
            dma((6,)), dma((11,)), dma((8,)), dma((8,)), dma((4,)), dma((4,)), dma((4,)), dma((4,)),
        ] + [dma((8,))] * 14,
        compiler_params=pltpu.CompilerParams(collective_id=0, has_side_effects=True, vmem_limit_bytes=61 << 20),
    )(sizes, tok, cot, cond, wada, bada, bqkv, bout, bdown, bup, wqkv, wout, wup, wdn)

def along(step):
    return lax.rem(lax.axis_index("rep") + step, 4)


def remote_z(src, dst, send, recv, z):
    return pltpu.make_async_remote_copy(
        src_ref=src, dst_ref=dst, send_sem=send, recv_sem=recv, device_id={"rep": z}, device_id_type=MESH
    )


DEPTH = 4


class LineSum:
    def __init__(self, chunks, held, halves, send, recv, lead):
        self.chunks, self.held, self.halves, self.send, self.recv = chunks, held, halves, send, recv
        rows = chunks.shape[1]
        self.parts = (pl.ds(0, lead), pl.ds(lead, rows - lead))
        self.sizes = (lead, rows - lead)

    def on(self, roles, action):
        z = lax.axis_index("rep")
        for role in roles:
            pl.when(z == role)(functools.partial(action, role))

    def enter(self, c, role):
        mate = (1, 0, 3, 2)[role]
        return remote_z(self.chunks.at[c], self.held.at[c], self.send.at[0, c], self.recv.at[0, c], mate)

    def give(self, c, role):
        half = 2 - role
        space = self.halves.at[c, pl.ds(0, self.sizes[half])]
        return remote_z(self.chunks.at[c, self.parts[half]], space, self.send.at[1, c], self.recv.at[1, c], 3 - role)

    def result(self, c, half, kind, target):
        ref = self.held.at[c, self.parts[half]]
        return remote_z(ref, ref, self.send.at[kind, c], self.recv.at[kind, c], target)

    def begin(self, c):
        def action(role):
            if c >= DEPTH:
                self.enter(c - DEPTH, role).wait_send()
            self.enter(c, role).start()

        self.on((0, 3), action)

    def first(self, c):
        def action(role):
            self.enter(c, role).wait_recv()
            self.chunks[c] += self.held[c]
            self.give(c, role).start()

        self.on((1, 2), action)

    def second(self, c):
        def action(role):
            mine = role - 1
            self.give(c, 3 - role).wait_recv()
            part, size = self.parts[mine], self.sizes[mine]
            self.held[c, part] = self.chunks[c, part] + self.halves[c, :size]
            self.result(c, mine, 2, 3 - role).start()
            self.result(c, mine, 3, (1, 0, 3, 2)[role]).start()

        self.on((1, 2), action)

    def third(self, c):
        def action(role):
            other = 2 - role
            self.result(c, other, 2, 3 - role).wait_recv()
            self.result(c, other, 4, (1, 0, 3, 2)[role]).start()

        self.on((1, 2), action)

    def tick(self, n):
        count = self.chunks.shape[0]
        for step, c in ((self.first, n), (self.second, n - 1), (self.third, n - 2)):
            if 0 <= c < count:
                step(c)

    def end(self):
        def outer(role):
            near = 0 if role == 0 else 1
            for c in range(self.chunks.shape[0]):
                self.result(c, near, 3, 1).wait_recv()
                self.result(c, 1 - near, 4, 1).wait_recv()
                if c >= self.chunks.shape[0] - DEPTH:
                    self.enter(c, role).wait_send()

        def inner(role):
            for c in range(self.chunks.shape[0]):
                self.give(c, role).wait_send()
                self.result(c, role - 1, 2, 3 - role).wait_send()
                self.result(c, role - 1, 3, 3 - role).wait_send()
                self.result(c, 2 - role, 4, 3 - role).wait_send()

        self.on((0, 3), outer)
        self.on((1, 2), inner)


def norm_back(values, scale_part, grad):
    normal, rate = normalized(values)
    inner = grad * (1.0 + scale_part)
    back = rate * (
        inner - jnp.mean(inner, axis=-1, keepdims=True) - normal * jnp.mean(inner * normal, axis=-1, keepdims=True)
    )
    return back, grad * normal


def back_kernel(
    sizes_ref, tok_ref, cot_ref, mod_ref, mid_ref, gbup_ref, pick_ref, na_hbm, proj_hbm, probs_hbm, att_hbm, wo_hbm,
    bra_hbm, gnb_hbm, bbs_hbm, gdn_hbm, gup_hbm, wq_hbm, wada_hbm,
    out_ref, gin_ref, sums, mods, gc_in, picks, bias_ref, gbup_out,
    na_ref, proj_ref, probs_ref, att_ref, wo_all,
    gup_in, bb_in, bb_cross, bb_from, zbuf, zhalf, gm_ref, gba_ref, gatt_ref, gp_ref, blocks, pair_in, cross_a, cross_b, from_x, from_y,
    wq_buf, wada_ref, modrow, bias_z, bias_in, gc_out,
    loc_sem, up_send, up_recv, bb_send, bb_recv, z_send, z_recv, ps_send, ps_recv, pc_send, pc_recv,
    md_send, md_recv, mz_send, mz_recv, pk_send, pk_recv, bz_send, bz_recv, bi_send, bi_recv, gc_send, gc_recv,
):
    rows, width = tok_ref.shape
    head_dim = width // H
    slots = sizes_ref.shape[0]
    part = width // 8
    hid = 8 * part // 2
    me, z = flipped(0), lax.axis_index("rep")
    core = lax.rem(me, 2)
    others, steps = range(1, 8), range(1, 4)

    line = LineSum(zbuf, sums, zhalf, z_send, z_recv, lead(part))
    planes = [
        PlaneSum(
            [blocks.at[i, flipped(2 * p)] for p in range(4)], [blocks.at[i, flipped(2 * p + 1)] for p in range(4)],
            [pair_in.at[i, p] for p in range(4)], cross_a.at[i], cross_b.at[i], from_x.at[i], from_y.at[i],
            ps_send.at[i], ps_recv.at[i], pc_send.at[i], pc_recv.at[i], part, lead(part),
        )
        for i in range(4)
    ]
    ups = [remote(gup_hbm.at[flipped(e)], gup_in.at[me], up_send.at[e], up_recv.at[e], e) for e in others]
    branch_sum = PlaneSum(
        [bb_in.at[p] for p in range(4)], None, None, bb_cross.at[pl.ds(0, rows // 2)], bb_cross.at[pl.ds(rows // 2, rows // 2)],
        bb_from.at[0], bb_from.at[1], None, None, bb_send, bb_recv, rows, rows // 2,
    )
    shift = (gdn_hbm.shape[0] - hid) * core
    local = [pltpu.make_async_copy(gdn_hbm.at[pl.ds(pl.multiple_of(shift + part * c, 16), part)], zbuf.at[c], loc_sem.at[c]) for c in range(4)]
    local.append(pltpu.make_async_copy(gup_hbm.at[me], gup_in.at[me], loc_sem.at[4]))
    local.append(pltpu.make_async_copy(bbs_hbm, bb_in, loc_sem.at[5]))
    local.append(pltpu.make_async_copy(wada_hbm, wada_ref, loc_sem.at[6]))
    loads = [pltpu.make_async_copy(wq_hbm.at[:, pl.ds(i * part, part)], wq_buf, loc_sem.at[7 + i]) for i in range(3)]
    local.append(pltpu.make_async_copy(bra_hbm, gm_ref, loc_sem.at[10]))
    local.append(pltpu.make_async_copy(gnb_hbm, gin_ref, loc_sem.at[11]))
    local += [
        pltpu.make_async_copy(src, dst, loc_sem.at[12 + i])
        for i, (src, dst) in enumerate((
            (wo_hbm, wo_all), (att_hbm, att_ref), (proj_hbm, proj_ref), (probs_hbm, probs_ref), (na_hbm, na_ref),
        ))
    ]
    for i in (7, 8, 0, 1, 9, 10, 2, 3, 5, 11, 12, 4, 13, 6):
        local[i].start()
    loads[0].start()
    picks[z] = pick_ref[...]

    barrier = pltpu.get_barrier_semaphore()
    for e in others:
        pl.semaphore_signal(barrier, inc=1, device_id={"fsdp": flipped(e)}, device_id_type=MESH)
    for s in steps:
        pl.semaphore_signal(barrier, inc=1, device_id={"rep": along(s)}, device_id_type=MESH)
    pl.semaphore_wait(barrier, 10)

    for copy in ups:
        copy.start()
    for c in range(4):
        local[c].wait()
    for c in range(DEPTH):
        line.begin(c)
    local[5].wait()
    for p in (3, 2, 1):
        branch_sum.leave(p)
    send_picks = [remote_z(picks.at[z], picks.at[z], pk_send.at[s], pk_recv.at[s], along(s)) for s in steps]
    for copy in send_picks:
        copy.start()

    image = image_of(lax.broadcasted_iota(jnp.int32, (rows, 1), 0), sizes_ref)
    selectors = [jnp.where(image == j, 1.0, 0.0) for j in range(slots)]
    slot = lax.broadcasted_iota(jnp.int32, (8, rows), 0)
    where = image_of(lax.broadcasted_iota(jnp.int32, (8, rows), 1), sizes_ref)
    gather_rows = (jnp.where((where == slot) & (slot < slots), 1.0, 0.0), jnp.where((where == slot - slots) & (where < slots), 1.0, 0.0))
    modrow[...] = jnp.zeros_like(modrow)

    def to_slots(index, values):
        modrow[:, (index % 3) * width : (index % 3 + 1) * width] += lax.dot_general(
            gather_rows[index // 3], values, (((1,), (0,)), ((), ())), precision=lax.Precision.HIGHEST, preferred_element_type=F32
        )

    cot = cot_ref[...].astype(F32)
    local[7].wait()
    local[8].wait()
    back, grad_scale = norm_back(mid_ref[...], per_row(selectors, mod_ref, 4, width), gin_ref[...])
    to_slots(3, gin_ref[...])
    to_slots(4, grad_scale)
    gm = cot + back
    to_slots(2, gm * gm_ref[...])
    gm_ref[...] = gm
    gba = (per_row(selectors, mod_ref, 2, width) * gm).astype(BF16)
    gba_ref[...] = gba
    bias_z[0] = jnp.zeros(bias_z.shape[1:], F32)
    bias_z[0, 2:3] = jnp.sum(gba.astype(F32), axis=0, keepdims=True)
    gbb = (per_row(selectors, mod_ref, 5, width) * cot).astype(BF16)
    bias_z[0, 3:4] = jnp.sum(gbb.astype(F32), axis=0, keepdims=True)
    bias_z[0, 4:5, : gbup_ref.shape[1]] = gbup_ref[...]
    local[9].wait()
    gatt_ref[...] = nt(gba_ref[...], wo_all[...].reshape(width, width)).astype(BF16)
    local[10].wait()
    blocks[0] = tn(att_ref[...], gba_ref[...]).astype(BF16).reshape(8, part, width)
    planes[0].pair()
    line.tick(0)

    gp_ref[...] = jnp.zeros_like(gp_ref)
    rate = head_dim ** (-0.5)

    def head_back(head):
        base, window, mask = head_window(head, head_dim)
        mask = mask.astype(BF16)
        at = [pl.ds(i * width + base, window) for i in range(3)]
        query, key, value = proj_ref[:, at[0]] * mask, proj_ref[:, at[1]] * mask, proj_ref[:, at[2]]
        grad = gatt_ref[:, at[0]] * mask
        low = probs_ref[head]
        probs = low.astype(F32)
        grad_probs = nt(grad, value)
        delta = jnp.sum(probs * grad_probs, axis=-1, keepdims=True)
        grad_scores = (probs * (grad_probs - delta)).astype(BF16)
        gp_ref[:, at[0]] += (nn(grad_scores, key) * rate).astype(BF16)
        gp_ref[:, at[1]] += (tn(grad_scores, query) * rate).astype(BF16)
        gp_ref[:, at[2]] += tn(low, grad).astype(BF16)

    local[11].wait()
    local[12].wait()
    for head in range(3):
        head_back(head)
    planes[0].combine()
    for head in range(3, 10):
        head_back(head)
    line.tick(1)
    for head in range(10, 16):
        head_back(head)
    local[4].wait()
    for copy in ups:
        copy.wait_recv()
    lap = gup_in.shape[2] - hid
    for c in range(4):
        left, right = gup_in[2 * c], gup_in[2 * c + 1]
        zbuf[4 + c, :, : hid - lap] = left[:, : hid - lap]
        zbuf[4 + c, :, hid - lap : hid + lap] = left[:, hid - lap :] + right[:, : 2 * lap]
        zbuf[4 + c, :, hid + lap :] = right[:, 2 * lap :]
    line.begin(4)
    line.begin(5)
    line.tick(2)

    def spread(i):
        blocks[i] = tn(na_ref[...], gp_ref[:, (i - 1) * width : i * width]).astype(BF16).reshape(8, part, width)
        planes[i].pair()

    def settle(i):
        zbuf[8 + i] = planes[i].total().astype(BF16)
        line.begin(8 + i)

    branch_sum.relay()
    local[13].wait()
    spread(1)
    spread(2)
    spread(3)
    for i in range(3):
        loads[i].wait()
        term = nt(gp_ref[:, i * width : (i + 1) * width], wq_buf[...].reshape(width, width))
        gin_ref[...] = term if i == 0 else gin_ref[...] + term
        if i < 2:
            loads[i + 1].start()
    gna = gin_ref[...]
    for i, c in ((0, 0), (2, 1)):
        bias_z[0, c : c + 1] = jnp.sum(gp_ref[:, i * width : (i + 1) * width].astype(F32), axis=0, keepdims=True)
    send_bias = [remote_z(bias_z.at[0], bias_z.at[s], bz_send.at[s], bz_recv.at[s], along(s)) for s in steps]
    for copy in send_bias:
        copy.start()
    back, grad_scale = norm_back(tok_ref[...].astype(F32), per_row(selectors, mod_ref, 1, width), gna)
    to_slots(0, gna)
    to_slots(1, grad_scale)
    gin_ref[...] = gm_ref[...] + back
    line.begin(6)
    line.tick(3)
    planes[0].relay()
    planes[1].combine()
    line.begin(7)
    line.tick(4)
    planes[2].combine()
    line.tick(5)
    branch = branch_sum.total()
    branch = branch + mod_ref[slots : slots + 1, 3 * width : 4 * width]
    out_ref[...] = (mid_ref[...] + per_row(selectors, mod_ref, 5, width) * branch).astype(BF16)
    to_slots(5, cot_ref[...].astype(F32) * branch)
    mine = mods.at[me, pl.ds(pl.multiple_of(8 * z, 8), 8)]
    mine[...] = modrow[...].astype(BF16)
    send_mods = [remote_z(mine, mine, mz_send.at[s], mz_recv.at[s], along(s)) for s in steps]
    for copy in send_mods:
        copy.start()
    planes[1].relay()
    planes[3].combine()
    settle(0)
    line.tick(6)
    planes[2].relay()
    settle(1)
    line.tick(7)
    planes[3].relay()
    settle(2)
    line.tick(8)
    settle(3)
    line.tick(9)
    for copy in send_mods + send_bias:
        copy.wait_recv()
    gather = Gather(lambda j: mods.at[j], mods.shape[1], md_send, md_recv, mods.shape[1] // 2)
    gather.own()
    total = bias_z[0] + bias_z[1] + bias_z[2] + bias_z[3]
    gbup_out[...] = total[4:5, : gbup_out.shape[1]]
    bias_in[me] = total
    send_total = [remote(bias_in.at[me], bias_in.at[me], bi_send.at[e], bi_recv.at[e], e) for e in others]
    for copy in send_total:
        copy.start()
    line.tick(10)
    gather.along()
    line.tick(11)
    gather.across()
    gather.finish()
    local[6].wait()
    plane_rows = mods[:, pl.ds(pl.multiple_of(8 * z, 8), 8), :].reshape(64, mods.shape[2])
    half = mods.shape[2]
    first, second = nt(plane_rows, wada_ref[:, :half]), nt(plane_rows, wada_ref[:, half:])
    upper = lax.rem(lax.broadcasted_iota(jnp.int32, (64, 1), 0), 8) < slots
    gc_out[...] = jnp.where(upper, first, second).reshape(gc_out.shape)
    send_gc = [remote(gc_out.at[flipped(e)], gc_in.at[me], gc_send.at[e], gc_recv.at[e], e) for e in others]
    for copy in send_gc:
        copy.start()
    gc_in[me] = gc_out[me]
    line.tick(12)
    for copy in send_total:
        copy.wait_recv()
    total = bias_in[0]
    for j in others:
        total = total + bias_in[j]
    bias_ref[...] = total
    line.tick(13)
    for copy in send_gc + send_picks:
        copy.wait_recv()
    line.end()
    for copy in ups + send_picks + send_bias + send_mods + send_total + send_gc:
        copy.wait_send()
    for plane in planes + [branch_sum]:
        plane.drain()
    gather.drain()


def backward(sizes, tok, cot, mod, mid, gbup, pick, na, proj, probs, att, wo, bra, gnb, bbs, gdn, gup, wq, wada):
    rows, width = tok.shape
    part, columns = wada.shape
    wide = gdn.shape[0]
    S, V = jax.ShapeDtypeStruct, pltpu.VMEM
    vm, hbm = pl.BlockSpec(memory_space=pltpu.VMEM), pl.BlockSpec(memory_space=pl.ANY)
    dma = pltpu.SemaphoreType.DMA
    shapes = (
        S((rows, width), BF16), S((rows, width), F32), S((12, part, width), BF16), S((8, 32, columns // 2), BF16),
        S((8, 8, part), F32), S((4, 64, part), BF16), S((8, width), F32), S((1, wide), F32),
    )
    return pl.pallas_call(
        back_kernel,
        out_shape=shapes,
        in_specs=[pl.BlockSpec(memory_space=pltpu.SMEM)] + [vm] * 6 + [hbm] * 12,
        out_specs=(vm,) * len(shapes),
        scratch_shapes=[
            V((rows, width), BF16), V((rows, 3 * width), BF16), V((H, rows, rows), BF16), V((rows, width), BF16), V((8, part, width), BF16),
            V((8, part, wide), BF16), V((4, rows, width), BF16), V((rows, width), BF16), V((2, rows, width), BF16), V((12, part, width), BF16), V((12, lead(part), width), BF16),
            V((rows, width), F32), V((rows, width), BF16), V((rows, width), BF16), V((rows, 3 * width), BF16),
            V((4, 8, part, width), BF16), V((4, 4, part, width), BF16), V((4, lead(part), width), BF16), V((4, part - lead(part), width), BF16),
            V((4, part, width), BF16), V((4, part, width), BF16), V((8, part, width), BF16), V((part, columns), BF16),
            V((8, columns // 2), F32), V((4, 8, width), F32), V((8, 8, width), F32), V((8, 8, part), F32),
            dma((17,)), dma((8,)), dma((8,)), dma((6,)), dma((6,)), dma((5, 12)), dma((5, 12)), dma((4, 4)), dma((4, 4)),
            dma((4, 6)), dma((4, 6)), dma((8,)), dma((8,)), dma((4,)), dma((4,)), dma((4,)), dma((4,)), dma((4,)), dma((4,)),
            dma((8,)), dma((8,)), dma((8,)), dma((8,)),
        ],
        compiler_params=pltpu.CompilerParams(collective_id=2, has_side_effects=True, vmem_limit_bytes=62 << 20),
    )(sizes, tok, cot, mod, mid, gbup, pick, na, proj, probs, att, wo, bra, gnb, bbs, gdn, gup, wq, wada)

def finish_kernel(
    picks_ref, gc_ref, bias_ref, gbup_ref, cond_ref, sums_hbm, mods_hbm, out_hbm, gin_hbm,
    gcond_ref, gada_hbm, gbada_ref, gqkv_hbm, gbqkv_ref, gout_hbm, gbout_ref, gup_hbm, gbup_out, gdown_hbm, gbdown_ref,
    out_final, gin_final,
    sums_ref, mods_ref, gada_ref, gqkv_ref, gout_ref, gup_ref, gdown_ref, lanes, out_ref, gin_ref, sem,
):
    pairs = (
        (sums_hbm.at[pl.ds(0, 4)], sums_ref.at[pl.ds(0, 4)]), (sums_hbm.at[pl.ds(4, 4)], sums_ref.at[pl.ds(4, 4)]),
        (sums_hbm.at[pl.ds(8, 4)], sums_ref.at[pl.ds(8, 4)]), (mods_hbm, mods_ref), (out_hbm, out_ref), (gin_hbm, gin_ref),
        (gdown_ref, gdown_hbm), (gup_ref, gup_hbm), (gout_ref, gout_hbm), (gqkv_ref, gqkv_hbm), (gada_ref, gada_hbm),
        (out_ref, out_final), (gin_ref, gin_final),
    )
    copies = [pltpu.make_async_copy(src, dst, sem.at[i]) for i, (src, dst) in enumerate(pairs)]
    for copy in copies[:6]:
        copy.start()
    slots, width = cond_ref.shape
    part = width // 8
    half = mods_ref.shape[2]
    me, z = lax.axis_index("fsdp"), lax.axis_index("rep")
    copies[0].wait()
    for c in range(4):
        gdown_ref[c * part : (c + 1) * part] = sums_ref[c].astype(F32)
    copies[6].start()
    copies[1].wait()
    for c in range(4):
        gup_ref[:, c * width : (c + 1) * width] = sums_ref[4 + c].astype(F32)
    copies[7].start()
    copies[2].wait()
    gout_ref[...] = sums_ref[8].astype(F32)
    copies[8].start()
    copies[4].wait()
    copies[11].start()
    copies[5].wait()
    copies[12].start()
    for c in range(3):
        gqkv_ref[:, c * width : (c + 1) * width] = sums_ref[9 + c].astype(F32)
    copies[9].start()
    copies[3].wait()
    rows = mods_ref[...].reshape(256, half)
    acts = jnp.stack([picks_ref[i] for i in range(4)], axis=0).reshape(4, 8, 8, part)
    acts = jnp.stack([acts[:, f] for f in range(8)], axis=0).reshape(256, part).astype(F32)
    upper = lax.rem(lax.broadcasted_iota(jnp.int32, (256, 1), 0), 8) < slots
    first, second = jnp.where(upper, acts, 0.0).astype(BF16), jnp.where(upper, 0.0, acts).astype(BF16)
    gada_ref[:, :half] = tn(first, rows)
    gada_ref[:, half:] = tn(second, rows)
    copies[10].start()
    floats = rows.astype(F32)
    lanes[...] = jnp.zeros_like(lanes)

    def own(row, size):
        total = row.shape[1]
        lanes[0:1, :total] = row
        return pltpu.roll(lanes[:, :total], lax.rem(total - me * size, total), 1)[0, :size]

    column = jnp.concatenate(
        [
            jnp.sum(jnp.where(upper, floats, 0.0), axis=0, keepdims=True),
            jnp.sum(jnp.where(upper, 0.0, floats), axis=0, keepdims=True),
        ],
        axis=1,
    )
    gbada_ref[...] = own(column, gbada_ref.shape[0])
    gbqkv_ref[...] = own(jnp.concatenate([bias_ref[0:1], bias_ref[1:2]], axis=1), gbqkv_ref.shape[0])
    gbout_ref[...] = own(bias_ref[2:3], part)
    gbdown_ref[...] = own(bias_ref[3:4], part)
    wide, hid = gbup_ref.shape[1], gbup_out.shape[0]
    lanes[0:1, :wide] = gbup_ref[...]
    gbup_out[...] = pltpu.roll(lanes[:, :wide], lax.rem(wide - lax.rem(me, 2) * (wide - hid), wide), 1)[0, :hid]
    grad = None
    for j in range(8):
        lanes[:, :width] = jnp.zeros((8, width), F32)
        lanes[0:slots, :part] = gc_ref[j, 0:slots] + gc_ref[j, slots : 2 * slots]
        term = pltpu.roll(lanes[:, :width], j * part, 1) if j else lanes[:, :width]
        grad = term if grad is None else grad + term
    cond = cond_ref[...].astype(F32)
    gate = jax.nn.sigmoid(cond)
    gcond_ref[...] = grad[0:slots] * (gate * (1.0 + cond * (1.0 - gate)))
    for copy in copies[6:]:
        copy.wait()


def finish(output, grad_input, sums, mods, picks, gc, bias, gbup, cond, sizes):
    S, V = jax.ShapeDtypeStruct, pltpu.VMEM
    vm, hbm = pl.BlockSpec(memory_space=pltpu.VMEM), pl.BlockSpec(memory_space=pl.ANY)
    large = (1, 3, 5, 7, 9)
    shapes = tuple(S(size, F32) for size in sizes) + (S(output.shape, output.dtype), S(grad_input.shape, F32))
    specs = tuple(hbm if i in large or i >= len(sizes) else vm for i in range(len(shapes)))
    *grads, output, grad_input = pl.pallas_call(
        finish_kernel,
        out_shape=shapes,
        in_specs=[vm] * 5 + [hbm] * 4,
        out_specs=specs,
        scratch_shapes=[V(sums.shape, BF16), V(mods.shape, BF16)] + [V(sizes[i], F32) for i in large] + [
            V((8, 2 * mods.shape[2]), F32), V(output.shape, output.dtype), V(grad_input.shape, F32), pltpu.SemaphoreType.DMA((13,)),
        ],
        compiler_params=pltpu.CompilerParams(vmem_limit_bytes=56 << 20),
    )(picks, gc, bias, gbup, cond, sums, mods, output, grad_input)
    return (output, grad_input, *grads)

def fast(tokens, cond, image_sizes, w_ada, b_ada, w_qkv, b_qkv, w_out, b_out, w_up, b_up, w_down, b_down, cotangent):
    width = tokens.shape[1]
    part, columns = w_ada.shape
    mod, gnb, gbup, pick, na, proj, probs, att, bra, mid, wq, wo, bbs, gdn, gup = front(
        image_sizes, tokens, cotangent, cond, w_ada, b_ada, b_qkv, b_out, b_down, b_up,
        w_qkv, w_out, w_up, w_down,
    )
    wq, wo = wq.reshape(8, 3 * part, width), wo.reshape(8, part, width)
    output, grad_input, sums, mods, gc, picks, bias, gbup = backward(
        image_sizes, tokens, cotangent, mod, mid, gbup, pick, na, proj, probs, att, wo, bra, gnb, bbs, gdn, gup, wq, w_ada
    )
    sizes = tuple(
        leaf.shape for leaf in (cond, w_ada, b_ada, w_qkv, b_qkv, w_out, b_out, w_up, b_up, w_down, b_down)
    )
    return finish(output, grad_input, sums, mods, picks, gc, bias, gbup, cond, sizes)


def solution(mesh):
    placed = (
        P(("fsdp", "rep"), None),
        P(("fsdp", "rep"), None),
        P(("fsdp", "rep")),
        P("fsdp", None),
        P("fsdp"),
        P("fsdp", None),
        P("fsdp"),
        P("fsdp", None),
        P("fsdp"),
        P("fsdp", None),
        P("fsdp"),
        P("fsdp", None),
        P("fsdp"),
        P(("fsdp", "rep"), None),
    )
    fits = mesh.shape["fsdp"] == 8 and mesh.shape["rep"] == 4
    return jax.shard_map(
        fast if fits else local,
        mesh=mesh,
        in_specs=placed,
        out_specs=(
            P(("fsdp", "rep"), None),
            P(("fsdp", "rep"), None),
            P(("fsdp", "rep"), None),
            P("fsdp", None),
            P("fsdp"),
            P("fsdp", None),
            P("fsdp"),
            P("fsdp", None),
            P("fsdp"),
            P("fsdp", None),
            P("fsdp"),
            P("fsdp", None),
            P("fsdp"),
        ),
        check_vma=False,
    )
```

```python
import functools

import jax
import jax.numpy as jnp
from jax import lax
from jax.experimental import pallas as pl
from jax.experimental.pallas import tpu as pltpu
from jax.sharding import PartitionSpec as P

H = 16
EPSILON = 1e-06
HIGHEST = lax.Precision.HIGHEST
MASKED = -1e30


def layer_norm(inputs):
    average = jnp.mean(inputs, axis=-1, keepdims=True)
    centered = inputs - average
    variance = jnp.mean(centered * centered, axis=-1, keepdims=True)
    return centered * lax.rsqrt(variance + EPSILON)


def modulate(hidden, shift_part, scale_part):
    return layer_norm(hidden) * (1.0 + scale_part) + shift_part


def gelu_tanh(inputs):
    return jax.nn.gelu(inputs, approximate=True)


def product(first_operand, second_operand):
    return jnp.dot(first_operand, second_operand, preferred_element_type=jnp.float32)


def product_back(first_operand, second_operand):
    return lax.dot_general(
        first_operand, second_operand, (((1,), (1,)), ((), ())), preferred_element_type=jnp.float32
    )


def outer_sum(first_operand, second_operand):
    return lax.dot_general(
        first_operand, second_operand, (((0,), (0,)), ((), ())), preferred_element_type=jnp.float32
    )


def fetch_forward(weight, bias_piece):
    return (
        lax.all_gather(weight, "fsdp", axis=0, tiled=True),
        lax.all_gather(bias_piece, "fsdp", axis=0, tiled=True),
    )


def weights_again(weight):
    return lax.all_gather(weight, "fsdp", axis=0, tiled=True)


def reduce_grads(weight_grad, bias_grad):
    row_part, bias_part = (
        lax.psum_scatter(weight_grad, "fsdp", scatter_dimension=0, tiled=True),
        lax.psum_scatter(bias_grad, "fsdp", scatter_dimension=0, tiled=True),
    )
    column_part = lax.psum_scatter(row_part, "rep", scatter_dimension=1, tiled=True)
    whole_rows, bias_stack = (
        lax.all_gather(column_part, "rep", axis=1, tiled=True),
        lax.all_gather(bias_part[None], "rep", axis=0, tiled=True),
    )
    return (whole_rows, jnp.sum(bias_stack, axis=0))


def local(
    tokens,
    cond,
    image_sizes,
    w_ada,
    b_ada,
    w_qkv,
    b_qkv,
    w_out,
    b_out,
    w_up,
    b_up,
    w_down,
    b_down,
    cotangent,
):
    row_count, model_width = tokens.shape
    head_count = H
    head_dim = model_width // head_count
    slot_count = image_sizes.shape[0]
    scale_factor = head_dim ** (-0.5)
    block_rows = min(512, row_count)
    block_count = row_count // block_rows
    image_ends = jnp.sum(
        jnp.where(jnp.arange(slot_count)[:, None] >= jnp.arange(slot_count)[None, :], image_sizes[None, :], 0), axis=1
    )
    positions = jnp.arange(row_count, dtype=jnp.int32)
    image_ids = jnp.sum((positions[:, None] >= image_ends[None, :]).astype(jnp.int32), axis=1)
    selector = (image_ids[:, None] == jnp.arange(slot_count, dtype=jnp.int32)[None, :]).astype(
        jnp.float32
    )
    cond_float = cond.astype(jnp.float32)
    activ_float, silu_pull = jax.vjp(jax.nn.silu, cond_float)
    activ_low = activ_float.astype(jnp.bfloat16)
    full_ada, full_bada = fetch_forward(w_ada, b_ada)
    modulation = product(activ_low, full_ada) + full_bada.astype(jnp.float32)
    per_token = jnp.dot(selector, modulation, precision=HIGHEST)
    shift_a, scale_a, gate_a, shift_b, scale_b, gate_b = jnp.split(per_token, 6, axis=1)
    hidden = tokens.astype(jnp.float32)
    normed_a, pull_a = jax.vjp(modulate, hidden, shift_a, scale_a)
    normed_a_low = normed_a.astype(jnp.bfloat16)
    full_qkv, full_bqkv = fetch_forward(w_qkv, b_qkv)
    bias_qkv = full_bqkv.astype(jnp.float32)
    bias_full = jnp.concatenate(
        [bias_qkv[:model_width], jnp.zeros((model_width,), jnp.float32), bias_qkv[model_width:]]
    )
    projected = (product(normed_a_low, full_qkv) + bias_full).astype(jnp.bfloat16)
    query_heads = projected[:, :model_width].reshape(row_count, head_count, head_dim)
    key_heads = projected[:, model_width : 2 * model_width].reshape(row_count, head_count, head_dim)
    value_heads = projected[:, 2 * model_width :].reshape(row_count, head_count, head_dim)
    query_blocks = query_heads.reshape(block_count, block_rows, head_count, head_dim)
    id_blocks = image_ids.reshape(block_count, block_rows)

    def scores_of(query_block, id_block):
        raw_scores = (
            jnp.einsum("qhd,khd->hqk", query_block, key_heads, preferred_element_type=jnp.float32)
            * scale_factor
        )
        same_image = id_block[:, None] == image_ids[None, :]
        return jnp.where(same_image[None], raw_scores, MASKED)

    def forward_block(block_item):
        query_block, id_block = block_item
        scores = scores_of(query_block, id_block)
        row_max = jnp.max(scores, axis=-1, keepdims=True)
        exponent = jnp.exp(scores - row_max)
        row_total = jnp.sum(exponent, axis=-1, keepdims=True)
        probabilities = (exponent / row_total).astype(jnp.bfloat16)
        attended_block = jnp.einsum(
            "hqk,khd->qhd", probabilities, value_heads, preferred_element_type=jnp.float32
        )
        return (attended_block.astype(jnp.bfloat16), (row_max + jnp.log(row_total))[:, :, 0])

    attended_blocks, lse_blocks = lax.map(forward_block, (query_blocks, id_blocks))
    attended = attended_blocks.reshape(row_count, model_width)
    full_out, full_bout = fetch_forward(w_out, b_out)
    branch_a = product(attended, full_out) + full_bout.astype(jnp.float32)
    middle = hidden + gate_a * branch_a
    normed_b, pull_b = jax.vjp(modulate, middle, shift_b, scale_b)
    normed_b_low = normed_b.astype(jnp.bfloat16)
    full_up, full_bup = fetch_forward(w_up, b_up)
    inner_pre = product(normed_b_low, full_up) + full_bup.astype(jnp.float32)
    activated, gelu_pull = jax.vjp(gelu_tanh, inner_pre)
    activated_low = activated.astype(jnp.bfloat16)
    full_down, full_bdown = fetch_forward(w_down, b_down)
    branch_b = product(activated_low, full_down) + full_bdown.astype(jnp.float32)
    output = (middle + gate_b * branch_b).astype(jnp.bfloat16)
    grad_out = cotangent.astype(jnp.float32)
    grad_gate_b = grad_out * branch_b
    grad_branch_b = (gate_b * grad_out).astype(jnp.bfloat16)
    grad_w_down, grad_b_down = reduce_grads(
        outer_sum(activated_low, grad_branch_b), jnp.sum(grad_branch_b.astype(jnp.float32), axis=0)
    )
    back_down = weights_again(w_down)
    grad_activated = product_back(grad_branch_b, back_down)
    (grad_inner,) = gelu_pull(grad_activated)
    grad_inner_low = grad_inner.astype(jnp.bfloat16)
    grad_w_up, grad_b_up = reduce_grads(
        outer_sum(normed_b_low, grad_inner_low), jnp.sum(grad_inner_low.astype(jnp.float32), axis=0)
    )
    back_up = weights_again(w_up)
    grad_normed_b = product_back(grad_inner_low, back_up)
    grad_middle_norm, grad_shift_b, grad_scale_b = pull_b(grad_normed_b)
    grad_middle = grad_out + grad_middle_norm
    grad_gate_a = grad_middle * branch_a
    grad_branch_a = (gate_a * grad_middle).astype(jnp.bfloat16)
    grad_w_out, grad_b_out = reduce_grads(
        outer_sum(attended, grad_branch_a), jnp.sum(grad_branch_a.astype(jnp.float32), axis=0)
    )
    back_out = weights_again(w_out)
    grad_attended = product_back(grad_branch_a, back_out).astype(jnp.bfloat16)
    grad_att_blocks = grad_attended.reshape(block_count, block_rows, head_count, head_dim)

    def backward_block(carried, block_item):
        key_grad, value_grad = carried
        query_block, id_block, grad_block, lse_block = block_item
        scores = scores_of(query_block, id_block)
        probabilities = jnp.exp(scores - lse_block[:, :, None])
        probabilities_low = probabilities.astype(jnp.bfloat16)
        grad_probs = jnp.einsum(
            "qhd,khd->hqk", grad_block, value_heads, preferred_element_type=jnp.float32
        )
        row_delta = jnp.sum(probabilities * grad_probs, axis=-1, keepdims=True)
        grad_scores = (probabilities * (grad_probs - row_delta)).astype(jnp.bfloat16)
        query_grad = (
            jnp.einsum("hqk,khd->qhd", grad_scores, key_heads, preferred_element_type=jnp.float32)
            * scale_factor
        )
        key_grad = (
            key_grad
            + jnp.einsum(
                "hqk,qhd->khd", grad_scores, query_block, preferred_element_type=jnp.float32
            )
            * scale_factor
        )
        value_grad = value_grad + jnp.einsum(
            "hqk,qhd->khd", probabilities_low, grad_block, preferred_element_type=jnp.float32
        )
        return ((key_grad, value_grad), query_grad)

    zero_heads = jnp.zeros((row_count, head_count, head_dim), jnp.float32)
    (grad_keys, grad_values), grad_query_blocks = lax.scan(
        backward_block,
        (zero_heads, zero_heads),
        (query_blocks, id_blocks, grad_att_blocks, lse_blocks),
    )
    grad_projected = jnp.concatenate(
        [
            grad_query_blocks.reshape(row_count, model_width),
            grad_keys.reshape(row_count, model_width),
            grad_values.reshape(row_count, model_width),
        ],
        axis=1,
    ).astype(jnp.bfloat16)
    column_sums = jnp.sum(grad_projected.astype(jnp.float32), axis=0)
    grad_bias_qkv = jnp.concatenate([column_sums[:model_width], column_sums[2 * model_width :]])
    grad_w_qkv, grad_b_qkv = reduce_grads(outer_sum(normed_a_low, grad_projected), grad_bias_qkv)
    back_qkv = weights_again(w_qkv)
    grad_normed_a = product_back(grad_projected, back_qkv)
    grad_hidden_norm, grad_shift_a, grad_scale_a = pull_a(grad_normed_a)
    grad_input = grad_middle + grad_hidden_norm
    grad_per_token = jnp.concatenate(
        [grad_shift_a, grad_scale_a, grad_gate_a, grad_shift_b, grad_scale_b, grad_gate_b], axis=1
    )
    grad_modulation = lax.dot_general(
        selector, grad_per_token, (((0,), (0,)), ((), ())), precision=HIGHEST
    ).astype(jnp.bfloat16)
    grad_w_ada, grad_b_ada = reduce_grads(
        outer_sum(activ_low, grad_modulation), jnp.sum(grad_modulation.astype(jnp.float32), axis=0)
    )
    back_ada = weights_again(w_ada)
    grad_activ = product_back(grad_modulation, back_ada)
    (grad_cond,) = silu_pull(grad_activ)
    return (
        output,
        grad_input,
        grad_cond,
        grad_w_ada,
        grad_b_ada,
        grad_w_qkv,
        grad_b_qkv,
        grad_w_out,
        grad_b_out,
        grad_w_up,
        grad_b_up,
        grad_w_down,
        grad_b_down,
    )


MESH = pl.DeviceIdType.MESH
F32, BF16 = jnp.float32, jnp.bfloat16


def flipped(offset):
    index = lax.axis_index("fsdp")
    y, x, core = index // 4, (index // 2) % 2, index % 2
    y = 1 - y if offset & 4 else y
    x = 1 - x if offset & 2 else x
    core = 1 - core if offset & 1 else core
    return y * 4 + x * 2 + core


def greet(offsets):
    barrier = pltpu.get_barrier_semaphore()
    for offset in offsets:
        pl.semaphore_signal(barrier, inc=1, device_id={"fsdp": flipped(offset)}, device_id_type=MESH)
    pl.semaphore_wait(barrier, len(offsets))


def remote(src, dst, send, recv, offset):
    return pltpu.make_async_remote_copy(
        src_ref=src, dst_ref=dst, send_sem=send, recv_sem=recv,
        device_id={"fsdp": flipped(offset)}, device_id_type=MESH,
    )


def lead(rows):
    return -(-rows // 32) * 16


class Gather:
    def __init__(self, shard, rows, send, recv, lead):
        first, second = pl.ds(0, lead), pl.ds(lead, rows - lead)
        piece = {e: shard(flipped(e)) for e in (0, 2, 4, 6)}
        plan = (
            (piece[0], 1), (piece[0], 2), (piece[0], 4),
            (piece[2].at[first], 4), (piece[4].at[second], 2),
            (piece[2], 1), (piece[4], 1), (piece[6], 1),
        )
        self.copies = [remote(ref, ref, send.at[i], recv.at[i], e) for i, (ref, e) in enumerate(plan)]

    def own(self):
        for i in (1, 2, 0):
            self.copies[i].start()

    def along(self):
        self.copies[1].wait_recv()
        self.copies[3].start()
        self.copies[5].start()
        self.copies[2].wait_recv()
        self.copies[4].start()
        self.copies[6].start()

    def across(self):
        self.copies[3].wait_recv()
        self.copies[4].wait_recv()
        self.copies[7].start()

    def sibling(self, p):
        self.copies[(0, 5, 6, 7)[p]].wait_recv()

    def finish(self):
        for p in range(4):
            self.sibling(p)

    def drain(self):
        for copy in self.copies:
            copy.wait_send()


class PlaneSum:
    def __init__(self, held, odd, pair_in, cross_a, cross_b, from_x, from_y, pair_send, pair_recv, send, recv, rows, lead):
        self.a, self.b = a, b = pl.ds(0, lead), pl.ds(lead, rows - lead)
        self.held, self.pair_in, self.cross_a, self.cross_b = held, pair_in, cross_a, cross_b
        self.from_x, self.from_y = from_x, from_y
        self.pairs = [] if odd is None else [
            remote(odd[p], pair_in[p], pair_send.at[p], pair_recv.at[p], 1) for p in range(4)
        ]
        plan = (
            (held[3].at[a], cross_a, 2), (held[3].at[b], cross_b, 4),
            (held[2].at[b], from_y.at[b], 4), (held[1].at[a], from_x.at[a], 2),
            (held[2].at[a], from_y.at[a], 4), (held[1].at[b], from_x.at[b], 2),
        )
        self.copies = [remote(src, dst, send.at[i], recv.at[i], e) for i, (src, dst, e) in enumerate(plan)]

    def pair(self):
        for p in (3, 2, 1, 0):
            self.pairs[p].start()

    def leave(self, p):
        if p == 3:
            self.copies[0].start()
            self.copies[1].start()
        elif p:
            self.copies[(None, 3, 2)[p]].start()

    def join(self, p):
        self.pairs[p].wait_recv()
        self.held[p][...] += self.pair_in[p][...]
        self.leave(p)

    def combine(self):
        for p in (3, 2, 1, 0):
            self.join(p)

    def relay(self):
        for i, p, part, came in ((0, 2, self.a, self.cross_a), (1, 1, self.b, self.cross_b)):
            self.copies[i].wait_recv()
            ref = self.held[p].at[part]
            ref[...] += came[...]
            self.copies[4 + i].start()

    def total(self):
        for i in (2, 3, 4, 5):
            self.copies[i].wait_recv()
        return self.held[0][...].astype(F32) + self.from_x[...].astype(F32) + self.from_y[...].astype(F32)

    def drain(self):
        for copy in self.pairs + self.copies:
            copy.wait_send()


def nt(a, b):
    return lax.dot_general(a, b, (((1,), (1,)), ((), ())), preferred_element_type=F32)


def tn(a, b):
    return lax.dot_general(a, b, (((0,), (0,)), ((), ())), preferred_element_type=F32)


def nn(a, b):
    return jnp.dot(a, b, preferred_element_type=F32)


def normalized(values):
    centered = values - jnp.mean(values, axis=-1, keepdims=True)
    variance = jnp.mean(centered * centered, axis=-1, keepdims=True)
    scale = lax.rsqrt(variance + EPSILON)
    return centered * scale, scale


def image_of(place, sizes_ref):
    end = jnp.int32(0)
    image = jnp.zeros(place.shape, jnp.int32)
    for j in range(sizes_ref.shape[0]):
        end = end + sizes_ref[j]
        image = image + (place >= end).astype(jnp.int32)
    return image


def per_row(selectors, modulation, part, width):
    total = None
    for j, chosen in enumerate(selectors):
        term = chosen * modulation[j : j + 1, part * width : (part + 1) * width]
        total = term if total is None else total + term
    return total


def head_window(head, head_dim):
    low = head * head_dim
    base = low // 128 * 128
    wide = 128 if low - base + head_dim <= 128 else 256
    lane = lax.broadcasted_iota(jnp.int32, (1, wide), 1) + (base - low)
    mask = jnp.where((lane >= 0) & (lane < head_dim), 1.0, 0.0)
    return base, wide, mask


GELU_RATE = 0.7978845608028654
GELU_CUBE = 0.044715


def gelu_parts(u):
    square = u * u
    bend = jnp.tanh(GELU_RATE * u * (1.0 + GELU_CUBE * square))
    half = 0.5 * (1.0 + bend)
    slope = half + 0.5 * u * (1.0 - bend * bend) * (GELU_RATE * (1.0 + 3.0 * GELU_CUBE * square))
    return u * half, slope


def front_kernel(
    sizes_ref, tok_ref, cot_ref, cond_ref, wada_ref, bada_ref, bqkv_ref, bout_ref, bdown_ref, bup_in,
    wqkv_hbm, wout_hbm, wup_hbm, wdn_hbm,
    mod_ref, gnb_ref, gbup_ref, pick_ref, na_hbm, proj_hbm, probs_hbm, att_hbm, bra_hbm, mid_hbm, wq_hbm, wo_hbm,
    bb_hbm, gdn_hbm, gup_hbm,
    na_ref, proj_ref, probs_ref, att_ref, bra_ref, mid_ref, arena, wo_all, bb_ref, gdn_ref, gup_ref,
    cond_all, pm, mpair, mfar, mlow, lay, lay_b, nb_all, gbb_all, wup_all, wdn_ref, act_all, gi_all, in_pair, cross_a, cross_b, from_x, from_y,
    loc_sem, save_sem, c_send, c_recv, mp_send, mp_recv, mf_send, mf_recv, up_send, up_recv,
    q_send, q_recv, o_send, o_recv, g_send, g_recv, n_send, n_recv, pr_send, pr_recv, far_send, far_recv,
):
    rows, width = tok_ref.shape
    head_dim = width // H
    slots = sizes_ref.shape[0]
    part = wada_ref.shape[0]
    own, wide = wdn_hbm.shape[0], wup_all.shape[1]
    me = flipped(0)
    others = range(1, 8)

    def strip(ref, size):
        return lambda j: ref.at[pl.ds(pl.multiple_of(j * size, 8), size)]

    def up_piece(e):
        j = flipped(e)
        begin = pl.multiple_of(2 * own * (j // 2) + (2 * own - wide) * (j % 2), 128)
        return wup_hbm.at[:, pl.ds(begin, wide)]

    shift = lax.rem(me, 2) * (wide - own)
    blank = lax.rem(me + 1, 2) * own
    wq_strip, wup_strip = strip(arena, 3 * part), strip(wup_all, part)
    sources = [
        (wqkv_hbm.at[:, pl.ds(i * width, width)], arena.at[pl.ds(pl.multiple_of(me * 3 * part + i * part, 8), part)]) for i in range(3)
    ] + [
        (wout_hbm, strip(wo_all, part)(me)), (up_piece(0), wup_strip(me)),
        (wdn_hbm, wdn_ref.at[pl.ds(pl.multiple_of(shift, 8), own)]),
    ]
    local = [pltpu.make_async_copy(src, dst, loc_sem.at[i]) for i, (src, dst) in enumerate(sources)]
    for copy in local:
        copy.start()
    saves = [
        pltpu.make_async_copy(src, dst, save_sem.at[i])
        for i, (src, dst) in enumerate((
            (na_ref, na_hbm), (proj_ref, proj_hbm), (probs_ref, probs_hbm), (att_ref, att_hbm),
            (bra_ref, bra_hbm), (mid_ref, mid_hbm), (arena, wq_hbm), (wo_all, wo_hbm),
            (bb_ref, bb_hbm), (gdn_ref, gdn_hbm), (gup_ref, gup_hbm),
        ))
    ]
    act = jax.nn.silu(cond_ref[...].astype(F32))
    cond_all[me, :slots] = act
    cond_all[me, slots:] = act
    qkv = Gather(wq_strip, 3 * part, q_send, q_recv, lead(3 * part))
    out = Gather(strip(wo_all, part), part, o_send, o_recv, lead(part))
    gbb = Gather(lambda j: gbb_all.at[j], rows, g_send, g_recv, rows // 2)
    nb = Gather(lambda j: nb_all.at[j], rows, n_send, n_recv, rows // 2)
    conds = [remote(cond_all.at[me], cond_all.at[me], c_send.at[e], c_recv.at[e], e) for e in others]
    ups = [remote(up_piece(e), wup_strip(me), up_send.at[e], up_recv.at[e], e) for e in others]
    pairs = [remote(pm.at[flipped(2 * p + 1)], mpair.at[p], mp_send.at[p], mp_recv.at[p], 1) for p in range(4)]
    fars = [remote(mlow.at[p], mfar.at[p], mf_send.at[p], mf_recv.at[p], 2 * p) for p in range(1, 4)]
    block = [arena.at[pl.ds(i * rows, rows)] for i in range(12)]
    gnb = PlaneSum(
        block[8:], block[:4], [in_pair.at[p] for p in range(4)], cross_a, cross_b, from_x, from_y,
        pr_send, pr_recv, far_send, far_recv, rows, rows // 2,
    )
    bb_pairs = [remote(block[4 + p], in_pair.at[4 + p], pr_send.at[4 + p], pr_recv.at[4 + p], 1) for p in range(4)]

    greet(others)
    for copy in conds:
        copy.start()
    for copy in local[:3]:
        copy.wait()
    qkv.own()
    lay[...] = jnp.zeros_like(lay)
    lay_b[...] = jnp.zeros_like(lay_b)
    lay[0:1, : bada_ref.shape[0]] = bada_ref[...].astype(F32)[None]
    bada = pltpu.roll(lay[...], me * bada_ref.shape[0], 1)[0:1]
    begin = 0
    for ref in (bqkv_ref, bout_ref, bdown_ref):
        size = ref.shape[0]
        lay_b[0:1, begin : begin + size] = ref[...].astype(F32)[None]
        lay_b[0:1, begin : begin + 8 * size] = pltpu.roll(lay_b[:, begin : begin + 8 * size], me * size, 1)[0:1]
        begin += 8 * size
    for copy in conds:
        copy.wait_recv()
    everyone = cond_all[...].reshape(8 * cond_all.shape[1], width).astype(BF16)
    pick = (
        lax.broadcasted_iota(jnp.int32, (width, part), 0) == lax.broadcasted_iota(jnp.int32, (width, part), 1) + me * part
    )
    chosen = nn(everyone, jnp.where(pick, 1.0, 0.0).astype(BF16)).astype(BF16)
    pick_ref[...] = chosen
    bias_row = lax.broadcasted_iota(jnp.int32, (8, 1), 0) == slots
    piece = nn(chosen, wada_ref[...]).reshape(pm.shape)
    pm[...] = piece + bada[None]
    pm[:, :, : lay_b.shape[1]] = jnp.where(bias_row[None], lay_b[0:1][None], pm[:, :, : lay_b.shape[1]])
    for copy in pairs:
        copy.start()
    for p in (3, 2, 1, 0):
        pairs[p].wait_recv()
        total = pm[flipped(2 * p)] + mpair[p]
        if p:
            mlow[p] = total.astype(BF16)
            fars[p - 1].start()
        else:
            pm[me] = total
    qkv.along()
    local[3].wait()
    out.own()
    lay[...] = jnp.zeros_like(lay)
    lay[0:1, :own] = bup_in[...].astype(F32)[None]
    bup = pltpu.roll(lay[:, :wide], shift, 1)[0:1]
    wdn_ref[pl.ds(pl.multiple_of(blank, 8), wide - own)] = jnp.zeros((wide - own, width), BF16)
    for copy in fars:
        copy.wait_recv()
    modulation = pm[me] + (mfar[1].astype(F32) + mfar[2].astype(F32) + mfar[3].astype(F32))
    mod_ref[...] = modulation
    bias = modulation[slots : slots + 1]
    image = image_of(lax.broadcasted_iota(jnp.int32, (rows, 1), 0), sizes_ref)
    selectors = [jnp.where(image == j, 1.0, 0.0) for j in range(slots)]
    gbb_all[me] = (per_row(selectors, mod_ref, 5, width) * cot_ref[...].astype(F32)).astype(BF16)
    gbb.own()
    hidden = tok_ref[...].astype(F32)
    na_ref[...] = (
        normalized(hidden)[0] * (1.0 + per_row(selectors, mod_ref, 1, width)) + per_row(selectors, mod_ref, 0, width)
    ).astype(BF16)
    saves[0].start()
    qkv.across()
    qkv.finish()
    saves[6].start()
    for i in range(3):
        strips = [arena[3 * part * j + i * part : 3 * part * j + (i + 1) * part] for j in range(8)]
        value = nn(na_ref[...], jnp.concatenate(strips, axis=0))
        if i == 0:
            value = value + bias[:, :width]
        if i == 2:
            value = value + bias[:, width : 2 * width]
        proj_ref[:, i * width : (i + 1) * width] = value.astype(BF16)
    saves[1].start()
    out.along()
    for copy in ups:
        copy.start()
    att_ref[...] = jnp.zeros_like(att_ref)
    row_image = image_of(lax.broadcasted_iota(jnp.int32, (rows, rows), 0), sizes_ref)
    column_image = image_of(lax.broadcasted_iota(jnp.int32, (rows, rows), 1), sizes_ref)
    hidden_pairs = jnp.where(row_image == column_image, 0.0, -1e30)
    for head in range(H):
        base, window, mask = head_window(head, head_dim)
        mask = mask.astype(BF16)
        query = proj_ref[:, base : base + window] * mask
        key = proj_ref[:, width + base : width + base + window]
        value = proj_ref[:, 2 * width + base : 2 * width + base + window] * mask
        scores = nt(query, key) * head_dim ** (-0.5) + hidden_pairs
        exponent = jnp.exp(scores - jnp.max(scores, axis=-1, keepdims=True))
        probs = (exponent * (1.0 / jnp.sum(exponent, axis=-1, keepdims=True))).astype(BF16)
        probs_ref[head] = probs
        att_ref[:, base : base + window] += nn(probs, value).astype(BF16)
        if head == 5:
            out.across()
    saves[2].start()
    saves[3].start()
    gbb.along()
    out.finish()
    saves[7].start()
    branch = nn(att_ref[...], wo_all[...]) + bias[:, 2 * width : 3 * width]
    bra_ref[...] = branch
    middle = tok_ref[...].astype(F32) + per_row(selectors, mod_ref, 2, width) * branch
    mid_ref[...] = middle
    nb_all[me] = (
        normalized(middle)[0] * (1.0 + per_row(selectors, mod_ref, 4, width)) + per_row(selectors, mod_ref, 3, width)
    ).astype(BF16)
    nb.own()
    saves[4].start()
    saves[5].start()

    qkv.drain()
    saves[6].wait()
    local[4].wait()
    local[5].wait()
    for copy in ups:
        copy.wait_recv()
    gbb.across()

    def one(slot):
        inner = nn(nb_all[slot], wup_all[...]) + bup
        act, slope = gelu_parts(inner)
        act_all[slot] = act.astype(BF16)
        gi_all[slot] = (slope * nt(gbb_all[slot], wdn_ref[...])).astype(BF16)

    for p in range(4):
        even, odd = flipped(2 * p), flipped(2 * p + 1)
        if p == 1:
            nb.along()
        if p == 3:
            nb.across()
        one(even)
        block[8 + p][...] = nt(gi_all[even], wup_all[...]).astype(BF16)
        gbb.sibling(p)
        nb.sibling(p)
        one(odd)
        block[p][...] = nt(gi_all[odd], wup_all[...]).astype(BF16)
        gnb.pairs[p].start()
        gnb.join(p)

    def forth(p):
        even, odd = flipped(2 * p), flipped(2 * p + 1)
        block[4 + p][...] = nn(act_all[odd], wdn_ref[...]).astype(BF16)
        bb_pairs[p].start()
        bb_ref[p] = nn(act_all[even], wdn_ref[...]).astype(BF16)

    forth(0)
    forth(1)
    forth(2)
    forth(3)
    gnb.relay()
    gdn_ref[...] = tn(act_all[...].reshape(8 * rows, wide), gbb_all[...].reshape(8 * rows, width)).astype(BF16)
    saves[9].start()
    inner_grads = gi_all[...].reshape(8 * rows, wide)
    gup_ref[...] = tn(nb_all[...].reshape(8 * rows, width), inner_grads).astype(BF16).reshape(gup_ref.shape)
    saves[10].start()
    gbup_ref[...] = jnp.sum(inner_grads.astype(F32), axis=0, keepdims=True)
    for p in range(4):
        bb_pairs[p].wait_recv()
        bb_ref[p] += in_pair[4 + p]
    saves[8].start()
    gnb_ref[...] = gnb.total()
    for copy in conds + pairs + fars + ups + bb_pairs:
        copy.wait_send()
    for gather in (out, gbb, nb, gnb):
        gather.drain()
    for i, copy in enumerate(saves):
        if i != 6:
            copy.wait()


def front(sizes, tok, cot, cond, wada, bada, bqkv, bout, bdown, bup, wqkv, wout, wup, wdn):
    rows, width = tok.shape
    part, columns = wada.shape
    wide = wdn.shape[0] + 64
    S, V = jax.ShapeDtypeStruct, pltpu.VMEM
    vm, hbm = pl.BlockSpec(memory_space=pltpu.VMEM), pl.BlockSpec(memory_space=pl.ANY)
    dma = pltpu.SemaphoreType.DMA
    kept = (
        ((rows, width), BF16), ((rows, 3 * width), BF16), ((H, rows, rows), BF16), ((rows, width), BF16),
        ((rows, width), F32), ((rows, width), F32), ((24 * part, width), BF16), ((8 * part, width), BF16),
        ((4, rows, width), BF16), ((wide, width), BF16), ((8, part, wide), BF16),
    )
    shapes = (S((8, columns), F32), S((rows, width), F32), S((1, wide), F32), S((64, part), BF16)) + tuple(S(*pair) for pair in kept)
    return pl.pallas_call(
        front_kernel,
        out_shape=shapes,
        in_specs=[pl.BlockSpec(memory_space=pltpu.SMEM)] + [vm] * 9 + [hbm] * 4,
        out_specs=(vm,) * 4 + (hbm,) * 11,
        scratch_shapes=[V(*pair) for pair in kept] + [
            V((8, 8, width), F32), V((8, 8, columns), F32), V((4, 8, columns), F32),
            V((4, 8, columns), BF16), V((4, 8, columns), BF16), V((8, columns), F32), V((8, 4 * width), F32),
            V((8, rows, width), BF16), V((8, rows, width), BF16), V((8 * part, wide), BF16), V((wide, width), BF16),
            V((8, rows, wide), BF16), V((8, rows, wide), BF16), V((8, rows, width), BF16),
            V((rows // 2, width), BF16), V((rows // 2, width), BF16), V((rows, width), BF16), V((rows, width), BF16),
            dma((6,)), dma((11,)), dma((8,)), dma((8,)), dma((4,)), dma((4,)), dma((4,)), dma((4,)),
        ] + [dma((8,))] * 14,
        compiler_params=pltpu.CompilerParams(collective_id=0, has_side_effects=True, vmem_limit_bytes=61 << 20),
    )(sizes, tok, cot, cond, wada, bada, bqkv, bout, bdown, bup, wqkv, wout, wup, wdn)

def along(step):
    return lax.rem(lax.axis_index("rep") + step, 4)


def remote_z(src, dst, send, recv, z):
    return pltpu.make_async_remote_copy(
        src_ref=src, dst_ref=dst, send_sem=send, recv_sem=recv, device_id={"rep": z}, device_id_type=MESH
    )


DEPTH = 4


class LineSum:
    def __init__(self, chunks, held, halves, send, recv, lead):
        self.chunks, self.held, self.halves, self.send, self.recv = chunks, held, halves, send, recv
        rows = chunks.shape[1]
        self.parts = (pl.ds(0, lead), pl.ds(lead, rows - lead))
        self.sizes = (lead, rows - lead)

    def on(self, roles, action):
        z = lax.axis_index("rep")
        for role in roles:
            pl.when(z == role)(functools.partial(action, role))

    def enter(self, c, role):
        mate = (1, 0, 3, 2)[role]
        return remote_z(self.chunks.at[c], self.held.at[c], self.send.at[0, c], self.recv.at[0, c], mate)

    def give(self, c, role):
        half = 2 - role
        space = self.halves.at[c, pl.ds(0, self.sizes[half])]
        return remote_z(self.chunks.at[c, self.parts[half]], space, self.send.at[1, c], self.recv.at[1, c], 3 - role)

    def result(self, c, half, kind, target):
        ref = self.held.at[c, self.parts[half]]
        return remote_z(ref, ref, self.send.at[kind, c], self.recv.at[kind, c], target)

    def begin(self, c):
        def action(role):
            if c >= DEPTH:
                self.enter(c - DEPTH, role).wait_send()
            self.enter(c, role).start()

        self.on((0, 3), action)

    def first(self, c):
        def action(role):
            self.enter(c, role).wait_recv()
            self.chunks[c] += self.held[c]
            self.give(c, role).start()

        self.on((1, 2), action)

    def second(self, c):
        def action(role):
            mine = role - 1
            self.give(c, 3 - role).wait_recv()
            part, size = self.parts[mine], self.sizes[mine]
            self.held[c, part] = self.chunks[c, part] + self.halves[c, :size]
            self.result(c, mine, 2, 3 - role).start()
            self.result(c, mine, 3, (1, 0, 3, 2)[role]).start()

        self.on((1, 2), action)

    def third(self, c):
        def action(role):
            other = 2 - role
            self.result(c, other, 2, 3 - role).wait_recv()
            self.result(c, other, 4, (1, 0, 3, 2)[role]).start()

        self.on((1, 2), action)

    def tick(self, n):
        count = self.chunks.shape[0]
        for step, c in ((self.first, n), (self.second, n - 1), (self.third, n - 2)):
            if 0 <= c < count:
                step(c)

    def end(self):
        def outer(role):
            near = 0 if role == 0 else 1
            for c in range(self.chunks.shape[0]):
                self.result(c, near, 3, 1).wait_recv()
                self.result(c, 1 - near, 4, 1).wait_recv()
                if c >= self.chunks.shape[0] - DEPTH:
                    self.enter(c, role).wait_send()

        def inner(role):
            for c in range(self.chunks.shape[0]):
                self.give(c, role).wait_send()
                self.result(c, role - 1, 2, 3 - role).wait_send()
                self.result(c, role - 1, 3, 3 - role).wait_send()
                self.result(c, 2 - role, 4, 3 - role).wait_send()

        self.on((0, 3), outer)
        self.on((1, 2), inner)


def norm_back(values, scale_part, grad):
    normal, rate = normalized(values)
    inner = grad * (1.0 + scale_part)
    back = rate * (
        inner - jnp.mean(inner, axis=-1, keepdims=True) - normal * jnp.mean(inner * normal, axis=-1, keepdims=True)
    )
    return back, grad * normal


def back_kernel(
    sizes_ref, tok_ref, cot_ref, mod_ref, mid_ref, gbup_ref, pick_ref, na_hbm, proj_hbm, probs_hbm, att_hbm, wo_hbm,
    bra_hbm, gnb_hbm, bbs_hbm, gdn_hbm, gup_hbm, wq_hbm, wada_hbm,
    out_ref, gin_ref, sums, mods, gc_in, picks, bias_ref, gbup_out,
    na_ref, proj_ref, probs_ref, att_ref, wo_all,
    gup_in, bb_in, bb_cross, bb_from, zbuf, zhalf, gm_ref, gba_ref, gatt_ref, gp_ref, blocks, pair_in, cross_a, cross_b, from_x, from_y,
    wq_buf, wada_ref, modrow, bias_z, bias_in, gc_out,
    loc_sem, up_send, up_recv, bb_send, bb_recv, z_send, z_recv, ps_send, ps_recv, pc_send, pc_recv,
    md_send, md_recv, mz_send, mz_recv, pk_send, pk_recv, bz_send, bz_recv, bi_send, bi_recv, gc_send, gc_recv,
):
    rows, width = tok_ref.shape
    head_dim = width // H
    slots = sizes_ref.shape[0]
    part = width // 8
    hid = 8 * part // 2
    me, z = flipped(0), lax.axis_index("rep")
    core = lax.rem(me, 2)
    others, steps = range(1, 8), range(1, 4)

    line = LineSum(zbuf, sums, zhalf, z_send, z_recv, lead(part))
    planes = [
        PlaneSum(
            [blocks.at[i, flipped(2 * p)] for p in range(4)], [blocks.at[i, flipped(2 * p + 1)] for p in range(4)],
            [pair_in.at[i, p] for p in range(4)], cross_a.at[i], cross_b.at[i], from_x.at[i], from_y.at[i],
            ps_send.at[i], ps_recv.at[i], pc_send.at[i], pc_recv.at[i], part, lead(part),
        )
        for i in range(4)
    ]
    ups = [remote(gup_hbm.at[flipped(e)], gup_in.at[me], up_send.at[e], up_recv.at[e], e) for e in others]
    branch_sum = PlaneSum(
        [bb_in.at[p] for p in range(4)], None, None, bb_cross.at[pl.ds(0, rows // 2)], bb_cross.at[pl.ds(rows // 2, rows // 2)],
        bb_from.at[0], bb_from.at[1], None, None, bb_send, bb_recv, rows, rows // 2,
    )
    shift = (gdn_hbm.shape[0] - hid) * core
    local = [pltpu.make_async_copy(gdn_hbm.at[pl.ds(pl.multiple_of(shift + part * c, 16), part)], zbuf.at[c], loc_sem.at[c]) for c in range(4)]
    local.append(pltpu.make_async_copy(gup_hbm.at[me], gup_in.at[me], loc_sem.at[4]))
    local.append(pltpu.make_async_copy(bbs_hbm, bb_in, loc_sem.at[5]))
    local.append(pltpu.make_async_copy(wada_hbm, wada_ref, loc_sem.at[6]))
    loads = [pltpu.make_async_copy(wq_hbm.at[:, pl.ds(i * part, part)], wq_buf, loc_sem.at[7 + i]) for i in range(3)]
    local.append(pltpu.make_async_copy(bra_hbm, gm_ref, loc_sem.at[10]))
    local.append(pltpu.make_async_copy(gnb_hbm, gin_ref, loc_sem.at[11]))
    local += [
        pltpu.make_async_copy(src, dst, loc_sem.at[12 + i])
        for i, (src, dst) in enumerate((
            (wo_hbm, wo_all), (att_hbm, att_ref), (proj_hbm, proj_ref), (probs_hbm, probs_ref), (na_hbm, na_ref),
        ))
    ]
    for i in (7, 8, 0, 1, 9, 10, 2, 3, 5, 11, 12, 4, 13, 6):
        local[i].start()
    loads[0].start()
    picks[z] = pick_ref[...]

    barrier = pltpu.get_barrier_semaphore()
    for e in others:
        pl.semaphore_signal(barrier, inc=1, device_id={"fsdp": flipped(e)}, device_id_type=MESH)
    for s in steps:
        pl.semaphore_signal(barrier, inc=1, device_id={"rep": along(s)}, device_id_type=MESH)
    pl.semaphore_wait(barrier, 10)

    for copy in ups:
        copy.start()
    for c in range(4):
        local[c].wait()
    for c in range(DEPTH):
        line.begin(c)
    local[5].wait()
    for p in (3, 2, 1):
        branch_sum.leave(p)
    send_picks = [remote_z(picks.at[z], picks.at[z], pk_send.at[s], pk_recv.at[s], along(s)) for s in steps]
    for copy in send_picks:
        copy.start()

    image = image_of(lax.broadcasted_iota(jnp.int32, (rows, 1), 0), sizes_ref)
    selectors = [jnp.where(image == j, 1.0, 0.0) for j in range(slots)]
    slot = lax.broadcasted_iota(jnp.int32, (8, rows), 0)
    where = image_of(lax.broadcasted_iota(jnp.int32, (8, rows), 1), sizes_ref)
    gather_rows = (jnp.where((where == slot) & (slot < slots), 1.0, 0.0), jnp.where((where == slot - slots) & (where < slots), 1.0, 0.0))
    modrow[...] = jnp.zeros_like(modrow)

    def to_slots(index, values):
        modrow[:, (index % 3) * width : (index % 3 + 1) * width] += lax.dot_general(
            gather_rows[index // 3], values, (((1,), (0,)), ((), ())), precision=lax.Precision.HIGHEST, preferred_element_type=F32
        )

    cot = cot_ref[...].astype(F32)
    local[7].wait()
    local[8].wait()
    back, grad_scale = norm_back(mid_ref[...], per_row(selectors, mod_ref, 4, width), gin_ref[...])
    to_slots(3, gin_ref[...])
    to_slots(4, grad_scale)
    gm = cot + back
    to_slots(2, gm * gm_ref[...])
    gm_ref[...] = gm
    gba = (per_row(selectors, mod_ref, 2, width) * gm).astype(BF16)
    gba_ref[...] = gba
    bias_z[0] = jnp.zeros(bias_z.shape[1:], F32)
    bias_z[0, 2:3] = jnp.sum(gba.astype(F32), axis=0, keepdims=True)
    gbb = (per_row(selectors, mod_ref, 5, width) * cot).astype(BF16)
    bias_z[0, 3:4] = jnp.sum(gbb.astype(F32), axis=0, keepdims=True)
    bias_z[0, 4:5, : gbup_ref.shape[1]] = gbup_ref[...]
    local[9].wait()
    gatt_ref[...] = nt(gba_ref[...], wo_all[...].reshape(width, width)).astype(BF16)
    local[10].wait()
    blocks[0] = tn(att_ref[...], gba_ref[...]).astype(BF16).reshape(8, part, width)
    planes[0].pair()
    line.tick(0)

    gp_ref[...] = jnp.zeros_like(gp_ref)
    rate = head_dim ** (-0.5)

    def head_back(head):
        base, window, mask = head_window(head, head_dim)
        mask = mask.astype(BF16)
        at = [pl.ds(i * width + base, window) for i in range(3)]
        query, key, value = proj_ref[:, at[0]] * mask, proj_ref[:, at[1]] * mask, proj_ref[:, at[2]]
        grad = gatt_ref[:, at[0]] * mask
        low = probs_ref[head]
        probs = low.astype(F32)
        grad_probs = nt(grad, value)
        delta = jnp.sum(probs * grad_probs, axis=-1, keepdims=True)
        grad_scores = (probs * (grad_probs - delta)).astype(BF16)
        gp_ref[:, at[0]] += (nn(grad_scores, key) * rate).astype(BF16)
        gp_ref[:, at[1]] += (tn(grad_scores, query) * rate).astype(BF16)
        gp_ref[:, at[2]] += tn(low, grad).astype(BF16)

    local[11].wait()
    local[12].wait()
    for head in range(3):
        head_back(head)
    planes[0].combine()
    for head in range(3, 10):
        head_back(head)
    line.tick(1)
    for head in range(10, 16):
        head_back(head)
    local[4].wait()
    for copy in ups:
        copy.wait_recv()
    lap = gup_in.shape[2] - hid
    for c in range(4):
        left, right = gup_in[2 * c], gup_in[2 * c + 1]
        zbuf[4 + c, :, : hid - lap] = left[:, : hid - lap]
        zbuf[4 + c, :, hid - lap : hid + lap] = left[:, hid - lap :] + right[:, : 2 * lap]
        zbuf[4 + c, :, hid + lap :] = right[:, 2 * lap :]
    line.begin(4)
    line.begin(5)
    line.tick(2)

    def spread(i):
        blocks[i] = tn(na_ref[...], gp_ref[:, (i - 1) * width : i * width]).astype(BF16).reshape(8, part, width)
        planes[i].pair()

    def settle(i):
        zbuf[8 + i] = planes[i].total().astype(BF16)
        line.begin(8 + i)

    branch_sum.relay()
    local[13].wait()
    spread(1)
    spread(2)
    spread(3)
    for i in range(3):
        loads[i].wait()
        term = nt(gp_ref[:, i * width : (i + 1) * width], wq_buf[...].reshape(width, width))
        gin_ref[...] = term if i == 0 else gin_ref[...] + term
        if i < 2:
            loads[i + 1].start()
    gna = gin_ref[...]
    for i, c in ((0, 0), (2, 1)):
        bias_z[0, c : c + 1] = jnp.sum(gp_ref[:, i * width : (i + 1) * width].astype(F32), axis=0, keepdims=True)
    send_bias = [remote_z(bias_z.at[0], bias_z.at[s], bz_send.at[s], bz_recv.at[s], along(s)) for s in steps]
    for copy in send_bias:
        copy.start()
    back, grad_scale = norm_back(tok_ref[...].astype(F32), per_row(selectors, mod_ref, 1, width), gna)
    to_slots(0, gna)
    to_slots(1, grad_scale)
    gin_ref[...] = gm_ref[...] + back
    line.begin(6)
    line.tick(3)
    planes[0].relay()
    planes[1].combine()
    line.begin(7)
    line.tick(4)
    planes[2].combine()
    line.tick(5)
    branch = branch_sum.total()
    branch = branch + mod_ref[slots : slots + 1, 3 * width : 4 * width]
    out_ref[...] = (mid_ref[...] + per_row(selectors, mod_ref, 5, width) * branch).astype(BF16)
    to_slots(5, cot_ref[...].astype(F32) * branch)
    mine = mods.at[me, pl.ds(pl.multiple_of(8 * z, 8), 8)]
    mine[...] = modrow[...].astype(BF16)
    send_mods = [remote_z(mine, mine, mz_send.at[s], mz_recv.at[s], along(s)) for s in steps]
    for copy in send_mods:
        copy.start()
    planes[1].relay()
    planes[3].combine()
    settle(0)
    line.tick(6)
    planes[2].relay()
    settle(1)
    line.tick(7)
    planes[3].relay()
    settle(2)
    line.tick(8)
    settle(3)
    line.tick(9)
    for copy in send_mods + send_bias:
        copy.wait_recv()
    gather = Gather(lambda j: mods.at[j], mods.shape[1], md_send, md_recv, mods.shape[1] // 2)
    gather.own()
    total = bias_z[0] + bias_z[1] + bias_z[2] + bias_z[3]
    gbup_out[...] = total[4:5, : gbup_out.shape[1]]
    bias_in[me] = total
    send_total = [remote(bias_in.at[me], bias_in.at[me], bi_send.at[e], bi_recv.at[e], e) for e in others]
    for copy in send_total:
        copy.start()
    line.tick(10)
    gather.along()
    line.tick(11)
    gather.across()
    gather.finish()
    local[6].wait()
    plane_rows = mods[:, pl.ds(pl.multiple_of(8 * z, 8), 8), :].reshape(64, mods.shape[2])
    half = mods.shape[2]
    first, second = nt(plane_rows, wada_ref[:, :half]), nt(plane_rows, wada_ref[:, half:])
    upper = lax.rem(lax.broadcasted_iota(jnp.int32, (64, 1), 0), 8) < slots
    gc_out[...] = jnp.where(upper, first, second).reshape(gc_out.shape)
    send_gc = [remote(gc_out.at[flipped(e)], gc_in.at[me], gc_send.at[e], gc_recv.at[e], e) for e in others]
    for copy in send_gc:
        copy.start()
    gc_in[me] = gc_out[me]
    line.tick(12)
    for copy in send_total:
        copy.wait_recv()
    total = bias_in[0]
    for j in others:
        total = total + bias_in[j]
    bias_ref[...] = total
    line.tick(13)
    for copy in send_gc + send_picks:
        copy.wait_recv()
    line.end()
    for copy in ups + send_picks + send_bias + send_mods + send_total + send_gc:
        copy.wait_send()
    for plane in planes + [branch_sum]:
        plane.drain()
    gather.drain()


def backward(sizes, tok, cot, mod, mid, gbup, pick, na, proj, probs, att, wo, bra, gnb, bbs, gdn, gup, wq, wada):
    rows, width = tok.shape
    part, columns = wada.shape
    wide = gdn.shape[0]
    S, V = jax.ShapeDtypeStruct, pltpu.VMEM
    vm, hbm = pl.BlockSpec(memory_space=pltpu.VMEM), pl.BlockSpec(memory_space=pl.ANY)
    dma = pltpu.SemaphoreType.DMA
    shapes = (
        S((rows, width), BF16), S((rows, width), F32), S((12, part, width), BF16), S((8, 32, columns // 2), BF16),
        S((8, 8, part), F32), S((4, 64, part), BF16), S((8, width), F32), S((1, wide), F32),
    )
    return pl.pallas_call(
        back_kernel,
        out_shape=shapes,
        in_specs=[pl.BlockSpec(memory_space=pltpu.SMEM)] + [vm] * 6 + [hbm] * 12,
        out_specs=(vm,) * len(shapes),
        scratch_shapes=[
            V((rows, width), BF16), V((rows, 3 * width), BF16), V((H, rows, rows), BF16), V((rows, width), BF16), V((8, part, width), BF16),
            V((8, part, wide), BF16), V((4, rows, width), BF16), V((rows, width), BF16), V((2, rows, width), BF16), V((12, part, width), BF16), V((12, lead(part), width), BF16),
            V((rows, width), F32), V((rows, width), BF16), V((rows, width), BF16), V((rows, 3 * width), BF16),
            V((4, 8, part, width), BF16), V((4, 4, part, width), BF16), V((4, lead(part), width), BF16), V((4, part - lead(part), width), BF16),
            V((4, part, width), BF16), V((4, part, width), BF16), V((8, part, width), BF16), V((part, columns), BF16),
            V((8, columns // 2), F32), V((4, 8, width), F32), V((8, 8, width), F32), V((8, 8, part), F32),
            dma((17,)), dma((8,)), dma((8,)), dma((6,)), dma((6,)), dma((5, 12)), dma((5, 12)), dma((4, 4)), dma((4, 4)),
            dma((4, 6)), dma((4, 6)), dma((8,)), dma((8,)), dma((4,)), dma((4,)), dma((4,)), dma((4,)), dma((4,)), dma((4,)),
            dma((8,)), dma((8,)), dma((8,)), dma((8,)),
        ],
        compiler_params=pltpu.CompilerParams(collective_id=2, has_side_effects=True, vmem_limit_bytes=62 << 20),
    )(sizes, tok, cot, mod, mid, gbup, pick, na, proj, probs, att, wo, bra, gnb, bbs, gdn, gup, wq, wada)

def finish_kernel(
    picks_ref, gc_ref, bias_ref, gbup_ref, cond_ref, sums_hbm, mods_hbm, out_hbm, gin_hbm,
    gcond_ref, gada_hbm, gbada_ref, gqkv_hbm, gbqkv_ref, gout_hbm, gbout_ref, gup_hbm, gbup_out, gdown_hbm, gbdown_ref,
    out_final, gin_final,
    sums_ref, mods_ref, gada_ref, gqkv_ref, gout_ref, gup_ref, gdown_ref, lanes, out_ref, gin_ref, sem,
):
    pairs = (
        (sums_hbm.at[pl.ds(0, 4)], sums_ref.at[pl.ds(0, 4)]), (sums_hbm.at[pl.ds(4, 4)], sums_ref.at[pl.ds(4, 4)]),
        (sums_hbm.at[pl.ds(8, 4)], sums_ref.at[pl.ds(8, 4)]), (mods_hbm, mods_ref), (out_hbm, out_ref), (gin_hbm, gin_ref),
        (gdown_ref, gdown_hbm), (gup_ref, gup_hbm), (gout_ref, gout_hbm), (gqkv_ref, gqkv_hbm), (gada_ref, gada_hbm),
        (out_ref, out_final), (gin_ref, gin_final),
    )
    copies = [pltpu.make_async_copy(src, dst, sem.at[i]) for i, (src, dst) in enumerate(pairs)]
    for copy in copies[:6]:
        copy.start()
    slots, width = cond_ref.shape
    part = width // 8
    half = mods_ref.shape[2]
    me, z = lax.axis_index("fsdp"), lax.axis_index("rep")
    copies[0].wait()
    for c in range(4):
        gdown_ref[c * part : (c + 1) * part] = sums_ref[c].astype(F32)
    copies[6].start()
    copies[1].wait()
    for c in range(4):
        gup_ref[:, c * width : (c + 1) * width] = sums_ref[4 + c].astype(F32)
    copies[7].start()
    copies[2].wait()
    gout_ref[...] = sums_ref[8].astype(F32)
    copies[8].start()
    copies[4].wait()
    copies[11].start()
    copies[5].wait()
    copies[12].start()
    for c in range(3):
        gqkv_ref[:, c * width : (c + 1) * width] = sums_ref[9 + c].astype(F32)
    copies[9].start()
    copies[3].wait()
    rows = mods_ref[...].reshape(256, half)
    acts = jnp.stack([picks_ref[i] for i in range(4)], axis=0).reshape(4, 8, 8, part)
    acts = jnp.stack([acts[:, f] for f in range(8)], axis=0).reshape(256, part).astype(F32)
    upper = lax.rem(lax.broadcasted_iota(jnp.int32, (256, 1), 0), 8) < slots
    first, second = jnp.where(upper, acts, 0.0).astype(BF16), jnp.where(upper, 0.0, acts).astype(BF16)
    gada_ref[:, :half] = tn(first, rows)
    gada_ref[:, half:] = tn(second, rows)
    copies[10].start()
    floats = rows.astype(F32)
    lanes[...] = jnp.zeros_like(lanes)

    def own(row, size):
        total = row.shape[1]
        lanes[0:1, :total] = row
        return pltpu.roll(lanes[:, :total], lax.rem(total - me * size, total), 1)[0, :size]

    column = jnp.concatenate(
        [
            jnp.sum(jnp.where(upper, floats, 0.0), axis=0, keepdims=True),
            jnp.sum(jnp.where(upper, 0.0, floats), axis=0, keepdims=True),
        ],
        axis=1,
    )
    gbada_ref[...] = own(column, gbada_ref.shape[0])
    gbqkv_ref[...] = own(jnp.concatenate([bias_ref[0:1], bias_ref[1:2]], axis=1), gbqkv_ref.shape[0])
    gbout_ref[...] = own(bias_ref[2:3], part)
    gbdown_ref[...] = own(bias_ref[3:4], part)
    wide, hid = gbup_ref.shape[1], gbup_out.shape[0]
    lanes[0:1, :wide] = gbup_ref[...]
    gbup_out[...] = pltpu.roll(lanes[:, :wide], lax.rem(wide - lax.rem(me, 2) * (wide - hid), wide), 1)[0, :hid]
    grad = None
    for j in range(8):
        lanes[:, :width] = jnp.zeros((8, width), F32)
        lanes[0:slots, :part] = gc_ref[j, 0:slots] + gc_ref[j, slots : 2 * slots]
        term = pltpu.roll(lanes[:, :width], j * part, 1) if j else lanes[:, :width]
        grad = term if grad is None else grad + term
    cond = cond_ref[...].astype(F32)
    gate = jax.nn.sigmoid(cond)
    gcond_ref[...] = grad[0:slots] * (gate * (1.0 + cond * (1.0 - gate)))
    for copy in copies[6:]:
        copy.wait()


def finish(output, grad_input, sums, mods, picks, gc, bias, gbup, cond, sizes):
    S, V = jax.ShapeDtypeStruct, pltpu.VMEM
    vm, hbm = pl.BlockSpec(memory_space=pltpu.VMEM), pl.BlockSpec(memory_space=pl.ANY)
    large = (1, 3, 5, 7, 9)
    shapes = tuple(S(size, F32) for size in sizes) + (S(output.shape, output.dtype), S(grad_input.shape, F32))
    specs = tuple(hbm if i in large or i >= len(sizes) else vm for i in range(len(shapes)))
    *grads, output, grad_input = pl.pallas_call(
        finish_kernel,
        out_shape=shapes,
        in_specs=[vm] * 5 + [hbm] * 4,
        out_specs=specs,
        scratch_shapes=[V(sums.shape, BF16), V(mods.shape, BF16)] + [V(sizes[i], F32) for i in large] + [
            V((8, 2 * mods.shape[2]), F32), V(output.shape, output.dtype), V(grad_input.shape, F32), pltpu.SemaphoreType.DMA((13,)),
        ],
        compiler_params=pltpu.CompilerParams(vmem_limit_bytes=56 << 20),
    )(picks, gc, bias, gbup, cond, sums, mods, output, grad_input)
    return (output, grad_input, *grads)

def fast(tokens, cond, image_sizes, w_ada, b_ada, w_qkv, b_qkv, w_out, b_out, w_up, b_up, w_down, b_down, cotangent):
    width = tokens.shape[1]
    part, columns = w_ada.shape
    mod, gnb, gbup, pick, na, proj, probs, att, bra, mid, wq, wo, bbs, gdn, gup = front(
        image_sizes, tokens, cotangent, cond, w_ada, b_ada, b_qkv, b_out, b_down, b_up,
        w_qkv, w_out, w_up, w_down,
    )
    wq, wo = wq.reshape(8, 3 * part, width), wo.reshape(8, part, width)
    output, grad_input, sums, mods, gc, picks, bias, gbup = backward(
        image_sizes, tokens, cotangent, mod, mid, gbup, pick, na, proj, probs, att, wo, bra, gnb, bbs, gdn, gup, wq, w_ada
    )
    sizes = tuple(
        leaf.shape for leaf in (cond, w_ada, b_ada, w_qkv, b_qkv, w_out, b_out, w_up, b_up, w_down, b_down)
    )
    return finish(output, grad_input, sums, mods, picks, gc, bias, gbup, cond, sizes)


def solution(mesh):
    placed = (
        P(("fsdp", "rep"), None),
        P(("fsdp", "rep"), None),
        P(("fsdp", "rep")),
        P("fsdp", None),
        P("fsdp"),
        P("fsdp", None),
        P("fsdp"),
        P("fsdp", None),
        P("fsdp"),
        P("fsdp", None),
        P("fsdp"),
        P("fsdp", None),
        P("fsdp"),
        P(("fsdp", "rep"), None),
    )
    fits = mesh.shape["fsdp"] == 8 and mesh.shape["rep"] == 4
    return jax.shard_map(
        fast if fits else local,
        mesh=mesh,
        in_specs=placed,
        out_specs=(
            P(("fsdp", "rep"), None),
            P(("fsdp", "rep"), None),
            P(("fsdp", "rep"), None),
            P("fsdp", None),
            P("fsdp"),
            P("fsdp", None),
            P("fsdp"),
            P("fsdp", None),
            P("fsdp"),
            P("fsdp", None),
            P("fsdp"),
            P("fsdp", None),
            P("fsdp"),
        ),
        check_vma=False,
    )
```

```python
import functools

import jax
import jax.numpy as jnp
from jax import lax
from jax.experimental import pallas as pl
from jax.experimental.pallas import tpu as pltpu
from jax.sharding import PartitionSpec as P

H = 16
EPSILON = 1e-06
HIGHEST = lax.Precision.HIGHEST
MASKED = -1e30


def layer_norm(inputs):
    average = jnp.mean(inputs, axis=-1, keepdims=True)
    centered = inputs - average
    variance = jnp.mean(centered * centered, axis=-1, keepdims=True)
    return centered * lax.rsqrt(variance + EPSILON)


def modulate(hidden, shift_part, scale_part):
    return layer_norm(hidden) * (1.0 + scale_part) + shift_part


def gelu_tanh(inputs):
    return jax.nn.gelu(inputs, approximate=True)


def product(first_operand, second_operand):
    return jnp.dot(first_operand, second_operand, preferred_element_type=jnp.float32)


def product_back(first_operand, second_operand):
    return lax.dot_general(
        first_operand, second_operand, (((1,), (1,)), ((), ())), preferred_element_type=jnp.float32
    )


def outer_sum(first_operand, second_operand):
    return lax.dot_general(
        first_operand, second_operand, (((0,), (0,)), ((), ())), preferred_element_type=jnp.float32
    )


def fetch_forward(weight, bias_piece):
    return (
        lax.all_gather(weight, "fsdp", axis=0, tiled=True),
        lax.all_gather(bias_piece, "fsdp", axis=0, tiled=True),
    )


def weights_again(weight):
    return lax.all_gather(weight, "fsdp", axis=0, tiled=True)


def reduce_grads(weight_grad, bias_grad):
    row_part, bias_part = (
        lax.psum_scatter(weight_grad, "fsdp", scatter_dimension=0, tiled=True),
        lax.psum_scatter(bias_grad, "fsdp", scatter_dimension=0, tiled=True),
    )
    column_part = lax.psum_scatter(row_part, "rep", scatter_dimension=1, tiled=True)
    whole_rows, bias_stack = (
        lax.all_gather(column_part, "rep", axis=1, tiled=True),
        lax.all_gather(bias_part[None], "rep", axis=0, tiled=True),
    )
    return (whole_rows, jnp.sum(bias_stack, axis=0))


def local(
    tokens,
    cond,
    image_sizes,
    w_ada,
    b_ada,
    w_qkv,
    b_qkv,
    w_out,
    b_out,
    w_up,
    b_up,
    w_down,
    b_down,
    cotangent,
):
    row_count, model_width = tokens.shape
    head_count = H
    head_dim = model_width // head_count
    slot_count = image_sizes.shape[0]
    scale_factor = head_dim ** (-0.5)
    block_rows = min(512, row_count)
    block_count = row_count // block_rows
    image_ends = jnp.sum(
        jnp.where(jnp.arange(slot_count)[:, None] >= jnp.arange(slot_count)[None, :], image_sizes[None, :], 0), axis=1
    )
    positions = jnp.arange(row_count, dtype=jnp.int32)
    image_ids = jnp.sum((positions[:, None] >= image_ends[None, :]).astype(jnp.int32), axis=1)
    selector = (image_ids[:, None] == jnp.arange(slot_count, dtype=jnp.int32)[None, :]).astype(
        jnp.float32
    )
    cond_float = cond.astype(jnp.float32)
    activ_float, silu_pull = jax.vjp(jax.nn.silu, cond_float)
    activ_low = activ_float.astype(jnp.bfloat16)
    full_ada, full_bada = fetch_forward(w_ada, b_ada)
    modulation = product(activ_low, full_ada) + full_bada.astype(jnp.float32)
    per_token = jnp.dot(selector, modulation, precision=HIGHEST)
    shift_a, scale_a, gate_a, shift_b, scale_b, gate_b = jnp.split(per_token, 6, axis=1)
    hidden = tokens.astype(jnp.float32)
    normed_a, pull_a = jax.vjp(modulate, hidden, shift_a, scale_a)
    normed_a_low = normed_a.astype(jnp.bfloat16)
    full_qkv, full_bqkv = fetch_forward(w_qkv, b_qkv)
    bias_qkv = full_bqkv.astype(jnp.float32)
    bias_full = jnp.concatenate(
        [bias_qkv[:model_width], jnp.zeros((model_width,), jnp.float32), bias_qkv[model_width:]]
    )
    projected = (product(normed_a_low, full_qkv) + bias_full).astype(jnp.bfloat16)
    query_heads = projected[:, :model_width].reshape(row_count, head_count, head_dim)
    key_heads = projected[:, model_width : 2 * model_width].reshape(row_count, head_count, head_dim)
    value_heads = projected[:, 2 * model_width :].reshape(row_count, head_count, head_dim)
    query_blocks = query_heads.reshape(block_count, block_rows, head_count, head_dim)
    id_blocks = image_ids.reshape(block_count, block_rows)

    def scores_of(query_block, id_block):
        raw_scores = (
            jnp.einsum("qhd,khd->hqk", query_block, key_heads, preferred_element_type=jnp.float32)
            * scale_factor
        )
        same_image = id_block[:, None] == image_ids[None, :]
        return jnp.where(same_image[None], raw_scores, MASKED)

    def forward_block(block_item):
        query_block, id_block = block_item
        scores = scores_of(query_block, id_block)
        row_max = jnp.max(scores, axis=-1, keepdims=True)
        exponent = jnp.exp(scores - row_max)
        row_total = jnp.sum(exponent, axis=-1, keepdims=True)
        probabilities = (exponent / row_total).astype(jnp.bfloat16)
        attended_block = jnp.einsum(
            "hqk,khd->qhd", probabilities, value_heads, preferred_element_type=jnp.float32
        )
        return (attended_block.astype(jnp.bfloat16), (row_max + jnp.log(row_total))[:, :, 0])

    attended_blocks, lse_blocks = lax.map(forward_block, (query_blocks, id_blocks))
    attended = attended_blocks.reshape(row_count, model_width)
    full_out, full_bout = fetch_forward(w_out, b_out)
    branch_a = product(attended, full_out) + full_bout.astype(jnp.float32)
    middle = hidden + gate_a * branch_a
    normed_b, pull_b = jax.vjp(modulate, middle, shift_b, scale_b)
    normed_b_low = normed_b.astype(jnp.bfloat16)
    full_up, full_bup = fetch_forward(w_up, b_up)
    inner_pre = product(normed_b_low, full_up) + full_bup.astype(jnp.float32)
    activated, gelu_pull = jax.vjp(gelu_tanh, inner_pre)
    activated_low = activated.astype(jnp.bfloat16)
    full_down, full_bdown = fetch_forward(w_down, b_down)
    branch_b = product(activated_low, full_down) + full_bdown.astype(jnp.float32)
    output = (middle + gate_b * branch_b).astype(jnp.bfloat16)
    grad_out = cotangent.astype(jnp.float32)
    grad_gate_b = grad_out * branch_b
    grad_branch_b = (gate_b * grad_out).astype(jnp.bfloat16)
    grad_w_down, grad_b_down = reduce_grads(
        outer_sum(activated_low, grad_branch_b), jnp.sum(grad_branch_b.astype(jnp.float32), axis=0)
    )
    back_down = weights_again(w_down)
    grad_activated = product_back(grad_branch_b, back_down)
    (grad_inner,) = gelu_pull(grad_activated)
    grad_inner_low = grad_inner.astype(jnp.bfloat16)
    grad_w_up, grad_b_up = reduce_grads(
        outer_sum(normed_b_low, grad_inner_low), jnp.sum(grad_inner_low.astype(jnp.float32), axis=0)
    )
    back_up = weights_again(w_up)
    grad_normed_b = product_back(grad_inner_low, back_up)
    grad_middle_norm, grad_shift_b, grad_scale_b = pull_b(grad_normed_b)
    grad_middle = grad_out + grad_middle_norm
    grad_gate_a = grad_middle * branch_a
    grad_branch_a = (gate_a * grad_middle).astype(jnp.bfloat16)
    grad_w_out, grad_b_out = reduce_grads(
        outer_sum(attended, grad_branch_a), jnp.sum(grad_branch_a.astype(jnp.float32), axis=0)
    )
    back_out = weights_again(w_out)
    grad_attended = product_back(grad_branch_a, back_out).astype(jnp.bfloat16)
    grad_att_blocks = grad_attended.reshape(block_count, block_rows, head_count, head_dim)

    def backward_block(carried, block_item):
        key_grad, value_grad = carried
        query_block, id_block, grad_block, lse_block = block_item
        scores = scores_of(query_block, id_block)
        probabilities = jnp.exp(scores - lse_block[:, :, None])
        probabilities_low = probabilities.astype(jnp.bfloat16)
        grad_probs = jnp.einsum(
            "qhd,khd->hqk", grad_block, value_heads, preferred_element_type=jnp.float32
        )
        row_delta = jnp.sum(probabilities * grad_probs, axis=-1, keepdims=True)
        grad_scores = (probabilities * (grad_probs - row_delta)).astype(jnp.bfloat16)
        query_grad = (
            jnp.einsum("hqk,khd->qhd", grad_scores, key_heads, preferred_element_type=jnp.float32)
            * scale_factor
        )
        key_grad = (
            key_grad
            + jnp.einsum(
                "hqk,qhd->khd", grad_scores, query_block, preferred_element_type=jnp.float32
            )
            * scale_factor
        )
        value_grad = value_grad + jnp.einsum(
            "hqk,qhd->khd", probabilities_low, grad_block, preferred_element_type=jnp.float32
        )
        return ((key_grad, value_grad), query_grad)

    zero_heads = jnp.zeros((row_count, head_count, head_dim), jnp.float32)
    (grad_keys, grad_values), grad_query_blocks = lax.scan(
        backward_block,
        (zero_heads, zero_heads),
        (query_blocks, id_blocks, grad_att_blocks, lse_blocks),
    )
    grad_projected = jnp.concatenate(
        [
            grad_query_blocks.reshape(row_count, model_width),
            grad_keys.reshape(row_count, model_width),
            grad_values.reshape(row_count, model_width),
        ],
        axis=1,
    ).astype(jnp.bfloat16)
    column_sums = jnp.sum(grad_projected.astype(jnp.float32), axis=0)
    grad_bias_qkv = jnp.concatenate([column_sums[:model_width], column_sums[2 * model_width :]])
    grad_w_qkv, grad_b_qkv = reduce_grads(outer_sum(normed_a_low, grad_projected), grad_bias_qkv)
    back_qkv = weights_again(w_qkv)
    grad_normed_a = product_back(grad_projected, back_qkv)
    grad_hidden_norm, grad_shift_a, grad_scale_a = pull_a(grad_normed_a)
    grad_input = grad_middle + grad_hidden_norm
    grad_per_token = jnp.concatenate(
        [grad_shift_a, grad_scale_a, grad_gate_a, grad_shift_b, grad_scale_b, grad_gate_b], axis=1
    )
    grad_modulation = lax.dot_general(
        selector, grad_per_token, (((0,), (0,)), ((), ())), precision=HIGHEST
    ).astype(jnp.bfloat16)
    grad_w_ada, grad_b_ada = reduce_grads(
        outer_sum(activ_low, grad_modulation), jnp.sum(grad_modulation.astype(jnp.float32), axis=0)
    )
    back_ada = weights_again(w_ada)
    grad_activ = product_back(grad_modulation, back_ada)
    (grad_cond,) = silu_pull(grad_activ)
    return (
        output,
        grad_input,
        grad_cond,
        grad_w_ada,
        grad_b_ada,
        grad_w_qkv,
        grad_b_qkv,
        grad_w_out,
        grad_b_out,
        grad_w_up,
        grad_b_up,
        grad_w_down,
        grad_b_down,
    )


MESH = pl.DeviceIdType.MESH
F32, BF16 = jnp.float32, jnp.bfloat16


def flipped(offset):
    index = lax.axis_index("fsdp")
    y, x, core = index // 4, (index // 2) % 2, index % 2
    y = 1 - y if offset & 4 else y
    x = 1 - x if offset & 2 else x
    core = 1 - core if offset & 1 else core
    return y * 4 + x * 2 + core


def greet(offsets):
    barrier = pltpu.get_barrier_semaphore()
    for offset in offsets:
        pl.semaphore_signal(barrier, inc=1, device_id={"fsdp": flipped(offset)}, device_id_type=MESH)
    pl.semaphore_wait(barrier, len(offsets))


def remote(src, dst, send, recv, offset):
    return pltpu.make_async_remote_copy(
        src_ref=src, dst_ref=dst, send_sem=send, recv_sem=recv,
        device_id={"fsdp": flipped(offset)}, device_id_type=MESH,
    )


def lead(rows):
    return -(-rows // 32) * 16


class Gather:
    def __init__(self, shard, rows, send, recv, lead):
        first, second = pl.ds(0, lead), pl.ds(lead, rows - lead)
        piece = {e: shard(flipped(e)) for e in (0, 2, 4, 6)}
        plan = (
            (piece[0], 1), (piece[0], 2), (piece[0], 4),
            (piece[2].at[first], 4), (piece[4].at[second], 2),
            (piece[2], 1), (piece[4], 1), (piece[6], 1),
        )
        self.copies = [remote(ref, ref, send.at[i], recv.at[i], e) for i, (ref, e) in enumerate(plan)]

    def own(self):
        for i in (1, 2, 0):
            self.copies[i].start()

    def along(self):
        self.copies[1].wait_recv()
        self.copies[3].start()
        self.copies[5].start()
        self.copies[2].wait_recv()
        self.copies[4].start()
        self.copies[6].start()

    def across(self):
        self.copies[3].wait_recv()
        self.copies[4].wait_recv()
        self.copies[7].start()

    def sibling(self, p):
        self.copies[(0, 5, 6, 7)[p]].wait_recv()

    def finish(self):
        for p in range(4):
            self.sibling(p)

    def drain(self):
        for copy in self.copies:
            copy.wait_send()


class PlaneSum:
    def __init__(self, held, odd, pair_in, cross_a, cross_b, from_x, from_y, pair_send, pair_recv, send, recv, rows, lead):
        self.a, self.b = a, b = pl.ds(0, lead), pl.ds(lead, rows - lead)
        self.held, self.pair_in, self.cross_a, self.cross_b = held, pair_in, cross_a, cross_b
        self.from_x, self.from_y = from_x, from_y
        self.pairs = [] if odd is None else [
            remote(odd[p], pair_in[p], pair_send.at[p], pair_recv.at[p], 1) for p in range(4)
        ]
        plan = (
            (held[3].at[a], cross_a, 2), (held[3].at[b], cross_b, 4),
            (held[2].at[b], from_y.at[b], 4), (held[1].at[a], from_x.at[a], 2),
            (held[2].at[a], from_y.at[a], 4), (held[1].at[b], from_x.at[b], 2),
        )
        self.copies = [remote(src, dst, send.at[i], recv.at[i], e) for i, (src, dst, e) in enumerate(plan)]

    def pair(self):
        for p in (3, 2, 1, 0):
            self.pairs[p].start()

    def leave(self, p):
        if p == 3:
            self.copies[0].start()
            self.copies[1].start()
        elif p:
            self.copies[(None, 3, 2)[p]].start()

    def join(self, p):
        self.pairs[p].wait_recv()
        self.held[p][...] += self.pair_in[p][...]
        self.leave(p)

    def combine(self):
        for p in (3, 2, 1, 0):
            self.join(p)

    def relay(self):
        for i, p, part, came in ((0, 2, self.a, self.cross_a), (1, 1, self.b, self.cross_b)):
            self.copies[i].wait_recv()
            ref = self.held[p].at[part]
            ref[...] += came[...]
            self.copies[4 + i].start()

    def total(self):
        for i in (2, 3, 4, 5):
            self.copies[i].wait_recv()
        return self.held[0][...].astype(F32) + self.from_x[...].astype(F32) + self.from_y[...].astype(F32)

    def drain(self):
        for copy in self.pairs + self.copies:
            copy.wait_send()


def nt(a, b):
    return lax.dot_general(a, b, (((1,), (1,)), ((), ())), preferred_element_type=F32)


def tn(a, b):
    return lax.dot_general(a, b, (((0,), (0,)), ((), ())), preferred_element_type=F32)


def nn(a, b):
    return jnp.dot(a, b, preferred_element_type=F32)


def normalized(values):
    centered = values - jnp.mean(values, axis=-1, keepdims=True)
    variance = jnp.mean(centered * centered, axis=-1, keepdims=True)
    scale = lax.rsqrt(variance + EPSILON)
    return centered * scale, scale


def image_of(place, sizes_ref):
    end = jnp.int32(0)
    image = jnp.zeros(place.shape, jnp.int32)
    for j in range(sizes_ref.shape[0]):
        end = end + sizes_ref[j]
        image = image + (place >= end).astype(jnp.int32)
    return image


def per_row(selectors, modulation, part, width):
    total = None
    for j, chosen in enumerate(selectors):
        term = chosen * modulation[j : j + 1, part * width : (part + 1) * width]
        total = term if total is None else total + term
    return total


def head_window(head, head_dim):
    low = head * head_dim
    base = low // 128 * 128
    wide = 128 if low - base + head_dim <= 128 else 256
    lane = lax.broadcasted_iota(jnp.int32, (1, wide), 1) + (base - low)
    mask = jnp.where((lane >= 0) & (lane < head_dim), 1.0, 0.0)
    return base, wide, mask


GELU_RATE = 0.7978845608028654
GELU_CUBE = 0.044715


def gelu_parts(u):
    square = u * u
    bend = jnp.tanh(GELU_RATE * u * (1.0 + GELU_CUBE * square))
    half = 0.5 * (1.0 + bend)
    slope = half + 0.5 * u * (1.0 - bend * bend) * (GELU_RATE * (1.0 + 3.0 * GELU_CUBE * square))
    return u * half, slope


def front_kernel(
    sizes_ref, tok_ref, cot_ref, cond_ref, wada_ref, bada_ref, bqkv_ref, bout_ref, bdown_ref, bup_in,
    wqkv_hbm, wout_hbm, wup_hbm, wdn_hbm,
    mod_ref, gnb_ref, gbup_ref, pick_ref, na_hbm, proj_hbm, probs_hbm, att_hbm, bra_hbm, mid_hbm, wq_hbm, wo_hbm,
    bb_hbm, gdn_hbm, gup_hbm,
    na_ref, proj_ref, probs_ref, att_ref, bra_ref, mid_ref, arena, wo_all, bb_ref, gdn_ref, gup_ref,
    cond_all, pm, mpair, mfar, mlow, lay, lay_b, nb_all, gbb_all, wup_all, wdn_ref, act_all, gi_all, in_pair, cross_a, cross_b, from_x, from_y,
    loc_sem, save_sem, c_send, c_recv, mp_send, mp_recv, mf_send, mf_recv, up_send, up_recv,
    q_send, q_recv, o_send, o_recv, g_send, g_recv, n_send, n_recv, pr_send, pr_recv, far_send, far_recv,
):
    rows, width = tok_ref.shape
    head_dim = width // H
    slots = sizes_ref.shape[0]
    part = wada_ref.shape[0]
    own, wide = wdn_hbm.shape[0], wup_all.shape[1]
    me = flipped(0)
    others = range(1, 8)

    def strip(ref, size):
        return lambda j: ref.at[pl.ds(pl.multiple_of(j * size, 8), size)]

    def up_piece(e):
        j = flipped(e)
        begin = pl.multiple_of(2 * own * (j // 2) + (2 * own - wide) * (j % 2), 128)
        return wup_hbm.at[:, pl.ds(begin, wide)]

    shift = lax.rem(me, 2) * (wide - own)
    blank = lax.rem(me + 1, 2) * own
    wq_strip, wup_strip = strip(arena, 3 * part), strip(wup_all, part)
    sources = [
        (wqkv_hbm.at[:, pl.ds(i * width, width)], arena.at[pl.ds(pl.multiple_of(me * 3 * part + i * part, 8), part)]) for i in range(3)
    ] + [
        (wout_hbm, strip(wo_all, part)(me)), (up_piece(0), wup_strip(me)),
        (wdn_hbm, wdn_ref.at[pl.ds(pl.multiple_of(shift, 8), own)]),
    ]
    local = [pltpu.make_async_copy(src, dst, loc_sem.at[i]) for i, (src, dst) in enumerate(sources)]
    for copy in local:
        copy.start()
    saves = [
        pltpu.make_async_copy(src, dst, save_sem.at[i])
        for i, (src, dst) in enumerate((
            (na_ref, na_hbm), (proj_ref, proj_hbm), (probs_ref, probs_hbm), (att_ref, att_hbm),
            (bra_ref, bra_hbm), (mid_ref, mid_hbm), (arena, wq_hbm), (wo_all, wo_hbm),
            (bb_ref, bb_hbm), (gdn_ref, gdn_hbm), (gup_ref, gup_hbm),
        ))
    ]
    act = jax.nn.silu(cond_ref[...].astype(F32))
    cond_all[me] = jnp.concatenate([act, act], axis=0).astype(BF16)
    qkv = Gather(wq_strip, 3 * part, q_send, q_recv, lead(3 * part))
    out = Gather(strip(wo_all, part), part, o_send, o_recv, lead(part))
    gbb = Gather(lambda j: gbb_all.at[j], rows, g_send, g_recv, rows // 2)
    nb = Gather(lambda j: nb_all.at[j], rows, n_send, n_recv, rows // 2)
    conds = [remote(cond_all.at[me], cond_all.at[me], c_send.at[e], c_recv.at[e], e) for e in others]
    ups = [remote(up_piece(e), wup_strip(me), up_send.at[e], up_recv.at[e], e) for e in others]
    pairs = [remote(pm.at[flipped(2 * p + 1)], mpair.at[p], mp_send.at[p], mp_recv.at[p], 1) for p in range(4)]
    fars = [remote(mlow.at[p], mfar.at[p], mf_send.at[p], mf_recv.at[p], 2 * p) for p in range(1, 4)]
    block = [arena.at[pl.ds(i * rows, rows)] for i in range(12)]
    gnb = PlaneSum(
        block[8:], block[:4], [in_pair.at[p] for p in range(4)], cross_a, cross_b, from_x, from_y,
        pr_send, pr_recv, far_send, far_recv, rows, rows // 2,
    )
    bb_pairs = [remote(block[4 + p], in_pair.at[4 + p], pr_send.at[4 + p], pr_recv.at[4 + p], 1) for p in range(4)]

    greet(others)
    for copy in conds:
        copy.start()
    for copy in local[:3]:
        copy.wait()
    qkv.own()
    lay[...] = jnp.zeros_like(lay)
    lay_b[...] = jnp.zeros_like(lay_b)
    lay[0:1, : bada_ref.shape[0]] = bada_ref[...].astype(F32)[None]
    bada = pltpu.roll(lay[...], me * bada_ref.shape[0], 1)[0:1]
    begin = 0
    for ref in (bqkv_ref, bout_ref, bdown_ref):
        size = ref.shape[0]
        lay_b[0:1, begin : begin + size] = ref[...].astype(F32)[None]
        lay_b[0:1, begin : begin + 8 * size] = pltpu.roll(lay_b[:, begin : begin + 8 * size], me * size, 1)[0:1]
        begin += 8 * size
    for copy in conds:
        copy.wait_recv()
    everyone = cond_all[...].astype(F32).reshape(8 * cond_all.shape[1], width).astype(BF16)
    pick = (
        lax.broadcasted_iota(jnp.int32, (width, part), 0) == lax.broadcasted_iota(jnp.int32, (width, part), 1) + me * part
    )
    chosen = nn(everyone, jnp.where(pick, 1.0, 0.0).astype(BF16)).astype(BF16)
    pick_ref[...] = chosen
    bias_row = lax.broadcasted_iota(jnp.int32, (8, 1), 0) == slots
    piece = nn(chosen, wada_ref[...]).reshape(pm.shape)
    pm[...] = piece + bada[None]
    pm[:, :, : lay_b.shape[1]] = jnp.where(bias_row[None], lay_b[0:1][None], pm[:, :, : lay_b.shape[1]])
    for copy in pairs:
        copy.start()
    for p in (3, 2, 1, 0):
        pairs[p].wait_recv()
        total = pm[flipped(2 * p)] + mpair[p]
        if p:
            mlow[p] = total.astype(BF16)
            fars[p - 1].start()
        else:
            pm[me] = total
    qkv.along()
    local[3].wait()
    out.own()
    lay[...] = jnp.zeros_like(lay)
    lay[0:1, :own] = bup_in[...].astype(F32)[None]
    bup = pltpu.roll(lay[:, :wide], shift, 1)[0:1]
    wdn_ref[pl.ds(pl.multiple_of(blank, 8), wide - own)] = jnp.zeros((wide - own, width), BF16)
    for copy in fars:
        copy.wait_recv()
    modulation = pm[me] + (mfar[1].astype(F32) + mfar[2].astype(F32) + mfar[3].astype(F32))
    mod_ref[...] = modulation
    bias = modulation[slots : slots + 1]
    image = image_of(lax.broadcasted_iota(jnp.int32, (rows, 1), 0), sizes_ref)
    selectors = [jnp.where(image == j, 1.0, 0.0) for j in range(slots)]
    gbb_all[me] = (per_row(selectors, mod_ref, 5, width) * cot_ref[...].astype(F32)).astype(BF16)
    gbb.own()
    hidden = tok_ref[...].astype(F32)
    na_ref[...] = (
        normalized(hidden)[0] * (1.0 + per_row(selectors, mod_ref, 1, width)) + per_row(selectors, mod_ref, 0, width)
    ).astype(BF16)
    saves[0].start()
    qkv.across()
    qkv.finish()
    saves[6].start()
    for i in range(3):
        strips = [arena[3 * part * j + i * part : 3 * part * j + (i + 1) * part] for j in range(8)]
        value = nn(na_ref[...], jnp.concatenate(strips, axis=0))
        if i == 0:
            value = value + bias[:, :width]
        if i == 2:
            value = value + bias[:, width : 2 * width]
        proj_ref[:, i * width : (i + 1) * width] = value.astype(BF16)
    saves[1].start()
    out.along()
    for copy in ups:
        copy.start()
    att_ref[...] = jnp.zeros_like(att_ref)
    row_image = image_of(lax.broadcasted_iota(jnp.int32, (rows, rows), 0), sizes_ref)
    column_image = image_of(lax.broadcasted_iota(jnp.int32, (rows, rows), 1), sizes_ref)
    hidden_pairs = jnp.where(row_image == column_image, 0.0, -1e30)
    for head in range(H):
        base, window, mask = head_window(head, head_dim)
        mask = mask.astype(BF16)
        query = proj_ref[:, base : base + window] * mask
        key = proj_ref[:, width + base : width + base + window]
        value = proj_ref[:, 2 * width + base : 2 * width + base + window] * mask
        scores = nt(query, key) * head_dim ** (-0.5) + hidden_pairs
        exponent = jnp.exp(scores - jnp.max(scores, axis=-1, keepdims=True))
        probs = (exponent * (1.0 / jnp.sum(exponent, axis=-1, keepdims=True))).astype(BF16)
        probs_ref[head] = probs
        att_ref[:, base : base + window] += nn(probs, value).astype(BF16)
        if head == 5:
            out.across()
    saves[2].start()
    saves[3].start()
    gbb.along()
    out.finish()
    saves[7].start()
    branch = nn(att_ref[...], wo_all[...]) + bias[:, 2 * width : 3 * width]
    bra_ref[...] = branch
    middle = tok_ref[...].astype(F32) + per_row(selectors, mod_ref, 2, width) * branch
    mid_ref[...] = middle
    nb_all[me] = (
        normalized(middle)[0] * (1.0 + per_row(selectors, mod_ref, 4, width)) + per_row(selectors, mod_ref, 3, width)
    ).astype(BF16)
    nb.own()
    saves[4].start()
    saves[5].start()

    qkv.drain()
    saves[6].wait()
    local[4].wait()
    local[5].wait()
    for copy in ups:
        copy.wait_recv()
    gbb.across()

    def one(slot):
        inner = nn(nb_all[slot], wup_all[...]) + bup
        act, slope = gelu_parts(inner)
        act_all[slot] = act.astype(BF16)
        gi_all[slot] = (slope * nt(gbb_all[slot], wdn_ref[...])).astype(BF16)

    for p in range(4):
        even, odd = flipped(2 * p), flipped(2 * p + 1)
        if p == 1:
            nb.along()
        if p == 3:
            nb.across()
        one(even)
        block[8 + p][...] = nt(gi_all[even], wup_all[...]).astype(BF16)
        gbb.sibling(p)
        nb.sibling(p)
        one(odd)
        block[p][...] = nt(gi_all[odd], wup_all[...]).astype(BF16)
        gnb.pairs[p].start()
        gnb.join(p)

    def forth(p):
        even, odd = flipped(2 * p), flipped(2 * p + 1)
        block[4 + p][...] = nn(act_all[odd], wdn_ref[...]).astype(BF16)
        bb_pairs[p].start()
        bb_ref[p] = nn(act_all[even], wdn_ref[...]).astype(BF16)

    forth(0)
    forth(1)
    forth(2)
    forth(3)
    gnb.relay()
    gdn_ref[...] = tn(act_all[...].reshape(8 * rows, wide), gbb_all[...].reshape(8 * rows, width)).astype(BF16)
    saves[9].start()
    inner_grads = gi_all[...].reshape(8 * rows, wide)
    gup_ref[...] = tn(nb_all[...].reshape(8 * rows, width), inner_grads).astype(BF16).reshape(gup_ref.shape)
    saves[10].start()
    gbup_ref[...] = jnp.sum(inner_grads.astype(F32), axis=0, keepdims=True)
    for p in range(4):
        bb_pairs[p].wait_recv()
        bb_ref[p] += in_pair[4 + p]
    saves[8].start()
    gnb_ref[...] = gnb.total()
    for copy in conds + pairs + fars + ups + bb_pairs:
        copy.wait_send()
    for gather in (out, gbb, nb, gnb):
        gather.drain()
    for i, copy in enumerate(saves):
        if i != 6:
            copy.wait()


def front(sizes, tok, cot, cond, wada, bada, bqkv, bout, bdown, bup, wqkv, wout, wup, wdn):
    rows, width = tok.shape
    part, columns = wada.shape
    wide = wdn.shape[0] + 64
    S, V = jax.ShapeDtypeStruct, pltpu.VMEM
    vm, hbm = pl.BlockSpec(memory_space=pltpu.VMEM), pl.BlockSpec(memory_space=pl.ANY)
    dma = pltpu.SemaphoreType.DMA
    kept = (
        ((rows, width), BF16), ((rows, 3 * width), BF16), ((H, rows, rows), BF16), ((rows, width), BF16),
        ((rows, width), F32), ((rows, width), F32), ((24 * part, width), BF16), ((8 * part, width), BF16),
        ((4, rows, width), BF16), ((wide, width), BF16), ((8, part, wide), BF16),
    )
    shapes = (S((8, columns), F32), S((rows, width), F32), S((1, wide), F32), S((64, part), BF16)) + tuple(S(*pair) for pair in kept)
    return pl.pallas_call(
        front_kernel,
        out_shape=shapes,
        in_specs=[pl.BlockSpec(memory_space=pltpu.SMEM)] + [vm] * 9 + [hbm] * 4,
        out_specs=(vm,) * 4 + (hbm,) * 11,
        scratch_shapes=[V(*pair) for pair in kept] + [
            V((8, 8, width), BF16), V((8, 8, columns), F32), V((4, 8, columns), F32),
            V((4, 8, columns), BF16), V((4, 8, columns), BF16), V((8, columns), F32), V((8, 4 * width), F32),
            V((8, rows, width), BF16), V((8, rows, width), BF16), V((8 * part, wide), BF16), V((wide, width), BF16),
            V((8, rows, wide), BF16), V((8, rows, wide), BF16), V((8, rows, width), BF16),
            V((rows // 2, width), BF16), V((rows // 2, width), BF16), V((rows, width), BF16), V((rows, width), BF16),
            dma((6,)), dma((11,)), dma((8,)), dma((8,)), dma((4,)), dma((4,)), dma((4,)), dma((4,)),
        ] + [dma((8,))] * 14,
        compiler_params=pltpu.CompilerParams(collective_id=0, has_side_effects=True, vmem_limit_bytes=61 << 20),
    )(sizes, tok, cot, cond, wada, bada, bqkv, bout, bdown, bup, wqkv, wout, wup, wdn)

def along(step):
    return lax.rem(lax.axis_index("rep") + step, 4)


def remote_z(src, dst, send, recv, z):
    return pltpu.make_async_remote_copy(
        src_ref=src, dst_ref=dst, send_sem=send, recv_sem=recv, device_id={"rep": z}, device_id_type=MESH
    )


DEPTH = 4


class LineSum:
    def __init__(self, chunks, held, halves, send, recv, lead):
        self.chunks, self.held, self.halves, self.send, self.recv = chunks, held, halves, send, recv
        rows = chunks.shape[1]
        self.parts = (pl.ds(0, lead), pl.ds(lead, rows - lead))
        self.sizes = (lead, rows - lead)

    def on(self, roles, action):
        z = lax.axis_index("rep")
        for role in roles:
            pl.when(z == role)(functools.partial(action, role))

    def enter(self, c, role):
        mate = (1, 0, 3, 2)[role]
        return remote_z(self.chunks.at[c], self.held.at[c], self.send.at[0, c], self.recv.at[0, c], mate)

    def give(self, c, role):
        half = 2 - role
        space = self.halves.at[c, pl.ds(0, self.sizes[half])]
        return remote_z(self.chunks.at[c, self.parts[half]], space, self.send.at[1, c], self.recv.at[1, c], 3 - role)

    def result(self, c, half, kind, target):
        ref = self.held.at[c, self.parts[half]]
        return remote_z(ref, ref, self.send.at[kind, c], self.recv.at[kind, c], target)

    def begin(self, c):
        def action(role):
            if c >= DEPTH:
                self.enter(c - DEPTH, role).wait_send()
            self.enter(c, role).start()

        self.on((0, 3), action)

    def first(self, c):
        def action(role):
            self.enter(c, role).wait_recv()
            self.chunks[c] += self.held[c]
            self.give(c, role).start()

        self.on((1, 2), action)

    def second(self, c):
        def action(role):
            mine = role - 1
            self.give(c, 3 - role).wait_recv()
            part, size = self.parts[mine], self.sizes[mine]
            self.held[c, part] = self.chunks[c, part] + self.halves[c, :size]
            self.result(c, mine, 2, 3 - role).start()
            self.result(c, mine, 3, (1, 0, 3, 2)[role]).start()

        self.on((1, 2), action)

    def third(self, c):
        def action(role):
            other = 2 - role
            self.result(c, other, 2, 3 - role).wait_recv()
            self.result(c, other, 4, (1, 0, 3, 2)[role]).start()

        self.on((1, 2), action)

    def tick(self, n):
        count = self.chunks.shape[0]
        for step, c in ((self.first, n), (self.second, n - 1), (self.third, n - 2)):
            if 0 <= c < count:
                step(c)

    def end(self):
        def outer(role):
            near = 0 if role == 0 else 1
            for c in range(self.chunks.shape[0]):
                self.result(c, near, 3, 1).wait_recv()
                self.result(c, 1 - near, 4, 1).wait_recv()
                if c >= self.chunks.shape[0] - DEPTH:
                    self.enter(c, role).wait_send()

        def inner(role):
            for c in range(self.chunks.shape[0]):
                self.give(c, role).wait_send()
                self.result(c, role - 1, 2, 3 - role).wait_send()
                self.result(c, role - 1, 3, 3 - role).wait_send()
                self.result(c, 2 - role, 4, 3 - role).wait_send()

        self.on((0, 3), outer)
        self.on((1, 2), inner)


def norm_back(values, scale_part, grad):
    normal, rate = normalized(values)
    inner = grad * (1.0 + scale_part)
    back = rate * (
        inner - jnp.mean(inner, axis=-1, keepdims=True) - normal * jnp.mean(inner * normal, axis=-1, keepdims=True)
    )
    return back, grad * normal


def back_kernel(
    sizes_ref, tok_ref, cot_ref, mod_ref, mid_ref, gbup_ref, pick_ref, na_hbm, proj_hbm, probs_hbm, att_hbm, wo_hbm,
    bra_hbm, gnb_hbm, bbs_hbm, gdn_hbm, gup_hbm, wq_hbm, wada_hbm,
    out_ref, gin_ref, sums, mods, gc_in, picks, bias_ref, gbup_out,
    na_ref, proj_ref, probs_ref, att_ref, wo_all,
    gup_in, bb_in, bb_cross, bb_from, zbuf, zhalf, gm_ref, gba_ref, gatt_ref, gp_ref, blocks, pair_in, cross_a, cross_b, from_x, from_y,
    wq_buf, wada_ref, modrow, bias_z, bias_in, gc_out,
    loc_sem, up_send, up_recv, bb_send, bb_recv, z_send, z_recv, ps_send, ps_recv, pc_send, pc_recv,
    md_send, md_recv, mz_send, mz_recv, pk_send, pk_recv, bz_send, bz_recv, bi_send, bi_recv, gc_send, gc_recv,
):
    rows, width = tok_ref.shape
    head_dim = width // H
    slots = sizes_ref.shape[0]
    part = width // 8
    hid = 8 * part // 2
    me, z = flipped(0), lax.axis_index("rep")
    core = lax.rem(me, 2)
    others, steps = range(1, 8), range(1, 4)

    line = LineSum(zbuf, sums, zhalf, z_send, z_recv, lead(part))
    planes = [
        PlaneSum(
            [blocks.at[i, flipped(2 * p)] for p in range(4)], [blocks.at[i, flipped(2 * p + 1)] for p in range(4)],
            [pair_in.at[i, p] for p in range(4)], cross_a.at[i], cross_b.at[i], from_x.at[i], from_y.at[i],
            ps_send.at[i], ps_recv.at[i], pc_send.at[i], pc_recv.at[i], part, lead(part),
        )
        for i in range(4)
    ]
    ups = [remote(gup_hbm.at[flipped(e)], gup_in.at[me], up_send.at[e], up_recv.at[e], e) for e in others]
    branch_sum = PlaneSum(
        [bb_in.at[p] for p in range(4)], None, None, bb_cross.at[pl.ds(0, rows // 2)], bb_cross.at[pl.ds(rows // 2, rows // 2)],
        bb_from.at[0], bb_from.at[1], None, None, bb_send, bb_recv, rows, rows // 2,
    )
    shift = (gdn_hbm.shape[0] - hid) * core
    local = [pltpu.make_async_copy(gdn_hbm.at[pl.ds(pl.multiple_of(shift + part * c, 16), part)], zbuf.at[c], loc_sem.at[c]) for c in range(4)]
    local.append(pltpu.make_async_copy(gup_hbm.at[me], gup_in.at[me], loc_sem.at[4]))
    local.append(pltpu.make_async_copy(bbs_hbm, bb_in, loc_sem.at[5]))
    local.append(pltpu.make_async_copy(wada_hbm, wada_ref, loc_sem.at[6]))
    loads = [pltpu.make_async_copy(wq_hbm.at[:, pl.ds(i * part, part)], wq_buf, loc_sem.at[7 + i]) for i in range(3)]
    local.append(pltpu.make_async_copy(bra_hbm, gm_ref, loc_sem.at[10]))
    local.append(pltpu.make_async_copy(gnb_hbm, gin_ref, loc_sem.at[11]))
    local += [
        pltpu.make_async_copy(src, dst, loc_sem.at[12 + i])
        for i, (src, dst) in enumerate((
            (wo_hbm, wo_all), (att_hbm, att_ref), (proj_hbm, proj_ref), (probs_hbm, probs_ref), (na_hbm, na_ref),
        ))
    ]
    for i in (7, 8, 0, 1, 9, 10, 2, 3, 5, 11, 12, 4, 13, 6):
        local[i].start()
    loads[0].start()
    picks[z] = pick_ref[...]

    barrier = pltpu.get_barrier_semaphore()
    for e in others:
        pl.semaphore_signal(barrier, inc=1, device_id={"fsdp": flipped(e)}, device_id_type=MESH)
    for s in steps:
        pl.semaphore_signal(barrier, inc=1, device_id={"rep": along(s)}, device_id_type=MESH)
    pl.semaphore_wait(barrier, 10)

    for copy in ups:
        copy.start()
    for c in range(4):
        local[c].wait()
    for c in range(DEPTH):
        line.begin(c)
    local[5].wait()
    for p in (3, 2, 1):
        branch_sum.leave(p)
    send_picks = [remote_z(picks.at[z], picks.at[z], pk_send.at[s], pk_recv.at[s], along(s)) for s in steps]
    for copy in send_picks:
        copy.start()

    image = image_of(lax.broadcasted_iota(jnp.int32, (rows, 1), 0), sizes_ref)
    selectors = [jnp.where(image == j, 1.0, 0.0) for j in range(slots)]
    slot = lax.broadcasted_iota(jnp.int32, (8, rows), 0)
    where = image_of(lax.broadcasted_iota(jnp.int32, (8, rows), 1), sizes_ref)
    gather_rows = (jnp.where((where == slot) & (slot < slots), 1.0, 0.0), jnp.where((where == slot - slots) & (where < slots), 1.0, 0.0))
    modrow[...] = jnp.zeros_like(modrow)

    def to_slots(index, values):
        modrow[:, (index % 3) * width : (index % 3 + 1) * width] += lax.dot_general(
            gather_rows[index // 3], values, (((1,), (0,)), ((), ())), precision=lax.Precision.HIGHEST, preferred_element_type=F32
        )

    cot = cot_ref[...].astype(F32)
    local[7].wait()
    local[8].wait()
    back, grad_scale = norm_back(mid_ref[...], per_row(selectors, mod_ref, 4, width), gin_ref[...])
    to_slots(3, gin_ref[...])
    to_slots(4, grad_scale)
    gm = cot + back
    to_slots(2, gm * gm_ref[...])
    gm_ref[...] = gm
    gba = (per_row(selectors, mod_ref, 2, width) * gm).astype(BF16)
    gba_ref[...] = gba
    bias_z[0] = jnp.zeros(bias_z.shape[1:], F32)
    bias_z[0, 2:3] = jnp.sum(gba.astype(F32), axis=0, keepdims=True)
    gbb = (per_row(selectors, mod_ref, 5, width) * cot).astype(BF16)
    bias_z[0, 3:4] = jnp.sum(gbb.astype(F32), axis=0, keepdims=True)
    bias_z[0, 4:5, : gbup_ref.shape[1]] = gbup_ref[...]
    local[9].wait()
    gatt_ref[...] = nt(gba_ref[...], wo_all[...].reshape(width, width)).astype(BF16)
    local[10].wait()
    blocks[0] = tn(att_ref[...], gba_ref[...]).astype(BF16).reshape(8, part, width)
    planes[0].pair()
    line.tick(0)

    gp_ref[...] = jnp.zeros_like(gp_ref)
    rate = head_dim ** (-0.5)

    def head_back(head):
        base, window, mask = head_window(head, head_dim)
        mask = mask.astype(BF16)
        at = [pl.ds(i * width + base, window) for i in range(3)]
        query, key, value = proj_ref[:, at[0]] * mask, proj_ref[:, at[1]] * mask, proj_ref[:, at[2]]
        grad = gatt_ref[:, at[0]] * mask
        low = probs_ref[head]
        probs = low.astype(F32)
        grad_probs = nt(grad, value)
        delta = jnp.sum(probs * grad_probs, axis=-1, keepdims=True)
        grad_scores = (probs * (grad_probs - delta)).astype(BF16)
        gp_ref[:, at[0]] += (nn(grad_scores, key) * rate).astype(BF16)
        gp_ref[:, at[1]] += (tn(grad_scores, query) * rate).astype(BF16)
        gp_ref[:, at[2]] += tn(low, grad).astype(BF16)

    local[11].wait()
    local[12].wait()
    for head in range(3):
        head_back(head)
    planes[0].combine()
    for head in range(3, 10):
        head_back(head)
    line.tick(1)
    for head in range(10, 16):
        head_back(head)
    local[4].wait()
    for copy in ups:
        copy.wait_recv()
    lap = gup_in.shape[2] - hid
    for c in range(4):
        left, right = gup_in[2 * c], gup_in[2 * c + 1]
        zbuf[4 + c, :, : hid - lap] = left[:, : hid - lap]
        zbuf[4 + c, :, hid - lap : hid + lap] = left[:, hid - lap :] + right[:, : 2 * lap]
        zbuf[4 + c, :, hid + lap :] = right[:, 2 * lap :]
    line.begin(4)
    line.begin(5)
    line.tick(2)

    def spread(i):
        blocks[i] = tn(na_ref[...], gp_ref[:, (i - 1) * width : i * width]).astype(BF16).reshape(8, part, width)
        planes[i].pair()

    def settle(i):
        zbuf[8 + i] = planes[i].total().astype(BF16)
        line.begin(8 + i)

    branch_sum.relay()
    local[13].wait()
    spread(1)
    spread(2)
    spread(3)
    for i in range(3):
        loads[i].wait()
        term = nt(gp_ref[:, i * width : (i + 1) * width], wq_buf[...].reshape(width, width))
        gin_ref[...] = term if i == 0 else gin_ref[...] + term
        if i < 2:
            loads[i + 1].start()
    gna = gin_ref[...]
    for i, c in ((0, 0), (2, 1)):
        bias_z[0, c : c + 1] = jnp.sum(gp_ref[:, i * width : (i + 1) * width].astype(F32), axis=0, keepdims=True)
    send_bias = [remote_z(bias_z.at[0], bias_z.at[s], bz_send.at[s], bz_recv.at[s], along(s)) for s in steps]
    for copy in send_bias:
        copy.start()
    back, grad_scale = norm_back(tok_ref[...].astype(F32), per_row(selectors, mod_ref, 1, width), gna)
    to_slots(0, gna)
    to_slots(1, grad_scale)
    gin_ref[...] = gm_ref[...] + back
    line.begin(6)
    line.tick(3)
    planes[0].relay()
    planes[1].combine()
    line.begin(7)
    line.tick(4)
    planes[2].combine()
    line.tick(5)
    branch = branch_sum.total()
    branch = branch + mod_ref[slots : slots + 1, 3 * width : 4 * width]
    out_ref[...] = (mid_ref[...] + per_row(selectors, mod_ref, 5, width) * branch).astype(BF16)
    to_slots(5, cot_ref[...].astype(F32) * branch)
    mine = mods.at[me, pl.ds(pl.multiple_of(8 * z, 8), 8)]
    mine[...] = modrow[...].astype(BF16)
    send_mods = [remote_z(mine, mine, mz_send.at[s], mz_recv.at[s], along(s)) for s in steps]
    for copy in send_mods:
        copy.start()
    planes[1].relay()
    planes[3].combine()
    settle(0)
    line.tick(6)
    planes[2].relay()
    settle(1)
    line.tick(7)
    planes[3].relay()
    settle(2)
    line.tick(8)
    settle(3)
    line.tick(9)
    for copy in send_mods + send_bias:
        copy.wait_recv()
    gather = Gather(lambda j: mods.at[j], mods.shape[1], md_send, md_recv, mods.shape[1] // 2)
    gather.own()
    total = bias_z[0] + bias_z[1] + bias_z[2] + bias_z[3]
    gbup_out[...] = total[4:5, : gbup_out.shape[1]]
    bias_in[me] = total
    send_total = [remote(bias_in.at[me], bias_in.at[me], bi_send.at[e], bi_recv.at[e], e) for e in others]
    for copy in send_total:
        copy.start()
    line.tick(10)
    gather.along()
    line.tick(11)
    gather.across()
    gather.finish()
    local[6].wait()
    plane_rows = mods[:, pl.ds(pl.multiple_of(8 * z, 8), 8), :].reshape(64, mods.shape[2])
    half = mods.shape[2]
    first, second = nt(plane_rows, wada_ref[:, :half]), nt(plane_rows, wada_ref[:, half:])
    upper = lax.rem(lax.broadcasted_iota(jnp.int32, (64, 1), 0), 8) < slots
    gc_out[...] = jnp.where(upper, first, second).reshape(gc_out.shape)
    send_gc = [remote(gc_out.at[flipped(e)], gc_in.at[me], gc_send.at[e], gc_recv.at[e], e) for e in others]
    for copy in send_gc:
        copy.start()
    gc_in[me] = gc_out[me]
    line.tick(12)
    for copy in send_total:
        copy.wait_recv()
    total = bias_in[0]
    for j in others:
        total = total + bias_in[j]
    bias_ref[...] = total
    line.tick(13)
    for copy in send_gc + send_picks:
        copy.wait_recv()
    line.end()
    for copy in ups + send_picks + send_bias + send_mods + send_total + send_gc:
        copy.wait_send()
    for plane in planes + [branch_sum]:
        plane.drain()
    gather.drain()


def backward(sizes, tok, cot, mod, mid, gbup, pick, na, proj, probs, att, wo, bra, gnb, bbs, gdn, gup, wq, wada):
    rows, width = tok.shape
    part, columns = wada.shape
    wide = gdn.shape[0]
    S, V = jax.ShapeDtypeStruct, pltpu.VMEM
    vm, hbm = pl.BlockSpec(memory_space=pltpu.VMEM), pl.BlockSpec(memory_space=pl.ANY)
    dma = pltpu.SemaphoreType.DMA
    shapes = (
        S((rows, width), BF16), S((rows, width), F32), S((12, part, width), BF16), S((8, 32, columns // 2), BF16),
        S((8, 8, part), F32), S((4, 64, part), BF16), S((8, width), F32), S((1, wide), F32),
    )
    return pl.pallas_call(
        back_kernel,
        out_shape=shapes,
        in_specs=[pl.BlockSpec(memory_space=pltpu.SMEM)] + [vm] * 6 + [hbm] * 12,
        out_specs=(vm,) * len(shapes),
        scratch_shapes=[
            V((rows, width), BF16), V((rows, 3 * width), BF16), V((H, rows, rows), BF16), V((rows, width), BF16), V((8, part, width), BF16),
            V((8, part, wide), BF16), V((4, rows, width), BF16), V((rows, width), BF16), V((2, rows, width), BF16), V((12, part, width), BF16), V((12, lead(part), width), BF16),
            V((rows, width), F32), V((rows, width), BF16), V((rows, width), BF16), V((rows, 3 * width), BF16),
            V((4, 8, part, width), BF16), V((4, 4, part, width), BF16), V((4, lead(part), width), BF16), V((4, part - lead(part), width), BF16),
            V((4, part, width), BF16), V((4, part, width), BF16), V((8, part, width), BF16), V((part, columns), BF16),
            V((8, columns // 2), F32), V((4, 8, width), F32), V((8, 8, width), F32), V((8, 8, part), F32),
            dma((17,)), dma((8,)), dma((8,)), dma((6,)), dma((6,)), dma((5, 12)), dma((5, 12)), dma((4, 4)), dma((4, 4)),
            dma((4, 6)), dma((4, 6)), dma((8,)), dma((8,)), dma((4,)), dma((4,)), dma((4,)), dma((4,)), dma((4,)), dma((4,)),
            dma((8,)), dma((8,)), dma((8,)), dma((8,)),
        ],
        compiler_params=pltpu.CompilerParams(collective_id=2, has_side_effects=True, vmem_limit_bytes=62 << 20),
    )(sizes, tok, cot, mod, mid, gbup, pick, na, proj, probs, att, wo, bra, gnb, bbs, gdn, gup, wq, wada)

def finish_kernel(
    picks_ref, gc_ref, bias_ref, gbup_ref, cond_ref, sums_hbm, mods_hbm, out_hbm, gin_hbm,
    gcond_ref, gada_hbm, gbada_ref, gqkv_hbm, gbqkv_ref, gout_hbm, gbout_ref, gup_hbm, gbup_out, gdown_hbm, gbdown_ref,
    out_final, gin_final,
    sums_ref, mods_ref, gada_ref, gqkv_ref, gout_ref, gup_ref, gdown_ref, lanes, out_ref, gin_ref, sem,
):
    pairs = (
        (sums_hbm.at[pl.ds(0, 4)], sums_ref.at[pl.ds(0, 4)]), (sums_hbm.at[pl.ds(4, 4)], sums_ref.at[pl.ds(4, 4)]),
        (sums_hbm.at[pl.ds(8, 4)], sums_ref.at[pl.ds(8, 4)]), (mods_hbm, mods_ref), (out_hbm, out_ref), (gin_hbm, gin_ref),
        (gdown_ref, gdown_hbm), (gup_ref, gup_hbm), (gout_ref, gout_hbm), (gqkv_ref, gqkv_hbm), (gada_ref, gada_hbm),
        (out_ref, out_final), (gin_ref, gin_final),
    )
    copies = [pltpu.make_async_copy(src, dst, sem.at[i]) for i, (src, dst) in enumerate(pairs)]
    for copy in copies[:6]:
        copy.start()
    slots, width = cond_ref.shape
    part = width // 8
    half = mods_ref.shape[2]
    me, z = lax.axis_index("fsdp"), lax.axis_index("rep")
    copies[0].wait()
    for c in range(4):
        gdown_ref[c * part : (c + 1) * part] = sums_ref[c].astype(F32)
    copies[6].start()
    copies[1].wait()
    for c in range(4):
        gup_ref[:, c * width : (c + 1) * width] = sums_ref[4 + c].astype(F32)
    copies[7].start()
    copies[2].wait()
    gout_ref[...] = sums_ref[8].astype(F32)
    copies[8].start()
    copies[4].wait()
    copies[11].start()
    copies[5].wait()
    copies[12].start()
    for c in range(3):
        gqkv_ref[:, c * width : (c + 1) * width] = sums_ref[9 + c].astype(F32)
    copies[9].start()
    copies[3].wait()
    rows = mods_ref[...].reshape(256, half)
    acts = jnp.stack([picks_ref[i] for i in range(4)], axis=0).reshape(4, 8, 8, part)
    acts = jnp.stack([acts[:, f] for f in range(8)], axis=0).reshape(256, part).astype(F32)
    upper = lax.rem(lax.broadcasted_iota(jnp.int32, (256, 1), 0), 8) < slots
    first, second = jnp.where(upper, acts, 0.0).astype(BF16), jnp.where(upper, 0.0, acts).astype(BF16)
    gada_ref[:, :half] = tn(first, rows)
    gada_ref[:, half:] = tn(second, rows)
    copies[10].start()
    floats = rows.astype(F32)
    lanes[...] = jnp.zeros_like(lanes)

    def own(row, size):
        total = row.shape[1]
        lanes[0:1, :total] = row
        return pltpu.roll(lanes[:, :total], lax.rem(total - me * size, total), 1)[0, :size]

    column = jnp.concatenate(
        [
            jnp.sum(jnp.where(upper, floats, 0.0), axis=0, keepdims=True),
            jnp.sum(jnp.where(upper, 0.0, floats), axis=0, keepdims=True),
        ],
        axis=1,
    )
    gbada_ref[...] = own(column, gbada_ref.shape[0])
    gbqkv_ref[...] = own(jnp.concatenate([bias_ref[0:1], bias_ref[1:2]], axis=1), gbqkv_ref.shape[0])
    gbout_ref[...] = own(bias_ref[2:3], part)
    gbdown_ref[...] = own(bias_ref[3:4], part)
    wide, hid = gbup_ref.shape[1], gbup_out.shape[0]
    lanes[0:1, :wide] = gbup_ref[...]
    gbup_out[...] = pltpu.roll(lanes[:, :wide], lax.rem(wide - lax.rem(me, 2) * (wide - hid), wide), 1)[0, :hid]
    grad = None
    for j in range(8):
        lanes[:, :width] = jnp.zeros((8, width), F32)
        lanes[0:slots, :part] = gc_ref[j, 0:slots] + gc_ref[j, slots : 2 * slots]
        term = pltpu.roll(lanes[:, :width], j * part, 1) if j else lanes[:, :width]
        grad = term if grad is None else grad + term
    cond = cond_ref[...].astype(F32)
    gate = jax.nn.sigmoid(cond)
    gcond_ref[...] = grad[0:slots] * (gate * (1.0 + cond * (1.0 - gate)))
    for copy in copies[6:]:
        copy.wait()


def finish(output, grad_input, sums, mods, picks, gc, bias, gbup, cond, sizes):
    S, V = jax.ShapeDtypeStruct, pltpu.VMEM
    vm, hbm = pl.BlockSpec(memory_space=pltpu.VMEM), pl.BlockSpec(memory_space=pl.ANY)
    large = (1, 3, 5, 7, 9)
    shapes = tuple(S(size, F32) for size in sizes) + (S(output.shape, output.dtype), S(grad_input.shape, F32))
    specs = tuple(hbm if i in large or i >= len(sizes) else vm for i in range(len(shapes)))
    *grads, output, grad_input = pl.pallas_call(
        finish_kernel,
        out_shape=shapes,
        in_specs=[vm] * 5 + [hbm] * 4,
        out_specs=specs,
        scratch_shapes=[V(sums.shape, BF16), V(mods.shape, BF16)] + [V(sizes[i], F32) for i in large] + [
            V((8, 2 * mods.shape[2]), F32), V(output.shape, output.dtype), V(grad_input.shape, F32), pltpu.SemaphoreType.DMA((13,)),
        ],
        compiler_params=pltpu.CompilerParams(vmem_limit_bytes=56 << 20),
    )(picks, gc, bias, gbup, cond, sums, mods, output, grad_input)
    return (output, grad_input, *grads)

def fast(tokens, cond, image_sizes, w_ada, b_ada, w_qkv, b_qkv, w_out, b_out, w_up, b_up, w_down, b_down, cotangent):
    width = tokens.shape[1]
    part, columns = w_ada.shape
    mod, gnb, gbup, pick, na, proj, probs, att, bra, mid, wq, wo, bbs, gdn, gup = front(
        image_sizes, tokens, cotangent, cond, w_ada, b_ada, b_qkv, b_out, b_down, b_up,
        w_qkv, w_out, w_up, w_down,
    )
    wq, wo = wq.reshape(8, 3 * part, width), wo.reshape(8, part, width)
    output, grad_input, sums, mods, gc, picks, bias, gbup = backward(
        image_sizes, tokens, cotangent, mod, mid, gbup, pick, na, proj, probs, att, wo, bra, gnb, bbs, gdn, gup, wq, w_ada
    )
    sizes = tuple(
        leaf.shape for leaf in (cond, w_ada, b_ada, w_qkv, b_qkv, w_out, b_out, w_up, b_up, w_down, b_down)
    )
    return finish(output, grad_input, sums, mods, picks, gc, bias, gbup, cond, sizes)


def solution(mesh):
    placed = (
        P(("fsdp", "rep"), None),
        P(("fsdp", "rep"), None),
        P(("fsdp", "rep")),
        P("fsdp", None),
        P("fsdp"),
        P("fsdp", None),
        P("fsdp"),
        P("fsdp", None),
        P("fsdp"),
        P("fsdp", None),
        P("fsdp"),
        P("fsdp", None),
        P("fsdp"),
        P(("fsdp", "rep"), None),
    )
    fits = mesh.shape["fsdp"] == 8 and mesh.shape["rep"] == 4
    return jax.shard_map(
        fast if fits else local,
        mesh=mesh,
        in_specs=placed,
        out_specs=(
            P(("fsdp", "rep"), None),
            P(("fsdp", "rep"), None),
            P(("fsdp", "rep"), None),
            P("fsdp", None),
            P("fsdp"),
            P("fsdp", None),
            P("fsdp"),
            P("fsdp", None),
            P("fsdp"),
            P("fsdp", None),
            P("fsdp"),
            P("fsdp", None),
            P("fsdp"),
        ),
        check_vma=False,
    )
```
